32 devices in a mesh: group: 2 (over x), vox: 4 (over y, core), snp: 4 (over z).
Axes of the slice: x: 2, y: 2, z: 4, core: 2. Of those that a mesh axis runs over, the one named last changes fastest.
Arguments:
- images: bfloat16 [4096, 4, 8, 256], P(('group', 'vox', 'snp')), parts along dimension 0, may hold values from 0 to 1
- genotypes: bfloat16 [4096, 512], P(('group', 'vox', 'snp')), parts along dimension 0, may hold values from 0 to 2
- covariates: bfloat16 [4096, 16], P(('group', 'vox', 'snp')), parts along dimension 0, may hold values from -6 to 6
- site_codes: int32 [4096], P(('group', 'vox', 'snp')), parts along dimension 0, may hold values from 0 to 3, as said below
Outputs:
- t_stats: float32 [1024, 4, 8, 256], P(('group', 'snp'), None, 'vox'), parts along dimension 0
The draws below stay inside these ranges and needn't reach their ends.
There are 2 independent parts, one for each index of `group`. The reference program is written for one: setup_inputs(seed, part) draws one part's arguments, and reference() takes and returns one part's arrays. A program takes and returns all parts, laid end to end along the dimension named above; each array names one. Nothing has to cross between parts.
Inputs may be any that keep to these rules, and one draw needn't show every extreme that they name: `site_codes`: each centre code is held by exactly 512 subjects.
All inputs are finite; a program needn't handle non-finite values.
Results may differ from the reference program's by a relative error of at most 0.0014.
The reference program's roundings to bfloat16 on the way count: a program that leaves them out, or rounds other values in their place, can miss the bound.
Values may be sent and summed in bfloat16 or wider, within the bound.
No kernel may reach another device: no remote copies, remote signals or barrier semaphores. Data moves between devices by JAX's collectives and lax.ppermute only.
A program may use at most 192 MiB of HBM per device.

```python
import math
import jax
import jax.numpy as jnp
from jax import lax

MAPS = 4
SY = 16
SZ = 16
COVS = 16
SITES = 4
SUBJECTS = 2048
SX = 8
PLANE = 256
SNPS = 512
DESIGN = 20


def draw_site_codes(key, part):
    order = jax.random.permutation(key, SUBJECTS)
    return (order % SITES).astype(jnp.int32)


def levels(key, shape, split, low, top_value):
    loudness = 1.0
    for dim, parts in split:
        steps = jax.random.uniform(jax.random.fold_in(jax.random.fold_in(key, 6), dim), (parts,), jnp.float32, low / len(split), top_value / len(split))
        loudness = loudness * jnp.repeat(jnp.exp(steps), shape[dim] // parts).reshape((-1,) + (1,) * (len(shape) - 1 - dim))
    return loudness


def scatter_about(stream_key, dims, deviation, reach, cuts=(), kind=jnp.bfloat16):
    level = levels(stream_key, dims, cuts, -0.22, 0.18) if cuts else 1.0
    entries = jax.random.normal(stream_key, dims, jnp.float32) * deviation * level
    return jnp.minimum(jnp.maximum(entries, -reach), reach).astype(kind)


def setup_inputs(seed: int = 0, part: int = 0) -> dict:
    key_of = jax.random.split(jax.random.key(seed), 5)
    own_keys = jax.random.split(jax.random.fold_in(key_of[4], part), 5)
    return {
        "images": jnp.clip(1.0 * jax.random.uniform(own_keys[0], (SUBJECTS, MAPS, SX, PLANE), jnp.float32) ** levels(own_keys[0], (SUBJECTS, MAPS, SX, PLANE), ((0, 16),), -0.2, 0.2), 0.0, 1.0).astype(jnp.bfloat16),
        "genotypes": jnp.clip(2.0 * jax.random.uniform(own_keys[1], (SUBJECTS, SNPS), jnp.float32) ** levels(own_keys[1], (SUBJECTS, SNPS), ((0, 16),), -0.2, 0.2), 0.0, 2.0).astype(jnp.bfloat16),
        "covariates": scatter_about(own_keys[2], (SUBJECTS, COVS), 1.0, 6.0, ((0, 16),)),
        "site_codes": draw_site_codes(jax.random.fold_in(jax.random.fold_in(key_of[4], part), 71), part),
    }


smooth_sigma = 1.0
kernel_reach = 2

def kernel_table(length):
    position = jnp.arange(length)
    offset = (position[:, None] - position[None, :]).astype(jnp.float32)
    weights = jnp.where(jnp.abs(offset) <= kernel_reach, jnp.exp(-offset * offset / (2.0 * smooth_sigma ** 2)), 0.0)
    weight_total = sum((math.exp(-(lag_value * lag_value) / (2.0 * smooth_sigma ** 2)) for lag_value in range(-kernel_reach, kernel_reach + 1)))
    return (weights / weight_total).astype(jnp.float32)

def smooth_maps(images):
    subj_here, map_count, planes, plane_size = images.shape
    row_table = kernel_table(SY)
    depth_table = kernel_table(SZ)
    plane_table = (row_table[:, None, :, None] * depth_table[None, :, None, :]).reshape(plane_size, plane_size).astype(jnp.bfloat16)
    slab_table = kernel_table(planes)
    results = []
    for channel in range(map_count):
        flat_map = images[:, channel].reshape(subj_here * planes, plane_size)
        inplane = jnp.dot(flat_map.astype(jnp.float32), plane_table.astype(jnp.float32), preferred_element_type=jnp.float32).reshape(subj_here, planes, plane_size)
        smoothed_map = jnp.einsum('ab,sbp->sap', slab_table, inplane, precision=lax.Precision.HIGHEST)
        results.append(smoothed_map.astype(jnp.bfloat16))
    return jnp.stack(results, axis=1)

def build_design(codes, covariates):
    one_hot = (codes[:, None] == jnp.arange(SITES)[None, :]).astype(jnp.bfloat16)
    return jnp.concatenate([one_hot, covariates], axis=1)

def contract(left, right):
    return lax.dot_general(left.astype(jnp.float32), right.astype(jnp.float32), (((0,), (0,)), ((), ())), preferred_element_type=jnp.float32)

def contract_exact(left, right):
    return lax.dot_general(left, right, (((0,), (0,)), ((), ())), precision=lax.Precision.HIGHEST)

def reference(images, genotypes, covariates, site_codes):
    smoothed = smooth_maps(images)
    design = build_design(site_codes, covariates)
    gram = contract(design, design)
    cross_gene = contract(design, genotypes)
    gene_sq = lax.optimization_barrier(jnp.sum(jnp.square(genotypes.astype(jnp.float32)), axis=0))
    factor = jnp.linalg.cholesky(gram)
    gene_coef = jax.scipy.linalg.cho_solve((factor, True), cross_gene)
    gene_rss = gene_sq - lax.optimization_barrier(jnp.sum(cross_gene * gene_coef, axis=0))
    freedom = float(SUBJECTS - DESIGN - 1)
    outputs = []
    for channel in range(MAPS):
        columns = smoothed[:, channel].reshape(SUBJECTS, SX * PLANE)
        cross_image = contract(design, columns)
        image_sq = lax.optimization_barrier(jnp.sum(jnp.square(columns.astype(jnp.float32)), axis=0))
        image_coef = jax.scipy.linalg.cho_solve((factor, True), cross_image)
        image_rss = image_sq - lax.optimization_barrier(jnp.sum(cross_image * image_coef, axis=0))
        products = contract_exact(genotypes.astype(jnp.float32), columns.astype(jnp.float32))
        numer = products - contract_exact(gene_coef, cross_image)
        ratio = numer * lax.rsqrt(gene_rss[:, None] * image_rss[None, :])
        stats = ratio * jnp.sqrt(freedom / (1.0 - ratio * ratio))
        outputs.append(stats.reshape(SNPS, SX, PLANE))
    return jnp.stack(outputs, axis=1)
```

```python
import functools

import jax
import jax.numpy as jnp
import ml_dtypes
import numpy as np
from jax import lax
from jax.experimental import pallas as pl
from jax.experimental.pallas import tpu as pltpu
from jax.sharding import PartitionSpec as P

SY = 16
SZ = 16
SITES = 4
REACH = 2
DPAD = 24
LANES = 128
SUBJ_TILE = 16
HIGHEST = lax.Precision.HIGHEST
VMEM_LIMIT = 56 * 2**20


def kernel_table(length):
    position = np.arange(length)
    offset = (position[:, None] - position[None, :]).astype(np.float32)
    weights = np.where(np.abs(offset) <= REACH, np.exp(-offset * offset / np.float32(2.0)), np.float32(0.0))
    total = sum(np.exp(-(k * k) / 2.0) for k in range(-REACH, REACH + 1))
    return (weights / np.float32(total)).astype(np.float32)


def plane_kernel(plane):
    row, depth = kernel_table(SY), kernel_table(SZ)
    table = row[:, None, :, None] * depth[None, :, None, :]
    return table.reshape(plane, plane).astype(ml_dtypes.bfloat16)


def row_order(maps, planes):
    rows = SUBJ_TILE * maps * planes
    source = np.arange(rows).reshape(SUBJ_TILE, maps * planes).T.reshape(-1)
    return np.eye(rows, dtype=np.float32)[source].astype(ml_dtypes.bfloat16)


def smooth_kernel(group, planes, per_vox, n_snp, width, images, order, table, out):
    plane = table.shape[0]
    subjects = images.shape[0]
    groups = images.shape[1] // (group * planes)
    near = kernel_table(2 * REACH + 1)[REACH]
    for tile in range(subjects // SUBJ_TILE):
        here = pl.ds(tile * SUBJ_TILE, SUBJ_TILE)
        for part in range(groups):
            rows = images[here, part * group * planes : (part + 1) * group * planes, :]
            rows = rows.reshape(SUBJ_TILE * group * planes, plane)
            rows = jnp.dot(order[...], rows, preferred_element_type=jnp.float32)
            inplane = jnp.dot(
                rows.astype(jnp.bfloat16), table[...], preferred_element_type=jnp.float32
            )
            for m in range(group):
                slabs = [
                    inplane[(m * planes + x) * SUBJ_TILE : (m * planes + x + 1) * SUBJ_TILE]
                    for x in range(planes)
                ]
                for x in range(planes):
                    total = slabs[x] * float(near[REACH])
                    for lag in range(1, REACH + 1):
                        sides = [slabs[i] for i in (x - lag, x + lag) if 0 <= i < planes]
                        if sides:
                            total = total + functools.reduce(jnp.add, sides) * float(
                                near[REACH + lag]
                            )
                    column = ((part * group + m) * per_vox + x % per_vox) * plane
                    target = (x // per_vox) * n_snp + column // width
                    first = column % width
                    out[target, here, first : first + plane] = total.astype(jnp.bfloat16)


def smooth(images, n_vox, n_snp):
    subjects, maps, planes, plane = images.shape
    per_vox = planes // n_vox
    width = maps * per_vox * plane // n_snp
    group = max(1, min(maps, 256 // (SUBJ_TILE * planes)))
    step = 32
    order = jnp.asarray(row_order(group, planes))
    table = jnp.asarray(plane_kernel(plane))
    return pl.pallas_call(
        functools.partial(smooth_kernel, group, planes, per_vox, n_snp, width),
        out_shape=jax.ShapeDtypeStruct((n_vox * n_snp, subjects, width), jnp.bfloat16),
        grid=(subjects // step,),
        in_specs=[
            pl.BlockSpec((step, maps * planes, plane), lambda i: (i, 0, 0)),
            pl.BlockSpec(order.shape, lambda i: (0, 0)),
            pl.BlockSpec(table.shape, lambda i: (0, 0)),
        ],
        out_specs=pl.BlockSpec((n_vox * n_snp, step, width), lambda i: (0, i, 0)),
        compiler_params=pltpu.CompilerParams(vmem_limit_bytes=VMEM_LIMIT),
        name="smooth",
    )(images.reshape(subjects, maps * planes, plane), order, table)


def gene_kernel(snps, design, blocks, joined, coef, inverse, cross, square):
    step = pl.program_id(0)
    rows = jnp.concatenate([blocks[i] for i in range(blocks.shape[0])], axis=1)
    joined[...] = rows
    tail = jnp.concatenate(
        [rows[snps:], jnp.zeros((LANES - DPAD, rows.shape[1]), rows.dtype)], axis=0
    )
    moments = lax.dot_general(
        rows, tail, (((1,), (1,)), ((), ())), preferred_element_type=jnp.float32
    )
    wide = rows[:snps].astype(jnp.float32)
    squares = jnp.sum(wide * wide, axis=1, keepdims=True)

    @pl.when(step == 0)
    def _():
        cross[...] = moments
        square[...] = squares

    @pl.when(step > 0)
    def _():
        cross[...] += moments
        square[...] += squares

    @pl.when(step == pl.num_programs(0) - 1)
    def _():
        lane = lax.broadcasted_iota(jnp.int32, (DPAD, LANES), 1)
        row = lax.broadcasted_iota(jnp.int32, (DPAD, LANES), 0)
        shift = 32
        work = cross[snps:, :]
        work = jnp.where((row >= design) & (lane == row), 1.0, work)
        work = jnp.where(lane == row + shift, 1.0, work)
        for k in range(design):
            pivot = work[k : k + 1, :] / work[k : k + 1, k : k + 1]
            work = jnp.where(row == k, pivot, work - work[:, k : k + 1] * pivot)
        solved = pltpu.roll(work, LANES - shift, 1)
        solved = jnp.where((lane < design) & (row < design), solved, 0.0)
        inverse[...] = solved
        square_inverse = jnp.concatenate(
            [solved, jnp.zeros((LANES - DPAD, LANES), jnp.float32)], axis=0
        )
        cross_gene = cross[:snps, :]
        fitted = jnp.dot(
            cross_gene, square_inverse, precision=HIGHEST, preferred_element_type=jnp.float32
        )
        rss = square[...] - jnp.sum(cross_gene * fitted, axis=1, keepdims=True)
        place = lax.broadcasted_iota(jnp.int32, (snps, LANES), 1)
        coef[...] = jnp.where(place == DPAD, rss, fitted)


def gene_side(blocks, design):
    devices, rows, subjects = blocks.shape
    snps = rows - DPAD
    step = min(devices, 16)
    return pl.pallas_call(
        functools.partial(gene_kernel, snps, design),
        out_shape=(
            jax.ShapeDtypeStruct((rows, devices * subjects), blocks.dtype),
            jax.ShapeDtypeStruct((snps, LANES), jnp.float32),
            jax.ShapeDtypeStruct((DPAD, LANES), jnp.float32),
        ),
        grid=(devices // step,),
        in_specs=[pl.BlockSpec((step, rows, subjects), lambda i: (i, 0, 0))],
        out_specs=(
            pl.BlockSpec((rows, step * subjects), lambda i: (0, i)),
            pl.BlockSpec((snps, LANES), lambda i: (0, 0)),
            pl.BlockSpec((DPAD, LANES), lambda i: (0, 0)),
        ),
        scratch_shapes=[
            pltpu.VMEM((rows, LANES), jnp.float32),
            pltpu.VMEM((snps, 1), jnp.float32),
        ],
        compiler_params=pltpu.CompilerParams(vmem_limit_bytes=VMEM_LIMIT),
        name="gene_side",
    )(blocks)


def test_kernel(snps, freedom, genes, columns, coef, inverse, out, sums, square):
    step = pl.program_id(1)
    values = columns[...]
    wide = values.astype(jnp.float32)
    partial = jnp.dot(genes[...], values, preferred_element_type=jnp.float32)
    partial_square = jnp.sum(wide * wide, axis=0, keepdims=True)

    @pl.when(step == 0)
    def _():
        sums[...] = partial
        square[...] = partial_square

    @pl.when(step > 0)
    def _():
        sums[...] += partial
        square[...] += partial_square

    @pl.when(step == pl.num_programs(1) - 1)
    def _():
        cross_image = sums[snps:, :]
        solved = jnp.dot(
            inverse[:, :DPAD], cross_image, precision=HIGHEST, preferred_element_type=jnp.float32
        )
        image_rss = square[...] - jnp.sum(cross_image * solved, axis=0, keepdims=True)
        numer = sums[:snps, :] - jnp.dot(
            coef[:, :DPAD], cross_image, precision=HIGHEST, preferred_element_type=jnp.float32
        )
        ratio = numer * lax.rsqrt(coef[:, DPAD : DPAD + 1] * image_rss)
        out[...] = ratio * jnp.sqrt(freedom / (1.0 - ratio * ratio))


def test_columns(genes, columns, coef, inverse, design):
    rows, subjects = genes.shape
    snps = rows - DPAD
    width = columns.shape[1]
    step = min(subjects, 2048)
    lanes = min(width, 256)
    freedom = float(subjects - design - 1)
    return pl.pallas_call(
        functools.partial(test_kernel, snps, freedom),
        out_shape=jax.ShapeDtypeStruct((snps, width), jnp.float32),
        grid=(width // lanes, subjects // step),
        in_specs=[
            pl.BlockSpec((rows, step), lambda j, k: (0, k)),
            pl.BlockSpec((step, lanes), lambda j, k: (k, j)),
            pl.BlockSpec((snps, LANES), lambda j, k: (0, 0)),
            pl.BlockSpec((DPAD, LANES), lambda j, k: (0, 0)),
        ],
        out_specs=pl.BlockSpec((snps, lanes), lambda j, k: (0, j)),
        scratch_shapes=[
            pltpu.VMEM((rows, lanes), jnp.float32),
            pltpu.VMEM((1, lanes), jnp.float32),
        ],
        compiler_params=pltpu.CompilerParams(vmem_limit_bytes=VMEM_LIMIT),
        name="test_columns",
    )(genes, columns, coef, inverse)


def on_device(images, genotypes, covariates, site_codes):
    subjects, maps, planes, plane = images.shape
    n_vox, n_snp = lax.axis_size("vox"), lax.axis_size("snp")
    snps = genotypes.shape[1]
    design = SITES + covariates.shape[1]
    per_vox = planes // n_vox
    one_hot = (jnp.arange(SITES)[:, None] == site_codes[None, :]).astype(jnp.bfloat16)
    tall = jnp.concatenate(
        [genotypes.T, one_hot, covariates.T, jnp.zeros((DPAD - design, subjects), jnp.bfloat16)],
        axis=0,
    )
    smoothed = smooth(images, n_vox, n_snp)
    columns = lax.all_to_all(smoothed, ("vox", "snp"), 0, 0, tiled=True)
    tall_all = lax.all_gather(lax.all_gather(tall, "snp"), "vox")
    tall_all = tall_all.reshape(n_vox * n_snp, snps + DPAD, subjects)
    genes, coef, inverse = gene_side(tall_all, design)
    columns = columns.reshape(n_vox * n_snp * subjects, columns.shape[2])
    stats = test_columns(genes, columns, coef, inverse, design)
    width = stats.shape[1]
    panel = snps // n_snp
    stats = lax.all_to_all(stats.reshape(n_snp, panel, width), "snp", 0, 0, tiled=True)
    stats = jnp.swapaxes(stats, 0, 1)
    return stats.reshape(panel, maps, per_vox, plane)


def solution(mesh):
    placed = (
        P(("group", "vox", "snp"), None, None, None),
        P(("group", "vox", "snp"), None),
        P(("group", "vox", "snp"), None),
        P(("group", "vox", "snp")),
    )
    return jax.shard_map(
        on_device,
        mesh=mesh,
        in_specs=placed,
        out_specs=P(("group", "snp"), None, "vox", None),
        check_vma=False,
    )
```

```python
import functools

import jax
import jax.numpy as jnp
import ml_dtypes
import numpy as np
from jax import lax
from jax.experimental import pallas as pl
from jax.experimental.pallas import tpu as pltpu
from jax.sharding import Mesh
from jax.sharding import PartitionSpec as P

SY = 16
SZ = 16
SITES = 4
REACH = 2
DPAD = 24
LANES = 128
SUBJ_TILE = 16
HIGHEST = lax.Precision.HIGHEST
VMEM_LIMIT = 56 * 2**20
SQUARE_ROW = 20
SCALE_LANE = DPAD
DRIFT_LANE = DPAD + 1
MEAN_ROW = 1
NORM_ROW = 8


def kernel_table(length):
    position = np.arange(length)
    offset = (position[:, None] - position[None, :]).astype(np.float32)
    weights = np.where(np.abs(offset) <= REACH, np.exp(-offset * offset / np.float32(2.0)), np.float32(0.0))
    total = sum(np.exp(-(k * k) / 2.0) for k in range(-REACH, REACH + 1))
    return (weights / np.float32(total)).astype(np.float32)


def plane_kernel(plane):
    row, depth = kernel_table(SY), kernel_table(SZ)
    table = row[:, None, :, None] * depth[None, :, None, :]
    return table.reshape(plane, plane).astype(ml_dtypes.bfloat16)


def row_order(maps, planes):
    rows = SUBJ_TILE * maps * planes
    source = np.arange(rows).reshape(SUBJ_TILE, maps * planes).T.reshape(-1)
    return np.eye(rows, dtype=np.float32)[source].astype(ml_dtypes.bfloat16)


def tree_sum(terms):
    while len(terms) > 1:
        terms = [terms[i] + terms[i + 1] for i in range(0, len(terms), 2)]
    return terms[0]


def params():
    return pltpu.CompilerParams(vmem_limit_bytes=VMEM_LIMIT)


def smooth_kernel(group, planes, per_vox, parts, width, images, order, table, out):
    plane = table.shape[0]
    subjects = images.shape[0]
    groups = images.shape[1] // (group * planes)
    near = kernel_table(2 * REACH + 1)[REACH]
    for tile in range(subjects // SUBJ_TILE):
        here = pl.ds(tile * SUBJ_TILE, SUBJ_TILE)
        for part in range(groups):
            rows = images[here, part * group * planes : (part + 1) * group * planes, :]
            rows = rows.reshape(SUBJ_TILE * group * planes, plane)
            rows = jnp.dot(order[...], rows, preferred_element_type=jnp.float32)
            inplane = jnp.dot(
                rows.astype(jnp.bfloat16), table[...], preferred_element_type=jnp.float32
            )
            for m in range(group):
                slabs = [
                    inplane[(m * planes + x) * SUBJ_TILE : (m * planes + x + 1) * SUBJ_TILE]
                    for x in range(planes)
                ]
                for x in range(planes):
                    total = slabs[x] * float(near[REACH])
                    for lag in range(1, REACH + 1):
                        sides = [slabs[i] for i in (x - lag, x + lag) if 0 <= i < planes]
                        if sides:
                            total = total + functools.reduce(jnp.add, sides) * float(
                                near[REACH + lag]
                            )
                    column = ((part * group + m) * per_vox + x % per_vox) * plane
                    target = (x // per_vox) * parts + column // width
                    first = column % width
                    out[target, here, first : first + plane] = total.astype(jnp.bfloat16)


def smooth(images, n_vox, parts):
    subjects, maps, planes, plane = images.shape
    per_vox = planes // n_vox
    width = maps * per_vox * plane // parts
    group = max(1, min(maps, 256 // (SUBJ_TILE * planes)))
    step = 32
    order = jnp.asarray(row_order(group, planes))
    table = jnp.asarray(plane_kernel(plane))
    return pl.pallas_call(
        functools.partial(smooth_kernel, group, planes, per_vox, parts, width),
        out_shape=jax.ShapeDtypeStruct((n_vox * parts, subjects, width), jnp.bfloat16),
        grid=(subjects // step,),
        in_specs=[
            pl.BlockSpec((step, maps * planes, plane), lambda i: (i, 0, 0)),
            pl.BlockSpec(order.shape, lambda i: (0, 0)),
            pl.BlockSpec(table.shape, lambda i: (0, 0)),
        ],
        out_specs=pl.BlockSpec((n_vox * parts, step, width), lambda i: (0, i, 0)),
        compiler_params=params(),
        name="smooth",
    )(images.reshape(subjects, maps * planes, plane), order, table)


def moments_kernel(snps, bits, me, blocks, joined, out):
    count = blocks.shape[0]
    rows = []
    for source in range(count):
        offset = jnp.bitwise_xor(me[0], source)
        index = 0
        for place, bit in enumerate(bits):
            index = index + ((offset >> bit) & 1) * (1 << place)
        rows.append(blocks[index])
    rows = jnp.concatenate(rows, axis=1)
    joined[...] = rows
    across = (((1,), (1,)), ((), ()))
    out[...] = jnp.zeros(out.shape, jnp.float32)
    out[:DPAD, : snps + DPAD] = lax.dot_general(
        rows[snps:], rows, across, preferred_element_type=jnp.float32
    )
    wide = rows[:snps].astype(jnp.float32)
    wide = wide * wide
    high = wide.astype(jnp.bfloat16)
    low = (wide - high.astype(jnp.float32)).astype(jnp.bfloat16)
    ones = jnp.ones((8, rows.shape[1]), jnp.bfloat16)
    squares = lax.dot_general(ones, high, across, preferred_element_type=jnp.float32)
    squares = squares + lax.dot_general(ones, low, across, preferred_element_type=jnp.float32)
    out[DPAD:, :snps] = squares


def moments(blocks, bits, me):
    count, rows, subjects = blocks.shape
    snps = rows - DPAD
    spread = -(-rows // LANES) * LANES
    return pl.pallas_call(
        functools.partial(moments_kernel, snps, bits),
        out_shape=(
            jax.ShapeDtypeStruct((rows, count * subjects), blocks.dtype),
            jax.ShapeDtypeStruct((DPAD + 8, spread), jnp.float32),
        ),
        in_specs=[
            pl.BlockSpec(memory_space=pltpu.SMEM),
            pl.BlockSpec(memory_space=pltpu.VMEM),
        ],
        compiler_params=params(),
        name="moments",
    )(me, blocks)


def solve_kernel(snps, design, here, *refs):
    parts, (coef, inverse, rows_out) = refs[:-3], refs[-3:]
    total = tree_sum([part[...] for part in parts])
    lane = lax.broadcasted_iota(jnp.int32, (DPAD, LANES), 1)
    row = lax.broadcasted_iota(jnp.int32, (DPAD, LANES), 0)
    shift = 32
    work = total[:DPAD, snps : snps + LANES]
    work = jnp.where((row >= design) & (lane == row), 1.0, work)
    work = jnp.where(lane == row + shift, 1.0, work)
    for k in range(design):
        pivot = work[k : k + 1, :] / work[k : k + 1, k : k + 1]
        work = jnp.where(row == k, pivot, work - work[:, k : k + 1] * pivot)
    solved = pltpu.roll(work, LANES - shift, 1)
    solved = jnp.where((lane < design) & (row < design), solved, 0.0)
    inverse[...] = solved
    cross_gene = total[:DPAD, :snps]
    fitted = jnp.dot(
        solved[:, :DPAD], cross_gene, precision=HIGHEST, preferred_element_type=jnp.float32
    )
    rss = total[DPAD : DPAD + 1, :snps] - jnp.sum(cross_gene * fitted, axis=0, keepdims=True)
    scale = lax.rsqrt(rss)
    site = lax.broadcasted_iota(jnp.int32, (DPAD, snps), 0) < SITES
    rows_out[...] = jnp.zeros(rows_out.shape, jnp.float32)
    for j, part in enumerate(parts):
        mine = part[...]
        count = jnp.sum(
            jnp.where(lane < SITES, mine[:DPAD, snps : snps + LANES], 0.0), axis=1, keepdims=True
        )
        drift = jnp.sum(jnp.where(site, mine[:DPAD, :snps], 0.0), axis=0, keepdims=True)
        drift = (drift - jnp.sum(fitted * count, axis=0, keepdims=True)) * scale
        rows_out[DRIFT_LANE + j : DRIFT_LANE + j + 1, :] = drift
        if j == 0:
            rows_out[:DPAD, :] = fitted * scale + jnp.where(site, drift * (1.0 / here), 0.0)
    rows_out[SCALE_LANE : SCALE_LANE + 1, :] = scale
    coef[...] = jnp.transpose(rows_out[...])


def solve(parts, snps, design, here):
    return pl.pallas_call(
        functools.partial(solve_kernel, snps, design, here),
        out_shape=(
            jax.ShapeDtypeStruct((snps, LANES), jnp.float32),
            jax.ShapeDtypeStruct((DPAD, LANES), jnp.float32),
        ),
        scratch_shapes=[pltpu.VMEM((LANES, snps), jnp.float32)],
        compiler_params=params(),
        name="solve",
    )(*parts)


def column_norm(sums, here):
    square = sums[SQUARE_ROW : SQUARE_ROW + 1, :]
    mean = jnp.sum(sums[:SITES, :], axis=0, keepdims=True) * (1.0 / here)
    spread = jnp.maximum(square - mean * mean * here, square * 2.0**-10)
    return jnp.sqrt(spread + 1e-30), mean


def products_kernel(snps, here, me, genes, columns, coef, own, *refs):
    far, stats, held = refs[:-2], refs[-2], refs[-1]
    values = columns[...]
    wide = values.astype(jnp.float32)
    sums = jnp.dot(genes[...], values, preferred_element_type=jnp.float32)
    square = jnp.sum(wide * wide, axis=0, keepdims=True)
    cross_image = sums[snps:, :]
    row = lax.broadcasted_iota(jnp.int32, cross_image.shape, 0)
    cross_image = jnp.where(row == SQUARE_ROW, square, cross_image)
    stats[...] = cross_image
    norm, _ = column_norm(cross_image, here)
    lanes = lax.broadcasted_iota(jnp.int32, (snps, DPAD), 1)
    fit = jnp.where(lanes < SQUARE_ROW, coef[:, :DPAD], 0.0)
    held[...] = coef[:, SCALE_LANE : SCALE_LANE + 1] * sums[:snps, :] - jnp.dot(
        fit, cross_image, precision=HIGHEST, preferred_element_type=jnp.float32
    )
    size = own.shape[0]
    over = 1.0 / norm
    own[...] = held[pl.ds(pl.multiple_of(me[0] * size, size), size), :]
    for j, out in enumerate(far):
        place = jnp.bitwise_xor(me[0], j + 1)
        out[...] = held[pl.ds(pl.multiple_of(place * size, size), size), :] * over


def products(genes, columns, coef, me, count):
    rows, here = genes.shape
    snps = rows - DPAD
    width = columns.shape[1]
    lanes = min(width, 256)
    size = snps // count
    piece = jax.ShapeDtypeStruct((size, width), jnp.float32)
    piece_spec = pl.BlockSpec((size, lanes), lambda j: (0, j))
    return pl.pallas_call(
        functools.partial(products_kernel, snps, float(here)),
        out_shape=(piece,) * count + (jax.ShapeDtypeStruct((DPAD, width), jnp.float32),),
        grid=(width // lanes,),
        in_specs=[
            pl.BlockSpec(memory_space=pltpu.SMEM),
            pl.BlockSpec((rows, here), lambda j: (0, 0)),
            pl.BlockSpec((here, lanes), lambda j: (0, j)),
            pl.BlockSpec((snps, LANES), lambda j: (0, 0)),
        ],
        out_specs=(piece_spec,) * count + (pl.BlockSpec((DPAD, lanes), lambda j: (0, j)),),
        scratch_shapes=[pltpu.VMEM((snps, lanes), jnp.float32)],
        compiler_params=params(),
        name="products",
    )(me, genes, columns, coef)


def image_kernel(here, design, inverse, *refs):
    parts, out = refs[:-1], refs[-1]
    out[...] = jnp.zeros(out.shape, jnp.float32)
    total = tree_sum([part[...] for part in parts])
    row = lax.broadcasted_iota(jnp.int32, total.shape, 0)
    cross_image = jnp.where(row < design, total, 0.0)
    solved = jnp.dot(
        inverse[:, :DPAD], cross_image, precision=HIGHEST, preferred_element_type=jnp.float32
    )
    rss = total[SQUARE_ROW : SQUARE_ROW + 1, :] - jnp.sum(
        cross_image * solved, axis=0, keepdims=True
    )
    out[0:1, :] = lax.rsqrt(rss)
    for j, part in enumerate(parts):
        norm, mean = column_norm(part[...], here)
        out[MEAN_ROW + j : MEAN_ROW + j + 1, :] = mean
        out[NORM_ROW + j : NORM_ROW + j + 1, :] = norm


def image_side(inverse, parts, here, design):
    return pl.pallas_call(
        functools.partial(image_kernel, float(here), design),
        out_shape=jax.ShapeDtypeStruct((16, parts[0].shape[1]), jnp.float32),
        compiler_params=params(),
        name="image_side",
    )(inverse, *parts)


def permute_xor(value, axis, bits):
    size = lax.axis_size(axis)
    return lax.ppermute(value, axis, [(i, i ^ bits) for i in range(size)])


def on_device(images, genotypes, covariates, site_codes):
    subjects, maps, planes, plane = images.shape
    n_vox, n_far, n_near = (lax.axis_size(name) for name in ("vox", "far", "near"))
    vox, far, near = (lax.axis_index(name) for name in ("vox", "far", "near"))
    snps = genotypes.shape[1]
    design = SITES + covariates.shape[1]
    per_vox = planes // n_vox
    here = n_vox * n_near * subjects

    one_hot = (jnp.arange(SITES)[:, None] == site_codes[None, :]).astype(jnp.bfloat16)
    tall = jnp.concatenate(
        [genotypes.T, one_hot, covariates.T, jnp.zeros((DPAD - design, subjects), jnp.bfloat16)],
        axis=0,
    )[None]
    bits = []
    stages = [("near", b, b) for b in range(n_near.bit_length() - 1)]
    shift = n_near.bit_length() - 1
    stages += [("vox", b, b + shift) for b in reversed(range(n_vox.bit_length() - 1))]
    for axis, bit, place in stages:
        tall = jnp.concatenate([tall, permute_xor(tall, axis, 1 << bit)], axis=0)
        bits.append(place)

    smoothed = smooth(images, n_vox, n_near)
    columns = lax.all_to_all(smoothed, ("vox", "near"), 0, 0, tiled=True)
    columns = columns.reshape(here, columns.shape[2])

    genes, part = moments(tall, tuple(bits), (vox * n_near + near)[None])
    parts = [part] + [permute_xor(part, "far", j) for j in range(1, n_far)]
    coef, inverse = solve(parts, snps, design, float(here))

    *pieces, stats = products(genes, columns, coef, far[None], n_far)
    all_stats = [stats] + [permute_xor(stats, "far", j) for j in range(1, n_far)]
    received = [
        permute_xor(pieces[j].astype(jnp.float16), "far", j) for j in range(1, n_far)
    ]
    rows = image_side(inverse, all_stats, here, design)

    size = snps // n_far
    panel = size // n_near
    freedom = float(subjects * n_vox * n_near * n_far - design - 1)

    def panel_stats(index):
        first = index * panel
        lines = lax.dynamic_slice_in_dim(coef, far * size + first, panel, 0)
        ratio = lax.dynamic_slice_in_dim(pieces[0], first, panel, 0)
        for j in range(n_far):
            ratio = ratio + lines[:, DRIFT_LANE + j, None] * rows[None, MEAN_ROW + j]
            if j:
                piece = lax.dynamic_slice_in_dim(received[j - 1], first, panel, 0)
                ratio = ratio + piece.astype(jnp.float32) * rows[None, NORM_ROW + j]
        ratio = ratio * rows[None, 0]
        return ratio * jnp.sqrt(freedom / (1.0 - ratio * ratio))

    away = permute_xor(panel_stats(jnp.bitwise_xor(near, 1)), "near", 1)
    home = panel_stats(near)
    both = jnp.where(near == 0, jnp.stack([home, away], 1), jnp.stack([away, home], 1))
    return both.reshape(panel, maps, per_vox, plane)


def solution(mesh):
    sizes = dict(mesh.shape)
    devices = mesh.devices.reshape(sizes["group"], sizes["vox"], sizes["snp"] // 2, 2)
    split = Mesh(devices, ("group", "vox", "far", "near"))
    owner = ("group", "vox", "far", "near")
    placed = (P(owner, None, None, None), P(owner, None), P(owner, None), P(owner))
    return jax.shard_map(
        on_device,
        mesh=split,
        in_specs=placed,
        out_specs=P(("group", "far", "near"), None, "vox", None),
        check_vma=False,
    )
```

```python
import functools

import jax
import jax.numpy as jnp
import ml_dtypes
import numpy as np
from jax import lax
from jax.experimental import pallas as pl
from jax.experimental.pallas import tpu as pltpu
from jax.sharding import Mesh
from jax.sharding import PartitionSpec as P

SY = 16
SZ = 16
SITES = 4
REACH = 2
DPAD = 24
LANES = 128
SUBJ_TILE = 16
HIGHEST = lax.Precision.HIGHEST
VMEM_LIMIT = 56 * 2**20
SQUARE_ROW = 20
SCALE_LANE = DPAD
STRIDE = 32


def kernel_table(length):
    position = np.arange(length)
    offset = (position[:, None] - position[None, :]).astype(np.float32)
    weights = np.where(np.abs(offset) <= REACH, np.exp(-offset * offset / np.float32(2.0)), np.float32(0.0))
    total = sum(np.exp(-(k * k) / 2.0) for k in range(-REACH, REACH + 1))
    return (weights / np.float32(total)).astype(np.float32)


def plane_kernel(plane):
    row, depth = kernel_table(SY), kernel_table(SZ)
    table = row[:, None, :, None] * depth[None, :, None, :]
    return table.reshape(plane, plane).astype(ml_dtypes.bfloat16)


def row_order(maps, planes):
    rows = SUBJ_TILE * maps * planes
    source = np.arange(rows).reshape(SUBJ_TILE, maps * planes).T.reshape(-1)
    return np.eye(rows, dtype=np.float32)[source].astype(ml_dtypes.bfloat16)


def tree_sum(terms):
    while len(terms) > 1:
        terms = [terms[i] + terms[i + 1] for i in range(0, len(terms), 2)]
    return terms[0]


def params():
    return pltpu.CompilerParams(vmem_limit_bytes=VMEM_LIMIT)


def smooth_kernel(group, planes, per_vox, parts, width, images, order, table, out):
    plane = table.shape[0]
    subjects = images.shape[0]
    groups = images.shape[1] // (group * planes)
    near = kernel_table(2 * REACH + 1)[REACH]
    for tile in range(subjects // SUBJ_TILE):
        here = pl.ds(tile * SUBJ_TILE, SUBJ_TILE)
        for part in range(groups):
            rows = images[here, part * group * planes : (part + 1) * group * planes, :]
            rows = rows.reshape(SUBJ_TILE * group * planes, plane)
            rows = jnp.dot(order[...], rows, preferred_element_type=jnp.float32)
            inplane = jnp.dot(
                rows.astype(jnp.bfloat16), table[...], preferred_element_type=jnp.float32
            )
            for m in range(group):
                slabs = [
                    inplane[(m * planes + x) * SUBJ_TILE : (m * planes + x + 1) * SUBJ_TILE]
                    for x in range(planes)
                ]
                for x in range(planes):
                    total = slabs[x] * float(near[REACH])
                    for lag in range(1, REACH + 1):
                        sides = [slabs[i] for i in (x - lag, x + lag) if 0 <= i < planes]
                        if sides:
                            total = total + functools.reduce(jnp.add, sides) * float(
                                near[REACH + lag]
                            )
                    column = ((part * group + m) * per_vox + x % per_vox) * plane
                    target = (x // per_vox) * parts + column // width
                    first = column % width
                    out[target, here, first : first + plane] = total.astype(jnp.bfloat16)


def smooth(images, n_vox, parts):
    subjects, maps, planes, plane = images.shape
    per_vox = planes // n_vox
    width = maps * per_vox * plane // parts
    group = max(1, min(maps, 256 // (SUBJ_TILE * planes)))
    step = 32
    order = jnp.asarray(row_order(group, planes))
    table = jnp.asarray(plane_kernel(plane))
    return pl.pallas_call(
        functools.partial(smooth_kernel, group, planes, per_vox, parts, width),
        out_shape=jax.ShapeDtypeStruct((n_vox * parts, subjects, width), jnp.bfloat16),
        grid=(subjects // step,),
        in_specs=[
            pl.BlockSpec((step, maps * planes, plane), lambda i: (i, 0, 0)),
            pl.BlockSpec(order.shape, lambda i: (0, 0)),
            pl.BlockSpec(table.shape, lambda i: (0, 0)),
        ],
        out_specs=pl.BlockSpec((n_vox * parts, step, width), lambda i: (0, i, 0)),
        compiler_params=params(),
        name="smooth",
    )(images.reshape(subjects, maps * planes, plane), order, table)


def moments_kernel(snps, slots, me, blocks, joined, out):
    rows = []
    for source in range(len(slots)):
        offset = jnp.bitwise_xor(me[0], source)
        index = 0
        for place, slot in enumerate(slots):
            index = index + jnp.where(offset == place, slot, 0)
        rows.append(blocks[index])
    rows = jnp.concatenate(rows, axis=1)
    joined[...] = rows
    across = (((1,), (1,)), ((), ()))
    out[...] = jnp.zeros(out.shape, jnp.float32)
    out[:DPAD, : snps + DPAD] = lax.dot_general(
        rows[snps:], rows, across, preferred_element_type=jnp.float32
    )
    wide = rows[:snps].astype(jnp.float32)
    wide = wide * wide
    high = wide.astype(jnp.bfloat16)
    low = (wide - high.astype(jnp.float32)).astype(jnp.bfloat16)
    ones = jnp.ones((8, rows.shape[1]), jnp.bfloat16)
    squares = lax.dot_general(ones, high, across, preferred_element_type=jnp.float32)
    squares = squares + lax.dot_general(ones, low, across, preferred_element_type=jnp.float32)
    out[DPAD:, :snps] = squares


def moments(blocks, slots, me):
    count, rows, subjects = blocks.shape
    snps = rows - DPAD
    spread = -(-rows // LANES) * LANES
    return pl.pallas_call(
        functools.partial(moments_kernel, snps, slots),
        out_shape=(
            jax.ShapeDtypeStruct((rows, count * subjects), blocks.dtype),
            jax.ShapeDtypeStruct((DPAD + 8, spread), jnp.float32),
        ),
        in_specs=[
            pl.BlockSpec(memory_space=pltpu.SMEM),
            pl.BlockSpec(memory_space=pltpu.VMEM),
        ],
        compiler_params=params(),
        name="moments",
    )(me, blocks)


def eliminate(total, snps, design, guard):
    lane = lax.broadcasted_iota(jnp.int32, (DPAD, LANES), 1)
    row = lax.broadcasted_iota(jnp.int32, (DPAD, LANES), 0)
    shift = 32
    gram = total[:DPAD, snps : snps + LANES]
    work = jnp.where((row >= design) & (lane == row), 1.0, gram)
    work = jnp.where(lane == row + shift, 1.0, work)
    for k in range(design):
        pivot = work[k : k + 1, k : k + 1]
        line = work[k : k + 1, :] / pivot
        if guard:
            line = jnp.where(pivot > gram[k : k + 1, k : k + 1] * 2.0**-14, line, 0.0)
        work = jnp.where(row == k, line, work - work[:, k : k + 1] * line)
    solved = pltpu.roll(work, LANES - shift, 1)
    return jnp.where((lane < design) & (row < design), solved, 0.0)


def gene_fit(total, snps, design, guard):
    solved = eliminate(total, snps, design, guard)
    cross_gene = total[:DPAD, :snps]
    fitted = jnp.dot(
        solved[:, :DPAD], cross_gene, precision=HIGHEST, preferred_element_type=jnp.float32
    )
    square = total[DPAD : DPAD + 1, :snps]
    rss = square - jnp.sum(cross_gene * fitted, axis=0, keepdims=True)
    if guard:
        rss = jnp.maximum(rss, square * 2.0**-10) + 1e-30
    return solved, fitted, lax.rsqrt(rss)


def pair_kernel(snps, design, moment, coef, lines):
    _, fitted, scale = gene_fit(moment[...], snps, design, True)
    lines[...] = jnp.zeros(lines.shape, jnp.float32)
    lines[:DPAD, :] = fitted * scale
    lines[SCALE_LANE : SCALE_LANE + 1, :] = scale
    coef[...] = jnp.transpose(lines[...])


def pair_fit(moment, snps, design):
    return pl.pallas_call(
        functools.partial(pair_kernel, snps, design),
        out_shape=jax.ShapeDtypeStruct((snps, LANES), jnp.float32),
        scratch_shapes=[pltpu.VMEM((LANES, snps), jnp.float32)],
        compiler_params=params(),
        name="pair_fit",
    )(moment)


def cohort_kernel(snps, design, *refs):
    parts, (coef, inverse, lines) = refs[:-3], refs[-3:]
    moment = [part[...] for part in parts]
    solved, fitted, scale = gene_fit(tree_sum(moment), snps, design, False)
    inverse[...] = solved
    lines[...] = jnp.zeros(lines.shape, jnp.float32)
    lines[:DPAD, :] = fitted * -scale
    lines[SCALE_LANE : SCALE_LANE + 1, :] = scale
    for j in range(1, len(parts)):
        _, fit, own_scale = gene_fit(moment[j], snps, design, True)
        lines[j * STRIDE : j * STRIDE + DPAD, :] = fit * scale
        lines[SCALE_LANE + j : SCALE_LANE + j + 1, :] = scale / own_scale
    coef[...] = jnp.transpose(lines[...])


def cohort_fit(parts, snps, design):
    return pl.pallas_call(
        functools.partial(cohort_kernel, snps, design),
        out_shape=(
            jax.ShapeDtypeStruct((snps, LANES), jnp.float32),
            jax.ShapeDtypeStruct((DPAD, LANES), jnp.float32),
        ),
        scratch_shapes=[pltpu.VMEM((LANES, snps), jnp.float32)],
        compiler_params=params(),
        name="cohort_fit",
    )(*parts)


def column_norm(sums, here):
    square = sums[SQUARE_ROW : SQUARE_ROW + 1, :]
    mean = jnp.sum(sums[:SITES, :], axis=0, keepdims=True) * (1.0 / here)
    spread = jnp.maximum(square - mean * mean * here, square * 2.0**-10)
    return jnp.sqrt(spread + 1e-30)


def products_kernel(here, me, genes, columns, coef, own, *refs):
    far, stats, held = refs[:-2], refs[-2], refs[-1]
    values = columns[...]
    wide = values.astype(jnp.float32)
    sums = jnp.dot(genes[...], values, preferred_element_type=jnp.float32)
    snps = held.shape[0]
    held[...] = sums[:snps, :]
    square = jnp.sum(wide * wide, axis=0, keepdims=True)
    cross_image = sums[snps:, :]
    row = lax.broadcasted_iota(jnp.int32, cross_image.shape, 0)
    cross_image = jnp.where(row == SQUARE_ROW, square, cross_image)
    stats[...] = cross_image
    over = 1.0 / column_norm(cross_image, here)
    size = own.shape[0]
    own[...] = held[pl.ds(pl.multiple_of(me[0] * size, size), size), :]
    for j, out in enumerate(far):
        place = pl.multiple_of(jnp.bitwise_xor(me[0], j + 1) * size, size)
        line = coef[pl.ds(place, size), :]
        fit = jnp.dot(
            line[:, :DPAD], cross_image, precision=HIGHEST, preferred_element_type=jnp.float32
        )
        scale = line[:, SCALE_LANE : SCALE_LANE + 1]
        out[...] = (scale * held[pl.ds(place, size), :] - fit) * over


def products(genes, columns, coef, me, count):
    rows, here = genes.shape
    snps = rows - DPAD
    width = columns.shape[1]
    lanes = min(width, 256)
    size = snps // count
    piece = jax.ShapeDtypeStruct((size, width), jnp.float32)
    piece_spec = pl.BlockSpec((size, lanes), lambda j: (0, j))
    return pl.pallas_call(
        functools.partial(products_kernel, float(here)),
        out_shape=(piece,) * count + (jax.ShapeDtypeStruct((DPAD, width), jnp.float32),),
        grid=(width // lanes,),
        in_specs=[
            pl.BlockSpec(memory_space=pltpu.SMEM),
            pl.BlockSpec((rows, here), lambda j: (0, 0)),
            pl.BlockSpec((here, lanes), lambda j: (0, j)),
            pl.BlockSpec((snps, LANES), lambda j: (0, 0)),
        ],
        out_specs=(piece_spec,) * count + (pl.BlockSpec((DPAD, lanes), lambda j: (0, j)),),
        scratch_shapes=[pltpu.VMEM((snps, lanes), jnp.float32)],
        compiler_params=params(),
        name="products",
    )(me, genes, columns, coef)


def base_kernel(here, me, own, coef, inverse, *refs):
    parts, (base, factors, stack) = refs[:-3], refs[-3:]
    stats = [part[...] for part in parts]
    row = lax.broadcasted_iota(jnp.int32, stats[0].shape, 0)
    total = tree_sum(stats)
    cross_image = jnp.where(row < SQUARE_ROW, total, 0.0)
    solved = jnp.dot(
        inverse[:, :DPAD], cross_image, precision=HIGHEST, preferred_element_type=jnp.float32
    )
    rss = total[SQUARE_ROW : SQUARE_ROW + 1, :] - jnp.sum(
        cross_image * solved, axis=0, keepdims=True
    )
    scale = lax.rsqrt(rss)
    stack[...] = jnp.zeros(stack.shape, jnp.float32)
    stack[:DPAD, :] = cross_image
    factors[...] = jnp.zeros(factors.shape, jnp.float32)
    for j in range(1, len(parts)):
        stack[j * STRIDE : j * STRIDE + DPAD, :] = jnp.where(row < SQUARE_ROW, stats[j], 0.0)
        factors[j : j + 1, :] = column_norm(stats[j], here) * scale
    size = own.shape[0]
    line = coef[pl.ds(pl.multiple_of(me[0] * size, size), size), :]
    terms = jnp.dot(line, stack[...], precision=HIGHEST, preferred_element_type=jnp.float32)
    base[...] = (line[:, SCALE_LANE : SCALE_LANE + 1] * own[...] + terms) * scale


def base_ratio(me, own, coef, inverse, parts, here):
    size, width = own.shape
    lanes = min(width, 256)
    snps = coef.shape[0]
    stat_spec = pl.BlockSpec((DPAD, lanes), lambda j: (0, j))
    return pl.pallas_call(
        functools.partial(base_kernel, float(here)),
        out_shape=(
            jax.ShapeDtypeStruct((size, width), jnp.float32),
            jax.ShapeDtypeStruct((8, width), jnp.float32),
        ),
        grid=(width // lanes,),
        in_specs=[
            pl.BlockSpec(memory_space=pltpu.SMEM),
            pl.BlockSpec((size, lanes), lambda j: (0, j)),
            pl.BlockSpec((snps, LANES), lambda j: (0, 0)),
            pl.BlockSpec((DPAD, LANES), lambda j: (0, 0)),
        ]
        + [stat_spec] * len(parts),
        out_specs=(
            pl.BlockSpec((size, lanes), lambda j: (0, j)),
            pl.BlockSpec((8, lanes), lambda j: (0, j)),
        ),
        scratch_shapes=[pltpu.VMEM((LANES, lanes), jnp.float32)],
        compiler_params=params(),
        name="base_ratio",
    )(me, own, coef, inverse, *parts)


def permute_xor(value, axes, bits):
    size = lax.axis_size(axes)
    return lax.ppermute(value, axes, [(i, i ^ bits) for i in range(size)])


def on_device(images, genotypes, covariates, site_codes):
    subjects, maps, planes, plane = images.shape
    n_vox, n_far, n_near = (lax.axis_size(name) for name in ("vox", "far", "near"))
    vox, far, near = (lax.axis_index(name) for name in ("vox", "far", "near"))
    snps = genotypes.shape[1]
    design = SITES + covariates.shape[1]
    per_vox = planes // n_vox
    count = n_vox * n_near
    here = count * subjects

    one_hot = (jnp.arange(SITES)[:, None] == site_codes[None, :]).astype(jnp.bfloat16)
    tall = jnp.concatenate(
        [genotypes.T, one_hot, covariates.T, jnp.zeros((DPAD - design, subjects), jnp.bfloat16)],
        axis=0,
    )
    other = n_near
    offsets = [o for o in range(count) if not o & other]
    blocks = [tall] + [permute_xor(tall, ("vox", "near"), o) for o in offsets[1:]]
    smoothed = smooth(images, n_vox, n_near)
    smoothed, *blocks = lax.optimization_barrier((smoothed, *blocks))
    columns = lax.all_to_all(smoothed, ("vox", "near"), 0, 0, tiled=True)
    columns = columns.reshape(here, columns.shape[2])
    blocks = jnp.stack(blocks)
    blocks = jnp.concatenate([blocks, permute_xor(blocks, ("vox", "near"), other)], axis=0)
    order = offsets + [o | other for o in offsets]
    slots = tuple(order.index(o) for o in range(count))

    genes, moment = moments(blocks, slots, (vox * n_near + near)[None])
    pair_coef = pair_fit(moment, snps, design)
    moment_parts = [moment] + [permute_xor(moment, "far", j) for j in range(1, n_far)]

    own, *pieces, stats = products(genes, columns, pair_coef, far[None], n_far)
    stat_parts = [stats] + [permute_xor(stats, "far", j) for j in range(1, n_far)]
    pieces = [
        permute_xor(pieces[j - 1].astype(jnp.float16), "far", j) for j in range(1, n_far)
    ]
    coef, inverse = cohort_fit(moment_parts, snps, design)
    base, factors = base_ratio(far[None], own, coef, inverse, stat_parts, here)

    size = snps // n_far
    panel = size // n_near
    freedom = float(here * n_far - design - 1)

    def panel_stats(index):
        first = index * panel
        line = lax.dynamic_slice_in_dim(coef, far * size + first, panel, 0)
        ratio = lax.dynamic_slice_in_dim(base, first, panel, 0)
        for j in range(1, n_far):
            piece = lax.dynamic_slice_in_dim(pieces[j - 1], first, panel, 0)
            weight = line[:, SCALE_LANE + j, None] * factors[None, j]
            ratio = ratio + piece.astype(jnp.float32) * weight
        return ratio * jnp.sqrt(freedom / (1.0 - ratio * ratio))

    away = permute_xor(panel_stats(jnp.bitwise_xor(near, 1)), "near", 1)
    home = panel_stats(near)
    both = jnp.where(near == 0, jnp.stack([home, away], 1), jnp.stack([away, home], 1))
    return both.reshape(panel, maps, per_vox, plane)


def solution(mesh):
    sizes = dict(mesh.shape)
    devices = mesh.devices.reshape(sizes["group"], sizes["vox"], sizes["snp"] // 2, 2)
    split = Mesh(devices, ("group", "vox", "far", "near"))
    owner = ("group", "vox", "far", "near")
    placed = (P(owner, None, None, None), P(owner, None), P(owner, None), P(owner))
    return jax.shard_map(
        on_device,
        mesh=split,
        in_specs=placed,
        out_specs=P(("group", "far", "near"), None, "vox", None),
        check_vma=False,
    )
```

```python
import functools

import jax
import jax.numpy as jnp
import ml_dtypes
import numpy as np
from jax import lax
from jax.experimental import pallas as pl
from jax.experimental.pallas import tpu as pltpu
from jax.sharding import Mesh
from jax.sharding import PartitionSpec as P

SY = 16
SZ = 16
SITES = 4
REACH = 2
DPAD = 24
LANES = 128
SUBJ_TILE = 16
HIGHEST = lax.Precision.HIGHEST
VMEM_LIMIT = 56 * 2**20
SQUARE_ROW = 20
CHUNKS = 2
SCALE_LANE = DPAD
STRIDE = 32


def kernel_table(length):
    position = np.arange(length)
    offset = (position[:, None] - position[None, :]).astype(np.float32)
    weights = np.where(np.abs(offset) <= REACH, np.exp(-offset * offset / np.float32(2.0)), np.float32(0.0))
    total = sum(np.exp(-(k * k) / 2.0) for k in range(-REACH, REACH + 1))
    return (weights / np.float32(total)).astype(np.float32)


def plane_kernel(plane):
    row, depth = kernel_table(SY), kernel_table(SZ)
    table = row[:, None, :, None] * depth[None, :, None, :]
    return table.reshape(plane, plane).astype(ml_dtypes.bfloat16)


def row_order(rows, picked, planes):
    source = [s * rows + m * planes + x for m in picked for x in range(planes) for s in range(SUBJ_TILE)]
    return np.eye(SUBJ_TILE * rows, dtype=np.float32)[source].astype(ml_dtypes.bfloat16)


def tree_sum(terms):
    while len(terms) > 1:
        terms = [terms[i] + terms[i + 1] for i in range(0, len(terms), 2)]
    return terms[0]


def params():
    return pltpu.CompilerParams(vmem_limit_bytes=VMEM_LIMIT)


def smooth_kernel(groups, planes, per_vox, parts, width, chunks, images, order, table, out):
    plane = table.shape[0]
    size = out.shape[2]
    near = kernel_table(2 * REACH + 1)[REACH]
    for tile in range(images.shape[0] // SUBJ_TILE):
        here = pl.ds(tile * SUBJ_TILE, SUBJ_TILE)
        for start, stop, maps in groups:
            rows = images[here, start:stop, :].reshape(SUBJ_TILE * (stop - start), plane)
            rows = jnp.dot(order[...], rows, preferred_element_type=jnp.float32)
            inplane = jnp.dot(
                rows.astype(jnp.bfloat16), table[...], preferred_element_type=jnp.float32
            )
            for i, m in enumerate(maps):
                slabs = [
                    inplane[(i * planes + x) * SUBJ_TILE : (i * planes + x + 1) * SUBJ_TILE]
                    for x in range(planes)
                ]
                for x in range(planes):
                    total = slabs[x] * float(near[REACH])
                    for lag in range(1, REACH + 1):
                        sides = [slabs[k] for k in (x - lag, x + lag) if 0 <= k < planes]
                        if sides:
                            total = total + functools.reduce(jnp.add, sides) * float(
                                near[REACH + lag]
                            )
                    column = (m * per_vox + x % per_vox) * plane
                    target = (x // per_vox) * parts + column // width
                    first = column % size
                    out[target, here, first : first + plane] = total.astype(jnp.bfloat16)


def smooth(images, n_vox, parts, chunk, chunks):
    subjects, maps, planes, plane = images.shape
    per_vox = planes // n_vox
    width = maps * per_vox * plane // parts
    size = width // chunks
    assert size % (per_vox * plane) == 0
    picked = [m for m in range(maps) if m * per_vox * plane % width // size == chunk]
    if SUBJ_TILE * planes * len(picked) <= 256:
        groups = [(0, maps * planes, picked)]
        order = row_order(maps * planes, picked, planes)
    else:
        groups = [(m * planes, (m + 1) * planes, [m]) for m in picked]
        order = row_order(planes, [0], planes)
    step = 32
    order = jnp.asarray(order)
    table = jnp.asarray(plane_kernel(plane))
    return pl.pallas_call(
        functools.partial(smooth_kernel, groups, planes, per_vox, parts, width, chunks),
        out_shape=jax.ShapeDtypeStruct((n_vox * parts, subjects, size), jnp.bfloat16),
        grid=(subjects // step,),
        in_specs=[
            pl.BlockSpec((step, maps * planes, plane), lambda i: (i, 0, 0)),
            pl.BlockSpec(order.shape, lambda i: (0, 0)),
            pl.BlockSpec(table.shape, lambda i: (0, 0)),
        ],
        out_specs=pl.BlockSpec((n_vox * parts, step, size), lambda i: (0, i, 0)),
        compiler_params=params(),
        name="smooth",
    )(images.reshape(subjects, maps * planes, plane), order, table)


def moments_kernel(snps, slots, me, blocks, joined, out):
    rows = []
    for source in range(len(slots)):
        offset = jnp.bitwise_xor(me[0], source)
        index = 0
        for place, slot in enumerate(slots):
            index = index + jnp.where(offset == place, slot, 0)
        rows.append(blocks[index])
    rows = jnp.concatenate(rows, axis=1)
    joined[...] = rows
    across = (((1,), (1,)), ((), ()))
    out[...] = jnp.zeros(out.shape, jnp.float32)
    out[:DPAD, : snps + DPAD] = lax.dot_general(
        rows[snps:], rows, across, preferred_element_type=jnp.float32
    )
    wide = rows[:snps].astype(jnp.float32)
    wide = wide * wide
    high = wide.astype(jnp.bfloat16)
    low = (wide - high.astype(jnp.float32)).astype(jnp.bfloat16)
    ones = jnp.ones((8, rows.shape[1]), jnp.bfloat16)
    squares = lax.dot_general(ones, high, across, preferred_element_type=jnp.float32)
    squares = squares + lax.dot_general(ones, low, across, preferred_element_type=jnp.float32)
    out[DPAD:, :snps] = squares


def moments(blocks, slots, me):
    count, rows, subjects = blocks.shape
    snps = rows - DPAD
    spread = -(-rows // LANES) * LANES
    return pl.pallas_call(
        functools.partial(moments_kernel, snps, slots),
        out_shape=(
            jax.ShapeDtypeStruct((rows, count * subjects), blocks.dtype),
            jax.ShapeDtypeStruct((DPAD + 8, spread), jnp.float32),
        ),
        in_specs=[
            pl.BlockSpec(memory_space=pltpu.SMEM),
            pl.BlockSpec(memory_space=pltpu.VMEM),
        ],
        compiler_params=params(),
        name="moments",
    )(me, blocks)


def eliminate(total, snps, design, guard):
    lane = lax.broadcasted_iota(jnp.int32, (DPAD, LANES), 1)
    row = lax.broadcasted_iota(jnp.int32, (DPAD, LANES), 0)
    shift = 32
    gram = total[:DPAD, snps : snps + LANES]
    work = jnp.where((row >= design) & (lane == row), 1.0, gram)
    work = jnp.where(lane == row + shift, 1.0, work)
    for k in range(design):
        pivot = work[k : k + 1, k : k + 1]
        line = work[k : k + 1, :] / pivot
        if guard:
            line = jnp.where(pivot > gram[k : k + 1, k : k + 1] * 2.0**-14, line, 0.0)
        work = jnp.where(row == k, line, work - work[:, k : k + 1] * line)
    solved = pltpu.roll(work, LANES - shift, 1)
    return jnp.where((lane < design) & (row < design), solved, 0.0)


def gene_fit(total, snps, design, guard):
    solved = eliminate(total, snps, design, guard)
    cross_gene = total[:DPAD, :snps]
    fitted = jnp.dot(
        solved[:, :DPAD], cross_gene, precision=HIGHEST, preferred_element_type=jnp.float32
    )
    square = total[DPAD : DPAD + 1, :snps]
    rss = square - jnp.sum(cross_gene * fitted, axis=0, keepdims=True)
    if guard:
        rss = jnp.maximum(rss, square * 2.0**-10) + 1e-30
    return solved, fitted, lax.rsqrt(rss)


def pair_kernel(snps, design, moment, coef, lines):
    _, fitted, scale = gene_fit(moment[...], snps, design, True)
    lines[...] = jnp.zeros(lines.shape, jnp.float32)
    lines[:DPAD, :] = fitted * scale
    lines[SCALE_LANE : SCALE_LANE + 1, :] = scale
    coef[...] = jnp.transpose(lines[...])


def pair_fit(moment, snps, design):
    return pl.pallas_call(
        functools.partial(pair_kernel, snps, design),
        out_shape=jax.ShapeDtypeStruct((snps, LANES), jnp.float32),
        scratch_shapes=[pltpu.VMEM((LANES, snps), jnp.float32)],
        compiler_params=params(),
        name="pair_fit",
    )(moment)


def cohort_kernel(snps, design, *refs):
    parts, (coef, inverse, lines) = refs[:-3], refs[-3:]
    moment = [part[...] for part in parts]
    solved, fitted, scale = gene_fit(tree_sum(moment), snps, design, False)
    inverse[...] = solved
    lines[...] = jnp.zeros(lines.shape, jnp.float32)
    lines[:DPAD, :] = fitted * -scale
    lines[SCALE_LANE : SCALE_LANE + 1, :] = scale
    for j in range(1, len(parts)):
        _, fit, own_scale = gene_fit(moment[j], snps, design, True)
        lines[j * STRIDE : j * STRIDE + DPAD, :] = fit * scale
        lines[SCALE_LANE + j : SCALE_LANE + j + 1, :] = scale / own_scale
    coef[...] = jnp.transpose(lines[...])


def cohort_fit(parts, snps, design):
    return pl.pallas_call(
        functools.partial(cohort_kernel, snps, design),
        out_shape=(
            jax.ShapeDtypeStruct((snps, LANES), jnp.float32),
            jax.ShapeDtypeStruct((DPAD, LANES), jnp.float32),
        ),
        scratch_shapes=[pltpu.VMEM((LANES, snps), jnp.float32)],
        compiler_params=params(),
        name="cohort_fit",
    )(*parts)


def column_norm(sums, here):
    square = sums[SQUARE_ROW : SQUARE_ROW + 1, :]
    mean = jnp.sum(sums[:SITES, :], axis=0, keepdims=True) * (1.0 / here)
    spread = jnp.maximum(square - mean * mean * here, square * 2.0**-10)
    return jnp.sqrt(spread + 1e-30)


def products_kernel(here, me, genes, columns, coef, own, *refs):
    far, stats, held = refs[:-2], refs[-2], refs[-1]
    values = columns[...]
    wide = values.astype(jnp.float32)
    sums = jnp.dot(genes[...], values, preferred_element_type=jnp.float32)
    snps = held.shape[0]
    held[...] = sums[:snps, :]
    square = jnp.sum(wide * wide, axis=0, keepdims=True)
    cross_image = sums[snps:, :]
    row = lax.broadcasted_iota(jnp.int32, cross_image.shape, 0)
    cross_image = jnp.where(row == SQUARE_ROW, square, cross_image)
    stats[...] = cross_image
    over = 1.0 / column_norm(cross_image, here)
    size = own.shape[0]
    own[...] = held[pl.ds(pl.multiple_of(me[0] * size, size), size), :]
    for j, out in enumerate(far):
        place = pl.multiple_of(jnp.bitwise_xor(me[0], j + 1) * size, size)
        line = coef[pl.ds(place, size), :]
        fit = jnp.dot(
            line[:, :DPAD], cross_image, precision=HIGHEST, preferred_element_type=jnp.float32
        )
        scale = line[:, SCALE_LANE : SCALE_LANE + 1]
        out[...] = (scale * held[pl.ds(place, size), :] - fit) * over


def products(genes, columns, coef, me, count):
    rows, here = genes.shape
    snps = rows - DPAD
    width = columns.shape[1]
    lanes = min(width, 256)
    size = snps // count
    piece = jax.ShapeDtypeStruct((size, width), jnp.float32)
    piece_spec = pl.BlockSpec((size, lanes), lambda j: (0, j))
    return pl.pallas_call(
        functools.partial(products_kernel, float(here)),
        out_shape=(piece,) * count + (jax.ShapeDtypeStruct((DPAD, width), jnp.float32),),
        grid=(width // lanes,),
        in_specs=[
            pl.BlockSpec(memory_space=pltpu.SMEM),
            pl.BlockSpec((rows, here), lambda j: (0, 0)),
            pl.BlockSpec((here, lanes), lambda j: (0, j)),
            pl.BlockSpec((snps, LANES), lambda j: (0, 0)),
        ],
        out_specs=(piece_spec,) * count + (pl.BlockSpec((DPAD, lanes), lambda j: (0, j)),),
        scratch_shapes=[pltpu.VMEM((snps, lanes), jnp.float32)],
        compiler_params=params(),
        name="products",
    )(me, genes, columns, coef)


def base_kernel(here, me, own, coef, inverse, *refs):
    parts, (base, factors, stack) = refs[:-3], refs[-3:]
    stats = [part[...] for part in parts]
    row = lax.broadcasted_iota(jnp.int32, stats[0].shape, 0)
    total = tree_sum(stats)
    cross_image = jnp.where(row < SQUARE_ROW, total, 0.0)
    solved = jnp.dot(
        inverse[:, :DPAD], cross_image, precision=HIGHEST, preferred_element_type=jnp.float32
    )
    rss = total[SQUARE_ROW : SQUARE_ROW + 1, :] - jnp.sum(
        cross_image * solved, axis=0, keepdims=True
    )
    scale = lax.rsqrt(rss)
    stack[...] = jnp.zeros(stack.shape, jnp.float32)
    stack[:DPAD, :] = cross_image
    factors[...] = jnp.zeros(factors.shape, jnp.float32)
    for j in range(1, len(parts)):
        stack[j * STRIDE : j * STRIDE + DPAD, :] = jnp.where(row < SQUARE_ROW, stats[j], 0.0)
        factors[j : j + 1, :] = column_norm(stats[j], here) * scale
    size = own.shape[0]
    line = coef[pl.ds(pl.multiple_of(me[0] * size, size), size), :]
    terms = jnp.dot(line, stack[...], precision=HIGHEST, preferred_element_type=jnp.float32)
    base[...] = (line[:, SCALE_LANE : SCALE_LANE + 1] * own[...] + terms) * scale


def base_ratio(me, own, coef, inverse, parts, here):
    size, width = own.shape
    lanes = min(width, 256)
    snps = coef.shape[0]
    stat_spec = pl.BlockSpec((DPAD, lanes), lambda j: (0, j))
    return pl.pallas_call(
        functools.partial(base_kernel, float(here)),
        out_shape=(
            jax.ShapeDtypeStruct((size, width), jnp.float32),
            jax.ShapeDtypeStruct((8, width), jnp.float32),
        ),
        grid=(width // lanes,),
        in_specs=[
            pl.BlockSpec(memory_space=pltpu.SMEM),
            pl.BlockSpec((size, lanes), lambda j: (0, j)),
            pl.BlockSpec((snps, LANES), lambda j: (0, 0)),
            pl.BlockSpec((DPAD, LANES), lambda j: (0, 0)),
        ]
        + [stat_spec] * len(parts),
        out_specs=(
            pl.BlockSpec((size, lanes), lambda j: (0, j)),
            pl.BlockSpec((8, lanes), lambda j: (0, j)),
        ),
        scratch_shapes=[pltpu.VMEM((LANES, lanes), jnp.float32)],
        compiler_params=params(),
        name="base_ratio",
    )(me, own, coef, inverse, *parts)


def permute_xor(value, axes, bits):
    size = lax.axis_size(axes)
    return lax.ppermute(value, axes, [(i, i ^ bits) for i in range(size)])


def on_device(images, genotypes, covariates, site_codes):
    subjects, maps, planes, plane = images.shape
    n_vox, n_far, n_near = (lax.axis_size(name) for name in ("vox", "far", "near"))
    vox, far, near = (lax.axis_index(name) for name in ("vox", "far", "near"))
    snps = genotypes.shape[1]
    design = SITES + covariates.shape[1]
    per_vox = planes // n_vox
    count = n_vox * n_near
    here = count * subjects

    one_hot = (jnp.arange(SITES)[:, None] == site_codes[None, :]).astype(jnp.bfloat16)
    tall = jnp.concatenate(
        [genotypes.T, one_hot, covariates.T, jnp.zeros((DPAD - design, subjects), jnp.bfloat16)],
        axis=0,
    )
    other = n_near
    offsets = [o for o in range(count) if not o & other]
    blocks = [tall] + [permute_xor(tall, ("vox", "near"), o) for o in offsets[1:]]
    smoothed = smooth(images, n_vox, n_near, 0, CHUNKS)
    smoothed, *blocks = lax.optimization_barrier((smoothed, *blocks))

    def exchange(value):
        value = lax.all_to_all(value, ("vox", "near"), 0, 0, tiled=True)
        return value.reshape(here, value.shape[2])

    columns = [exchange(smoothed)]
    blocks = jnp.stack(blocks)
    blocks = jnp.concatenate([blocks, permute_xor(blocks, ("vox", "near"), other)], axis=0)
    order = offsets + [o | other for o in offsets]
    slots = tuple(order.index(o) for o in range(count))
    genes, moment = moments(blocks, slots, (vox * n_near + near)[None])
    pair_coef = pair_fit(moment, snps, design)
    moment_parts = [moment] + [permute_xor(moment, "far", j) for j in range(1, n_far)]
    for chunk in range(1, CHUNKS):
        smoothed = smooth(images, n_vox, n_near, chunk, CHUNKS)
        smoothed, columns[-1], pair_coef, *moment_parts = lax.optimization_barrier(
            (smoothed, columns[-1], pair_coef, *moment_parts)
        )
        columns.append(exchange(smoothed))
    coef, inverse = cohort_fit(moment_parts, snps, design)

    size = snps // n_far
    panel = size // n_near
    freedom = float(here * n_far - design - 1)

    def send(pieces):
        return [permute_xor(pieces[j - 1], "far", j) for j in range(1, n_far)]

    def panel_stats(index, base, factors, pieces):
        first = index * panel
        line = lax.dynamic_slice_in_dim(coef, far * size + first, panel, 0)
        ratio = lax.dynamic_slice_in_dim(base, first, panel, 0)
        for j in range(1, n_far):
            piece = lax.dynamic_slice_in_dim(pieces[j - 1], first, panel, 0)
            weight = line[:, SCALE_LANE + j, None] * factors[None, j]
            ratio = ratio + piece.astype(jnp.float32) * weight
        return ratio * jnp.sqrt(freedom / (1.0 - ratio * ratio))

    owns, received, sums = [], [], []
    for chunk in range(CHUNKS):
        own, *pieces, stats = products(genes, columns[chunk], pair_coef, far[None], n_far)
        pieces = [piece.astype(jnp.float16) for piece in pieces]
        owns.append(own)
        sums.append([stats] + [permute_xor(stats, "far", j) for j in range(1, n_far)])
        if chunk == CHUNKS - 1:
            sums, pieces = lax.optimization_barrier((sums, pieces))
        received.append(send(pieces))
    outs = []
    gate = None
    for chunk in range(CHUNKS):
        base, factors = base_ratio(far[None], owns[chunk], coef, inverse, sums[chunk], here)
        if gate is not None:
            base, gate = lax.optimization_barrier((base, gate))
            outs[-1][0] = gate
        pieces = received[chunk]
        gate = panel_stats(jnp.bitwise_xor(near, 1), base, factors, pieces)
        outs.append([gate, panel_stats(near, base, factors, pieces)])
    outs = [(permute_xor(away, "near", 1), home) for away, home in outs]
    outs = [
        jnp.where(near == 0, jnp.stack([home, away], 1), jnp.stack([away, home], 1))
        for away, home in outs
    ]
    return jnp.stack(outs, axis=2).reshape(panel, maps, per_vox, plane)


def solution(mesh):
    sizes = dict(mesh.shape)
    devices = mesh.devices.reshape(sizes["group"], sizes["vox"], sizes["snp"] // 2, 2)
    split = Mesh(devices, ("group", "vox", "far", "near"))
    owner = ("group", "vox", "far", "near")
    placed = (P(owner, None, None, None), P(owner, None), P(owner, None), P(owner))
    return jax.shard_map(
        on_device,
        mesh=split,
        in_specs=placed,
        out_specs=P(("group", "far", "near"), None, "vox", None),
        check_vma=False,
    )
```

```python
import functools

import jax
import jax.numpy as jnp
import ml_dtypes
import numpy as np
from jax import lax
from jax.experimental import pallas as pl
from jax.experimental.pallas import tpu as pltpu
from jax.sharding import Mesh
from jax.sharding import PartitionSpec as P

SY = 16
SZ = 16
SITES = 4
REACH = 2
DPAD = 24
LANES = 128
SUBJ_TILE = 16
HIGHEST = lax.Precision.HIGHEST
VMEM_MOST = 56 * 2**20
VMEM_BASE = 12 * 2**20
SQUARE_ROW = 20
CHUNKS = 2
SCALE_LANE = DPAD
STRIDE = 32


def kernel_table(length):
    position = np.arange(length)
    offset = (position[:, None] - position[None, :]).astype(np.float32)
    weights = np.where(np.abs(offset) <= REACH, np.exp(-offset * offset / np.float32(2.0)), np.float32(0.0))
    total = sum(np.exp(-(k * k) / 2.0) for k in range(-REACH, REACH + 1))
    return (weights / np.float32(total)).astype(np.float32)


def plane_kernel(plane):
    row, depth = kernel_table(SY), kernel_table(SZ)
    table = row[:, None, :, None] * depth[None, :, None, :]
    return table.reshape(plane, plane).astype(ml_dtypes.bfloat16)


def row_order(maps, planes):
    rows = SUBJ_TILE * maps * planes
    source = np.arange(rows).reshape(SUBJ_TILE, maps * planes).T.reshape(-1)
    return np.eye(rows, dtype=np.float32)[source].astype(ml_dtypes.bfloat16)


def tree_sum(terms):
    while len(terms) > 1:
        terms = [terms[i] + terms[i + 1] for i in range(0, len(terms), 2)]
    return terms[0]


RESIDENT = 3 * 2**20
IN_VMEM = pl.BlockSpec(memory_space=pltpu.VMEM)
IN_SMEM = pl.BlockSpec(memory_space=pltpu.SMEM)


def params(extra=0):
    return pltpu.CompilerParams(vmem_limit_bytes=min(VMEM_MOST, VMEM_BASE + extra))


def size_of(value):
    return int(np.prod(value.shape)) * jnp.dtype(value.dtype).itemsize


def small(shape, dtype):
    return int(np.prod(shape)) * jnp.dtype(dtype).itemsize <= RESIDENT


def keep(value):
    if small(value.shape, value.dtype):
        return pltpu.with_memory_space_constraint(value, pltpu.VMEM)
    return value


def result(shape, dtype):
    if small(shape, dtype):
        return pltpu.VMEM(shape, dtype)
    return jax.ShapeDtypeStruct(shape, dtype)


def call(kernel, name, outs, scalars, arrays, scratch=()):
    many = isinstance(outs, tuple)
    sizes = [size_of(value) for value in (*arrays, *(outs if many else (outs,)))]
    extra = 3 * sum(size for size in sizes if size > RESIDENT)
    return pl.pallas_call(
        kernel,
        out_shape=outs,
        in_specs=[IN_SMEM] * len(scalars) + [IN_VMEM] * len(arrays),
        out_specs=(IN_VMEM,) * len(outs) if many else IN_VMEM,
        scratch_shapes=list(scratch),
        compiler_params=params(extra),
        name=name,
    )(*scalars, *[keep(value) for value in arrays])


def tall_kernel(genotypes, codes, covariates, out, rows):
    snps = genotypes.shape[1]
    out[:snps, :] = jnp.transpose(genotypes[...])
    count = covariates.shape[0]
    site = lax.broadcasted_iota(jnp.int32, (SITES, codes.shape[1]), 0)
    rows[...] = jnp.zeros(rows.shape, jnp.float32)
    rows[:SITES, :] = (site == codes[...]).astype(jnp.float32)
    rows[SITES : SITES + count, :] = covariates[...].astype(jnp.float32)
    out[snps:, :] = rows[...].astype(jnp.bfloat16)


def tall_design(genotypes, covariates, site_codes):
    subjects, snps = genotypes.shape
    return pl.pallas_call(
        tall_kernel,
        out_shape=result((snps + DPAD, subjects), jnp.bfloat16),
        in_specs=[IN_VMEM] * 3,
        out_specs=IN_VMEM,
        scratch_shapes=[pltpu.VMEM((DPAD, subjects), jnp.float32)],
        compiler_params=params(),
        name="tall_design",
    )(genotypes, site_codes[None, :], covariates.T)


def smooth_kernel(group, planes, per_vox, parts, width, images, order, table, *outs):
    plane = table.shape[0]
    size = width // len(outs)
    groups = images.shape[1] // (group * planes)
    near = kernel_table(2 * REACH + 1)[REACH]
    for tile in range(images.shape[0] // SUBJ_TILE):
        here = pl.ds(tile * SUBJ_TILE, SUBJ_TILE)
        for part in range(groups):
            rows = images[here, part * group * planes : (part + 1) * group * planes, :]
            rows = rows.reshape(SUBJ_TILE * group * planes, plane)
            rows = jnp.dot(order[...], rows, preferred_element_type=jnp.float32)
            inplane = jnp.dot(
                rows.astype(jnp.bfloat16), table[...], preferred_element_type=jnp.float32
            )
            for m in range(group):
                slabs = [
                    inplane[(m * planes + x) * SUBJ_TILE : (m * planes + x + 1) * SUBJ_TILE]
                    for x in range(planes)
                ]
                for x in range(planes):
                    total = slabs[x] * float(near[REACH])
                    for lag in range(1, REACH + 1):
                        sides = [slabs[k] for k in (x - lag, x + lag) if 0 <= k < planes]
                        if sides:
                            total = total + functools.reduce(jnp.add, sides) * float(
                                near[REACH + lag]
                            )
                    column = ((part * group + m) * per_vox + x % per_vox) * plane
                    target = (x // per_vox) * parts + column // width
                    chunk, first = column % width // size, column % size
                    out = outs[chunk]
                    out[target, here, first : first + plane] = total.astype(jnp.bfloat16)


def smooth(images, n_vox, parts, chunks):
    subjects, maps, planes, plane = images.shape
    per_vox = planes // n_vox
    width = maps * per_vox * plane // parts
    size = width // chunks
    assert size % plane == 0
    group = max(1, min(maps, 256 // (SUBJ_TILE * planes)))
    step = 32
    order = jnp.asarray(row_order(group, planes))
    table = jnp.asarray(plane_kernel(plane))
    return pl.pallas_call(
        functools.partial(smooth_kernel, group, planes, per_vox, parts, width),
        out_shape=[jax.ShapeDtypeStruct((n_vox * parts, subjects, size), jnp.bfloat16)] * chunks,
        grid=(subjects // step,),
        in_specs=[
            pl.BlockSpec((step, maps * planes, plane), lambda i: (i, 0, 0)),
            pl.BlockSpec(order.shape, lambda i: (0, 0)),
            pl.BlockSpec(table.shape, lambda i: (0, 0)),
        ],
        out_specs=[pl.BlockSpec((n_vox * parts, step, size), lambda i: (0, i, 0))] * chunks,
        compiler_params=params(VMEM_MOST),
        name="smooth",
    )(images.reshape(subjects, maps * planes, plane), order, table)


def moments_kernel(snps, slots, me, blocks, others, joined, out):
    rows = []
    half = len(slots) // 2
    for source in range(len(slots)):
        offset = jnp.bitwise_xor(me[0], source)
        index = 0
        for place, slot in enumerate(slots):
            index = index + jnp.where(offset == place, slot, 0)
        place = lax.rem(index, half)
        rows.append(jnp.where(index < half, blocks[place], others[place]))
    rows = jnp.concatenate(rows, axis=1)
    joined[...] = rows
    across = (((1,), (1,)), ((), ()))
    out[...] = jnp.zeros(out.shape, jnp.float32)
    out[:DPAD, : snps + DPAD] = lax.dot_general(
        rows[snps:], rows, across, preferred_element_type=jnp.float32
    )
    wide = rows[:snps].astype(jnp.float32)
    wide = wide * wide
    high = wide.astype(jnp.bfloat16)
    low = (wide - high.astype(jnp.float32)).astype(jnp.bfloat16)
    ones = jnp.ones((8, rows.shape[1]), jnp.bfloat16)
    squares = lax.dot_general(ones, high, across, preferred_element_type=jnp.float32)
    squares = squares + lax.dot_general(ones, low, across, preferred_element_type=jnp.float32)
    out[DPAD:, :snps] = squares


def moments(blocks, others, slots, me):
    count, rows, subjects = blocks.shape
    snps = rows - DPAD
    spread = -(-rows // LANES) * LANES
    outs = (
        result((rows, 2 * count * subjects), blocks.dtype),
        result((DPAD + 8, spread), jnp.float32),
    )
    kernel = functools.partial(moments_kernel, snps, slots)
    return call(kernel, "moments", outs, [me], [blocks, others])


def eliminate(total, snps, design, guard):
    lane = lax.broadcasted_iota(jnp.int32, (DPAD, LANES), 1)
    row = lax.broadcasted_iota(jnp.int32, (DPAD, LANES), 0)
    shift = 32
    gram = total[:DPAD, snps : snps + LANES]
    work = jnp.where((row >= design) & (lane == row), 1.0, gram)
    work = jnp.where(lane == row + shift, 1.0, work)
    for k in range(design):
        pivot = work[k : k + 1, k : k + 1]
        line = work[k : k + 1, :] / pivot
        if guard:
            line = jnp.where(pivot > gram[k : k + 1, k : k + 1] * 2.0**-14, line, 0.0)
        work = jnp.where(row == k, line, work - work[:, k : k + 1] * line)
    solved = pltpu.roll(work, LANES - shift, 1)
    return jnp.where((lane < design) & (row < design), solved, 0.0)


def gene_fit(total, snps, design, guard):
    solved = eliminate(total, snps, design, guard)
    cross_gene = total[:DPAD, :snps]
    fitted = jnp.dot(
        solved[:, :DPAD], cross_gene, precision=HIGHEST, preferred_element_type=jnp.float32
    )
    square = total[DPAD : DPAD + 1, :snps]
    rss = square - jnp.sum(cross_gene * fitted, axis=0, keepdims=True)
    if guard:
        rss = jnp.maximum(rss, square * 2.0**-10) + 1e-30
    return solved, fitted, lax.rsqrt(rss)


def pair_kernel(snps, design, moment, coef, lines):
    _, fitted, scale = gene_fit(moment[...], snps, design, True)
    lines[...] = jnp.zeros(lines.shape, jnp.float32)
    lines[:DPAD, :] = fitted * scale
    lines[SCALE_LANE : SCALE_LANE + 1, :] = scale
    coef[...] = jnp.transpose(lines[...])


def pair_fit(moment, snps, design):
    kernel = functools.partial(pair_kernel, snps, design)
    scratch = [pltpu.VMEM((LANES, snps), jnp.float32)]
    return call(kernel, "pair_fit", result((snps, LANES), jnp.float32), [], [moment], scratch)


def cohort_kernel(snps, design, *refs):
    parts, (coef, inverse, lines) = refs[:-3], refs[-3:]
    moment = [part[...] for part in parts]
    solved, fitted, scale = gene_fit(tree_sum(moment), snps, design, False)
    inverse[...] = solved
    lines[...] = jnp.zeros(lines.shape, jnp.float32)
    lines[:DPAD, :] = fitted * -scale
    lines[SCALE_LANE : SCALE_LANE + 1, :] = scale
    for j in range(1, len(parts)):
        _, fit, own_scale = gene_fit(moment[j], snps, design, True)
        lines[j * STRIDE : j * STRIDE + DPAD, :] = fit * scale
        lines[SCALE_LANE + j : SCALE_LANE + j + 1, :] = scale / own_scale
    coef[...] = jnp.transpose(lines[...])


def cohort_fit(parts, snps, design):
    kernel = functools.partial(cohort_kernel, snps, design)
    outs = (result((snps, LANES), jnp.float32), result((DPAD, LANES), jnp.float32))
    scratch = [pltpu.VMEM((LANES, snps), jnp.float32)]
    return call(kernel, "cohort_fit", outs, [], parts, scratch)


def column_norm(sums, here):
    square = sums[SQUARE_ROW : SQUARE_ROW + 1, :]
    mean = jnp.sum(sums[:SITES, :], axis=0, keepdims=True) * (1.0 / here)
    spread = jnp.maximum(square - mean * mean * here, square * 2.0**-10)
    return jnp.sqrt(spread + 1e-30)


def products_kernel(here, me, genes, columns, coef, own, *refs):
    far, stats, held = refs[:-2], refs[-2], refs[-1]
    values = columns[...]
    wide = values.astype(jnp.float32)
    sums = jnp.dot(genes[...], values, preferred_element_type=jnp.float32)
    snps = held.shape[0]
    held[...] = sums[:snps, :]
    square = jnp.sum(wide * wide, axis=0, keepdims=True)
    cross_image = sums[snps:, :]
    row = lax.broadcasted_iota(jnp.int32, cross_image.shape, 0)
    cross_image = jnp.where(row == SQUARE_ROW, square, cross_image)
    stats[...] = cross_image
    over = 1.0 / column_norm(cross_image, here)
    size = own.shape[0]
    own[...] = held[pl.ds(pl.multiple_of(me[0] * size, size), size), :]
    for j, out in enumerate(far):
        place = pl.multiple_of(jnp.bitwise_xor(me[0], j + 1) * size, size)
        line = coef[pl.ds(place, size), :]
        fit = jnp.dot(
            line[:, :DPAD], cross_image, precision=HIGHEST, preferred_element_type=jnp.float32
        )
        scale = line[:, SCALE_LANE : SCALE_LANE + 1]
        out[...] = (scale * held[pl.ds(place, size), :] - fit) * over


def products(genes, columns, coef, me, count):
    rows, here = genes.shape
    snps = rows - DPAD
    width = columns.shape[1]
    outs = (result((snps // count, width), jnp.float32),) * count
    outs += (result((DPAD, width), jnp.float32),)
    kernel = functools.partial(products_kernel, float(here))
    scratch = [pltpu.VMEM((snps, width), jnp.float32)]
    return call(kernel, "products", outs, [me], [genes, columns, coef], scratch)


def base_kernel(here, me, own, coef, inverse, *refs):
    parts, (base, factors, stack) = refs[:-3], refs[-3:]
    stats = [part[...] for part in parts]
    row = lax.broadcasted_iota(jnp.int32, stats[0].shape, 0)
    total = tree_sum(stats)
    cross_image = jnp.where(row < SQUARE_ROW, total, 0.0)
    solved = jnp.dot(
        inverse[:, :DPAD], cross_image, precision=HIGHEST, preferred_element_type=jnp.float32
    )
    rss = total[SQUARE_ROW : SQUARE_ROW + 1, :] - jnp.sum(
        cross_image * solved, axis=0, keepdims=True
    )
    scale = lax.rsqrt(rss)
    stack[...] = jnp.zeros(stack.shape, jnp.float32)
    stack[:DPAD, :] = cross_image
    factors[...] = jnp.zeros(factors.shape, jnp.float32)
    for j in range(1, len(parts)):
        stack[j * STRIDE : j * STRIDE + DPAD, :] = jnp.where(row < SQUARE_ROW, stats[j], 0.0)
        factors[j : j + 1, :] = column_norm(stats[j], here) * scale
    size = own.shape[0]
    line = coef[pl.ds(pl.multiple_of(me[0] * size, size), size), :]
    terms = jnp.dot(line, stack[...], precision=HIGHEST, preferred_element_type=jnp.float32)
    base[...] = (line[:, SCALE_LANE : SCALE_LANE + 1] * own[...] + terms) * scale


def base_ratio(me, own, coef, inverse, parts, here):
    size, width = own.shape
    outs = (result((size, width), jnp.float32), result((8, width), jnp.float32))
    kernel = functools.partial(base_kernel, float(here))
    scratch = [pltpu.VMEM((LANES, width), jnp.float32)]
    return call(kernel, "base_ratio", outs, [me], [own, coef, inverse, *parts], scratch)


def permute_xor(value, axes, bits):
    size = lax.axis_size(axes)
    return lax.ppermute(value, axes, [(i, i ^ bits) for i in range(size)])


def on_device(images, genotypes, covariates, site_codes):
    subjects, maps, planes, plane = images.shape
    n_vox, n_far, n_near = (lax.axis_size(name) for name in ("vox", "far", "near"))
    vox, far, near = (lax.axis_index(name) for name in ("vox", "far", "near"))
    snps = genotypes.shape[1]
    design = SITES + covariates.shape[1]
    per_vox = planes // n_vox
    count = n_vox * n_near
    here = count * subjects

    tall = tall_design(genotypes, covariates, site_codes)
    other = n_near
    offsets = [o for o in range(count) if not o & other]
    blocks = [tall] + [permute_xor(tall, ("vox", "near"), o) for o in offsets[1:]]
    smoothed = smooth(images, n_vox, n_near, CHUNKS)
    smoothed, *blocks = lax.optimization_barrier((smoothed, *blocks))

    def exchange(value):
        value = lax.all_to_all(value, ("vox", "near"), 0, 0, tiled=True)
        return value.reshape(here, value.shape[2])

    columns = [exchange(smoothed[0])]
    blocks = jnp.stack(blocks)
    others = permute_xor(blocks, ("vox", "near"), other)
    order = offsets + [o | other for o in offsets]
    slots = tuple(order.index(o) for o in range(count))
    genes, moment = moments(blocks, others, slots, (vox * n_near + near)[None])
    pair_coef = pair_fit(moment, snps, design)
    moment_parts = [moment] + [permute_xor(moment, "far", j) for j in range(1, n_far)]
    for chunk in range(1, CHUNKS):
        value, columns[-1], pair_coef, moment_parts = lax.optimization_barrier(
            (smoothed[chunk], columns[-1], pair_coef, moment_parts)
        )
        columns.append(exchange(value))
    coef, inverse = cohort_fit(moment_parts, snps, design)
    columns[-1], coef, inverse = lax.optimization_barrier((columns[-1], coef, inverse))

    size = snps // n_far
    panel = size // n_near
    freedom = float(here * n_far - design - 1)

    def send(pieces):
        return [permute_xor(pieces[j - 1], "far", j) for j in range(1, n_far)]

    def panel_stats(index, base, factors, pieces):
        first = index * panel
        line = lax.dynamic_slice_in_dim(coef, far * size + first, panel, 0)
        ratio = lax.dynamic_slice_in_dim(base, first, panel, 0)
        for j in range(1, n_far):
            piece = lax.dynamic_slice_in_dim(pieces[j - 1], first, panel, 0)
            weight = line[:, SCALE_LANE + j, None] * factors[None, j]
            ratio = ratio + piece.astype(jnp.float32) * weight
        return ratio * jnp.sqrt(freedom / (1.0 - ratio * ratio))

    owns, received, sums = [], [], []
    for chunk in range(CHUNKS):
        own, *pieces, stats = products(genes, columns[chunk], pair_coef, far[None], n_far)
        pieces = [piece.astype(jnp.float16) for piece in pieces]
        owns.append(own)
        sums.append([stats] + [permute_xor(stats, "far", j) for j in range(1, n_far)])
        if chunk == CHUNKS - 1:
            sums, pieces = lax.optimization_barrier((sums, pieces))
        received.append(send(pieces))
    outs = []
    gate = None
    for chunk in range(CHUNKS):
        base, factors = base_ratio(far[None], owns[chunk], coef, inverse, sums[chunk], here)
        if gate is not None:
            base, gate = lax.optimization_barrier((base, gate))
            outs[-1][0] = gate
        pieces = received[chunk]
        gate = panel_stats(jnp.bitwise_xor(near, 1), base, factors, pieces)
        outs.append([gate, panel_stats(near, base, factors, pieces)])
    outs = [(permute_xor(away, "near", 1), home) for away, home in outs]
    outs = [
        jnp.where(near == 0, jnp.stack([home, away], 1), jnp.stack([away, home], 1))
        for away, home in outs
    ]
    return jnp.stack(outs, axis=2).reshape(panel, maps, per_vox, plane)


def solution(mesh):
    sizes = dict(mesh.shape)
    devices = mesh.devices.reshape(sizes["group"], sizes["vox"], sizes["snp"] // 2, 2)
    split = Mesh(devices, ("group", "vox", "far", "near"))
    owner = ("group", "vox", "far", "near")
    placed = (P(owner, None, None, None), P(owner, None), P(owner, None), P(owner))
    return jax.shard_map(
        on_device,
        mesh=split,
        in_specs=placed,
        out_specs=P(("group", "far", "near"), None, "vox", None),
        check_vma=False,
    )
```

```python
import functools

import jax
import jax.numpy as jnp
import ml_dtypes
import numpy as np
from jax import lax
from jax.experimental import pallas as pl
from jax.experimental.pallas import tpu as pltpu
from jax.sharding import Mesh
from jax.sharding import PartitionSpec as P

SY = 16
SZ = 16
SITES = 4
REACH = 2
DPAD = 24
LANES = 128
SUBJ_TILE = 16
HIGHEST = lax.Precision.HIGHEST
VMEM_MOST = 56 * 2**20
VMEM_BASE = 12 * 2**20
SQUARE_ROW = 20
CHUNKS = 2
NARROW = 2.0**-4
SCALE_LANE = DPAD
STRIDE = 32


def kernel_table(length):
    position = np.arange(length)
    offset = (position[:, None] - position[None, :]).astype(np.float32)
    weights = np.where(np.abs(offset) <= REACH, np.exp(-offset * offset / np.float32(2.0)), np.float32(0.0))
    total = sum(np.exp(-(k * k) / 2.0) for k in range(-REACH, REACH + 1))
    return (weights / np.float32(total)).astype(np.float32)


def plane_kernel(plane):
    row, depth = kernel_table(SY), kernel_table(SZ)
    table = row[:, None, :, None] * depth[None, :, None, :]
    return table.reshape(plane, plane).astype(ml_dtypes.bfloat16)


def row_order(maps, planes):
    rows = SUBJ_TILE * maps * planes
    source = np.arange(rows).reshape(SUBJ_TILE, maps * planes).T.reshape(-1)
    return np.eye(rows, dtype=np.float32)[source].astype(ml_dtypes.bfloat16)


def tree_sum(terms):
    while len(terms) > 1:
        terms = [terms[i] + terms[i + 1] for i in range(0, len(terms), 2)]
    return terms[0]


RESIDENT = 3 * 2**20
IN_VMEM = pl.BlockSpec(memory_space=pltpu.VMEM)
IN_SMEM = pl.BlockSpec(memory_space=pltpu.SMEM)


def params(extra=0):
    return pltpu.CompilerParams(vmem_limit_bytes=min(VMEM_MOST, VMEM_BASE + extra))


def size_of(value):
    return int(np.prod(value.shape)) * jnp.dtype(value.dtype).itemsize


def small(shape, dtype):
    return int(np.prod(shape)) * jnp.dtype(dtype).itemsize <= RESIDENT


def keep(value):
    if small(value.shape, value.dtype):
        return pltpu.with_memory_space_constraint(value, pltpu.VMEM)
    return value


def result(shape, dtype):
    if small(shape, dtype):
        return pltpu.VMEM(shape, dtype)
    return jax.ShapeDtypeStruct(shape, dtype)


def call(kernel, name, outs, scalars, arrays, scratch=(), moved=0):
    many = isinstance(outs, tuple)
    sizes = [size_of(value) for value in (*arrays, *(outs if many else (outs,)))]
    extra = 3 * sum(size for size in sizes if size > RESIDENT)
    return pl.pallas_call(
        kernel,
        out_shape=outs,
        in_specs=[IN_SMEM] * len(scalars) + [IN_VMEM] * len(arrays),
        out_specs=(IN_VMEM,) * len(outs) if many else IN_VMEM,
        scratch_shapes=list(scratch),
        compiler_params=params(extra),
        name=name,
    )(*scalars, *arrays[:moved], *[keep(value) for value in arrays[moved:]])


def tall_kernel(genotypes, codes, covariates, out, rows):
    snps = genotypes.shape[1]
    out[:snps, :] = jnp.transpose(genotypes[...])
    count = covariates.shape[0]
    site = lax.broadcasted_iota(jnp.int32, (SITES, codes.shape[1]), 0)
    rows[...] = jnp.zeros(rows.shape, jnp.float32)
    rows[:SITES, :] = (site == codes[...]).astype(jnp.float32)
    rows[SITES : SITES + count, :] = covariates[...].astype(jnp.float32)
    out[snps:, :] = rows[...].astype(jnp.bfloat16)


def tall_design(genotypes, covariates, site_codes):
    subjects, snps = genotypes.shape
    return pl.pallas_call(
        tall_kernel,
        out_shape=result((snps + DPAD, subjects), jnp.bfloat16),
        in_specs=[IN_VMEM] * 3,
        out_specs=IN_VMEM,
        scratch_shapes=[pltpu.VMEM((DPAD, subjects), jnp.float32)],
        compiler_params=params(),
        name="tall_design",
    )(genotypes, site_codes[None, :], covariates.T)


def smooth_kernel(group, planes, per_vox, parts, width, images, order, table, *outs):
    plane = table.shape[0]
    size = width // len(outs)
    groups = images.shape[1] // (group * planes)
    near = kernel_table(2 * REACH + 1)[REACH]
    for tile in range(images.shape[0] // SUBJ_TILE):
        here = pl.ds(tile * SUBJ_TILE, SUBJ_TILE)
        for part in range(groups):
            rows = images[here, part * group * planes : (part + 1) * group * planes, :]
            rows = rows.reshape(SUBJ_TILE * group * planes, plane)
            rows = jnp.dot(order[...], rows, preferred_element_type=jnp.float32)
            inplane = jnp.dot(
                rows.astype(jnp.bfloat16), table[...], preferred_element_type=jnp.float32
            )
            for m in range(group):
                slabs = [
                    inplane[(m * planes + x) * SUBJ_TILE : (m * planes + x + 1) * SUBJ_TILE]
                    for x in range(planes)
                ]
                for x in range(planes):
                    total = slabs[x] * float(near[REACH])
                    for lag in range(1, REACH + 1):
                        sides = [slabs[k] for k in (x - lag, x + lag) if 0 <= k < planes]
                        if sides:
                            total = total + functools.reduce(jnp.add, sides) * float(
                                near[REACH + lag]
                            )
                    column = ((part * group + m) * per_vox + x % per_vox) * plane
                    target = (x // per_vox) * parts + column // width
                    chunk, first = column % width // size, column % size
                    out = outs[chunk]
                    out[target, here, first : first + plane] = total.astype(jnp.bfloat16)


def smooth(images, n_vox, parts, chunks):
    subjects, maps, planes, plane = images.shape
    per_vox = planes // n_vox
    width = maps * per_vox * plane // parts
    size = width // chunks
    assert size % plane == 0
    group = max(1, min(maps, 256 // (SUBJ_TILE * planes)))
    step = 32
    order = jnp.asarray(row_order(group, planes))
    table = jnp.asarray(plane_kernel(plane))
    return pl.pallas_call(
        functools.partial(smooth_kernel, group, planes, per_vox, parts, width),
        out_shape=[jax.ShapeDtypeStruct((n_vox * parts, subjects, size), jnp.bfloat16)] * chunks,
        grid=(subjects // step,),
        in_specs=[
            pl.BlockSpec((step, maps * planes, plane), lambda i: (i, 0, 0)),
            pl.BlockSpec(order.shape, lambda i: (0, 0)),
            pl.BlockSpec(table.shape, lambda i: (0, 0)),
        ],
        out_specs=[pl.BlockSpec((n_vox * parts, step, size), lambda i: (0, i, 0))] * chunks,
        compiler_params=params(VMEM_MOST),
        name="smooth",
    )(images.reshape(subjects, maps * planes, plane), order, table)


def moments_kernel(snps, slots, me, blocks, others, joined, out):
    rows = []
    half = len(slots) // 2
    for source in range(len(slots)):
        offset = jnp.bitwise_xor(me[0], source)
        index = 0
        for place, slot in enumerate(slots):
            index = index + jnp.where(offset == place, slot, 0)
        place = lax.rem(index, half)
        rows.append(jnp.where(index < half, blocks[place], others[place]))
    rows = jnp.concatenate(rows, axis=1)
    joined[...] = rows
    across = (((1,), (1,)), ((), ()))
    out[...] = jnp.zeros(out.shape, jnp.float32)
    out[:DPAD, : snps + DPAD] = lax.dot_general(
        rows[snps:], rows, across, preferred_element_type=jnp.float32
    )
    wide = rows[:snps].astype(jnp.float32)
    wide = wide * wide
    high = wide.astype(jnp.bfloat16)
    low = (wide - high.astype(jnp.float32)).astype(jnp.bfloat16)
    ones = jnp.ones((8, rows.shape[1]), jnp.bfloat16)
    squares = lax.dot_general(ones, high, across, preferred_element_type=jnp.float32)
    squares = squares + lax.dot_general(ones, low, across, preferred_element_type=jnp.float32)
    out[DPAD:, :snps] = squares


def moments(blocks, others, slots, me):
    count, rows, subjects = blocks.shape
    snps = rows - DPAD
    spread = -(-rows // LANES) * LANES
    outs = (
        result((rows, 2 * count * subjects), blocks.dtype),
        result((DPAD + 8, spread), jnp.float32),
    )
    kernel = functools.partial(moments_kernel, snps, slots)
    return call(kernel, "moments", outs, [me], [blocks, others])


def eliminate(total, snps, design, guard):
    lane = lax.broadcasted_iota(jnp.int32, (DPAD, LANES), 1)
    row = lax.broadcasted_iota(jnp.int32, (DPAD, LANES), 0)
    shift = 32
    gram = total[:DPAD, snps : snps + LANES]
    work = jnp.where((row >= design) & (lane == row), 1.0, gram)
    work = jnp.where(lane == row + shift, 1.0, work)
    for k in range(design):
        pivot = work[k : k + 1, k : k + 1]
        line = work[k : k + 1, :] / pivot
        if guard:
            line = jnp.where(pivot > gram[k : k + 1, k : k + 1] * 2.0**-14, line, 0.0)
        work = jnp.where(row == k, line, work - work[:, k : k + 1] * line)
    solved = pltpu.roll(work, LANES - shift, 1)
    return jnp.where((lane < design) & (row < design), solved, 0.0)


def gene_fit(total, snps, design, guard):
    solved = eliminate(total, snps, design, guard)
    cross_gene = total[:DPAD, :snps]
    fitted = jnp.dot(
        solved[:, :DPAD], cross_gene, precision=HIGHEST, preferred_element_type=jnp.float32
    )
    square = total[DPAD : DPAD + 1, :snps]
    rss = square - jnp.sum(cross_gene * fitted, axis=0, keepdims=True)
    if guard:
        rss = jnp.maximum(rss, square * 2.0**-10) + 1e-30
    return solved, fitted, lax.rsqrt(rss)


def pair_kernel(snps, design, moment, coef, lines):
    _, fitted, scale = gene_fit(moment[...], snps, design, True)
    lines[...] = jnp.zeros(lines.shape, jnp.float32)
    lines[:DPAD, :] = fitted * scale
    lines[SCALE_LANE : SCALE_LANE + 1, :] = scale
    coef[...] = jnp.transpose(lines[...])


def pair_fit(moment, snps, design):
    kernel = functools.partial(pair_kernel, snps, design)
    scratch = [pltpu.VMEM((LANES, snps), jnp.float32)]
    return call(kernel, "pair_fit", result((snps, LANES), jnp.float32), [], [moment], scratch)


def cohort_kernel(snps, design, *refs):
    parts, (coef, inverse, lines) = refs[:-3], refs[-3:]
    moment = [part[...] for part in parts]
    solved, fitted, scale = gene_fit(tree_sum(moment), snps, design, False)
    inverse[...] = solved
    lines[...] = jnp.zeros(lines.shape, jnp.float32)
    lines[:DPAD, :] = fitted * -scale
    lines[SCALE_LANE : SCALE_LANE + 1, :] = scale
    for j in range(1, len(parts)):
        _, fit, own_scale = gene_fit(moment[j], snps, design, True)
        lines[j * STRIDE : j * STRIDE + DPAD, :] = fit * scale
        lines[SCALE_LANE + j : SCALE_LANE + j + 1, :] = scale / own_scale
    coef[...] = jnp.transpose(lines[...])


def cohort_fit(parts, snps, design):
    kernel = functools.partial(cohort_kernel, snps, design)
    outs = (result((snps, LANES), jnp.float32), result((DPAD, LANES), jnp.float32))
    scratch = [pltpu.VMEM((LANES, snps), jnp.float32)]
    return call(kernel, "cohort_fit", outs, [], parts, scratch)


def column_norm(sums, here):
    square = sums[SQUARE_ROW : SQUARE_ROW + 1, :]
    mean = jnp.sum(sums[:SITES, :], axis=0, keepdims=True) * (1.0 / here)
    spread = jnp.maximum(square - mean * mean * here, square * 2.0**-10)
    return jnp.sqrt(spread + 1e-30)


def products_kernel(here, me, genes, columns, coef, own, *refs):
    far, stats, held = refs[:-2], refs[-2], refs[-1]
    values = columns[...]
    wide = values.astype(jnp.float32)
    sums = jnp.dot(genes[...], values, preferred_element_type=jnp.float32)
    snps = held.shape[0]
    held[...] = sums[:snps, :]
    square = jnp.sum(wide * wide, axis=0, keepdims=True)
    cross_image = sums[snps:, :]
    row = lax.broadcasted_iota(jnp.int32, cross_image.shape, 0)
    cross_image = jnp.where(row == SQUARE_ROW, square, cross_image)
    stats[...] = cross_image
    over = 1.0 / column_norm(cross_image, here)
    size = own.shape[0]
    own[...] = held[pl.ds(pl.multiple_of(me[0] * size, size), size), :]
    for j, out in enumerate(far):
        place = pl.multiple_of(jnp.bitwise_xor(me[0], j + 1) * size, size)
        line = coef[pl.ds(place, size), :]
        fit = jnp.dot(
            line[:, :DPAD], cross_image, precision=HIGHEST, preferred_element_type=jnp.float32
        )
        scale = line[:, SCALE_LANE : SCALE_LANE + 1]
        out[...] = (scale * held[pl.ds(place, size), :] - fit) * over


def products(genes, columns, coef, me, count):
    rows, here = genes.shape
    snps = rows - DPAD
    width = columns.shape[1]
    size = snps // count
    outs = (jax.ShapeDtypeStruct((size, width), jnp.float32),)
    outs += (result((size, width), jnp.float32),) * (count - 1)
    outs += (result((DPAD, width), jnp.float32),)
    kernel = functools.partial(products_kernel, float(here))
    scratch = [pltpu.VMEM((snps, width), jnp.float32)]
    return call(kernel, "products", outs, [me], [genes, columns, coef], scratch)


def base_kernel(here, me, own, coef, inverse, *refs):
    parts, (base, factors, stack) = refs[:-3], refs[-3:]
    stats = [part[...] for part in parts]
    row = lax.broadcasted_iota(jnp.int32, stats[0].shape, 0)
    total = tree_sum(stats)
    cross_image = jnp.where(row < SQUARE_ROW, total, 0.0)
    solved = jnp.dot(
        inverse[:, :DPAD], cross_image, precision=HIGHEST, preferred_element_type=jnp.float32
    )
    rss = total[SQUARE_ROW : SQUARE_ROW + 1, :] - jnp.sum(
        cross_image * solved, axis=0, keepdims=True
    )
    scale = lax.rsqrt(rss)
    stack[...] = jnp.zeros(stack.shape, jnp.float32)
    stack[:DPAD, :] = cross_image
    factors[...] = jnp.zeros(factors.shape, jnp.float32)
    for j in range(1, len(parts)):
        stack[j * STRIDE : j * STRIDE + DPAD, :] = jnp.where(row < SQUARE_ROW, stats[j], 0.0)
        factors[j : j + 1, :] = column_norm(stats[j], here) * scale
    size = own.shape[0]
    line = coef[pl.ds(pl.multiple_of(me[0] * size, size), size), :]
    terms = jnp.dot(line, stack[...], precision=HIGHEST, preferred_element_type=jnp.float32)
    base[...] = (line[:, SCALE_LANE : SCALE_LANE + 1] * own[...] + terms) * scale


def base_ratio(me, own, coef, inverse, parts, here):
    size, width = own.shape
    outs = (result((size, width), jnp.float32), result((8, width), jnp.float32))
    kernel = functools.partial(base_kernel, float(here))
    scratch = [pltpu.VMEM((LANES, width), jnp.float32)]
    return call(kernel, "base_ratio", outs, [me], [own, coef, inverse, *parts], scratch, 1)


def permute_xor(value, axes, bits):
    size = lax.axis_size(axes)
    return lax.ppermute(value, axes, [(i, i ^ bits) for i in range(size)])


def on_device(images, genotypes, covariates, site_codes):
    subjects, maps, planes, plane = images.shape
    n_vox, n_far, n_near = (lax.axis_size(name) for name in ("vox", "far", "near"))
    vox, far, near = (lax.axis_index(name) for name in ("vox", "far", "near"))
    snps = genotypes.shape[1]
    design = SITES + covariates.shape[1]
    per_vox = planes // n_vox
    count = n_vox * n_near
    here = count * subjects

    def exchange(value):
        value = lax.all_to_all(value, ("vox", "near"), 0, 0, tiled=True)
        return value.reshape(here, value.shape[2])

    smoothed = smooth(images, n_vox, n_near, CHUNKS)
    smoothed, genotypes = lax.optimization_barrier((smoothed, genotypes))
    columns = [exchange(smoothed[0])]
    tall = tall_design(genotypes, covariates, site_codes)
    other = n_near
    offsets = [o for o in range(count) if not o & other]
    blocks = [tall] + [permute_xor(tall, ("vox", "near"), o) for o in offsets[1:]]
    for chunk in range(1, CHUNKS):
        value, columns[-1], *blocks = lax.optimization_barrier(
            (smoothed[chunk], columns[-1], *blocks)
        )
        columns.append(exchange(value))
    blocks = jnp.stack(blocks)
    others = permute_xor(blocks, ("vox", "near"), other)
    order = offsets + [o | other for o in offsets]
    slots = tuple(order.index(o) for o in range(count))
    genes, moment = moments(blocks, others, slots, (vox * n_near + near)[None])
    pair_coef = pair_fit(moment, snps, design)
    moment_parts = [moment] + [permute_xor(moment, "far", j) for j in range(1, n_far)]
    size = snps // n_far
    panel = size // n_near
    freedom = float(here * n_far - design - 1)

    def send(pieces):
        return [permute_xor(pieces[j - 1], "far", j) for j in range(1, n_far)]

    def panel_stats(index, coef, base, factors, pieces):
        first = index * panel
        line = lax.dynamic_slice_in_dim(coef, far * size + first, panel, 0)
        ratio = lax.dynamic_slice_in_dim(base, first, panel, 0)
        for j in range(1, n_far):
            piece = lax.dynamic_slice_in_dim(pieces[j - 1], first, panel, 0)
            weight = line[:, SCALE_LANE + j, None] * factors[None, j]
            ratio = ratio + piece.astype(jnp.float32) * weight
        return ratio * jnp.sqrt(freedom / (1.0 - ratio * ratio))

    owns, received, sums = [], [], []
    for chunk in range(CHUNKS):
        own, *pieces, stats = products(genes, columns[chunk], pair_coef, far[None], n_far)
        pieces = [piece.astype(jnp.float16) for piece in pieces]
        owns.append(own)
        sums.append([stats] + [permute_xor(stats, "far", j) for j in range(1, n_far)])
        received.append(send(pieces))
    moment_parts, sums[-1][0] = lax.optimization_barrier((moment_parts, sums[-1][0]))
    coef, inverse = cohort_fit(moment_parts, snps, design)
    outs = []
    gate = None
    for chunk in range(CHUNKS):
        base, factors = base_ratio(far[None], owns[chunk], coef, inverse, sums[chunk], here)
        if gate is not None:
            base, gate = lax.optimization_barrier((base, gate))
            outs[-1][0] = gate
        pieces = received[chunk]
        gate = panel_stats(jnp.bitwise_xor(near, 1), coef, base, factors, pieces)
        outs.append([gate, panel_stats(near, coef, base, factors, pieces)])
    outs = [
        (permute_xor((away * NARROW).astype(jnp.float16), "near", 1), home) for away, home in outs
    ]
    outs = [(away.astype(jnp.float32) * (1.0 / NARROW), home) for away, home in outs]
    outs = [
        jnp.where(near == 0, jnp.stack([home, away], 1), jnp.stack([away, home], 1))
        for away, home in outs
    ]
    return jnp.stack(outs, axis=2).reshape(panel, maps, per_vox, plane)


def solution(mesh):
    sizes = dict(mesh.shape)
    devices = mesh.devices.reshape(sizes["group"], sizes["vox"], sizes["snp"] // 2, 2)
    split = Mesh(devices, ("group", "vox", "far", "near"))
    owner = ("group", "vox", "far", "near")
    placed = (P(owner, None, None, None), P(owner, None), P(owner, None), P(owner))
    return jax.shard_map(
        on_device,
        mesh=split,
        in_specs=placed,
        out_specs=P(("group", "far", "near"), None, "vox", None),
        check_vma=False,
    )
```

```python
import functools

import jax
import jax.numpy as jnp
import ml_dtypes
import numpy as np
from jax import lax
from jax.experimental import pallas as pl
from jax.experimental.pallas import tpu as pltpu
from jax.sharding import Mesh
from jax.sharding import PartitionSpec as P

SY = 16
SZ = 16
SITES = 4
REACH = 2
DPAD = 24
LANES = 128
SUBJ_TILE = 16
HIGHEST = lax.Precision.HIGHEST
VMEM_MOST = 56 * 2**20
VMEM_BASE = 12 * 2**20
SQUARE_ROW = 20
CHUNKS = 2
NARROW = 2.0**-4
SCALE_LANE = DPAD
STRIDE = 32


def kernel_table(length):
    position = np.arange(length)
    offset = (position[:, None] - position[None, :]).astype(np.float32)
    weights = np.where(np.abs(offset) <= REACH, np.exp(-offset * offset / np.float32(2.0)), np.float32(0.0))
    total = sum(np.exp(-(k * k) / 2.0) for k in range(-REACH, REACH + 1))
    return (weights / np.float32(total)).astype(np.float32)


def plane_kernel(plane):
    row, depth = kernel_table(SY), kernel_table(SZ)
    table = row[:, None, :, None] * depth[None, :, None, :]
    return table.reshape(plane, plane).astype(ml_dtypes.bfloat16)


def row_order(maps, planes):
    rows = SUBJ_TILE * maps * planes
    source = np.arange(rows).reshape(SUBJ_TILE, maps * planes).T.reshape(-1)
    return np.eye(rows, dtype=np.float32)[source].astype(ml_dtypes.bfloat16)


def tree_sum(terms):
    while len(terms) > 1:
        terms = [terms[i] + terms[i + 1] for i in range(0, len(terms), 2)]
    return terms[0]


RESIDENT = 3 * 2**20
IN_VMEM = pl.BlockSpec(memory_space=pltpu.VMEM)
IN_SMEM = pl.BlockSpec(memory_space=pltpu.SMEM)


def params(extra=0):
    return pltpu.CompilerParams(vmem_limit_bytes=min(VMEM_MOST, VMEM_BASE + extra))


def size_of(value):
    return int(np.prod(value.shape)) * jnp.dtype(value.dtype).itemsize


def small(shape, dtype):
    return int(np.prod(shape)) * jnp.dtype(dtype).itemsize <= RESIDENT


def keep(value):
    if small(value.shape, value.dtype):
        return pltpu.with_memory_space_constraint(value, pltpu.VMEM)
    return value


def result(shape, dtype):
    if small(shape, dtype):
        return pltpu.VMEM(shape, dtype)
    return jax.ShapeDtypeStruct(shape, dtype)


def call(kernel, name, outs, scalars, arrays, scratch=(), moved=0):
    many = isinstance(outs, tuple)
    sizes = [size_of(value) for value in (*arrays, *(outs if many else (outs,)))]
    extra = 3 * sum(size for size in sizes if size > RESIDENT)
    return pl.pallas_call(
        kernel,
        out_shape=outs,
        in_specs=[IN_SMEM] * len(scalars) + [IN_VMEM] * len(arrays),
        out_specs=(IN_VMEM,) * len(outs) if many else IN_VMEM,
        scratch_shapes=list(scratch),
        compiler_params=params(extra),
        name=name,
    )(*scalars, *arrays[:moved], *[keep(value) for value in arrays[moved:]])


def tall_kernel(genotypes, codes, covariates, out, rows):
    snps = genotypes.shape[1]
    out[:snps, :] = jnp.transpose(genotypes[...])
    count = covariates.shape[0]
    site = lax.broadcasted_iota(jnp.int32, (SITES, codes.shape[1]), 0)
    rows[...] = jnp.zeros(rows.shape, jnp.float32)
    rows[:SITES, :] = (site == codes[...]).astype(jnp.float32)
    rows[SITES : SITES + count, :] = covariates[...].astype(jnp.float32)
    out[snps:, :] = rows[...].astype(jnp.bfloat16)


def tall_design(genotypes, covariates, site_codes):
    subjects, snps = genotypes.shape
    return pl.pallas_call(
        tall_kernel,
        out_shape=result((snps + DPAD, subjects), jnp.bfloat16),
        in_specs=[IN_VMEM] * 3,
        out_specs=IN_VMEM,
        scratch_shapes=[pltpu.VMEM((DPAD, subjects), jnp.float32)],
        compiler_params=params(VMEM_MOST),
        name="tall_design",
    )(genotypes, site_codes[None, :], covariates.T)


def smooth_kernel(group, planes, per_vox, parts, width, images, order, table, *outs):
    plane = table.shape[0]
    size = width // len(outs)
    groups = images.shape[1] // (group * planes)
    near = kernel_table(2 * REACH + 1)[REACH]
    for tile in range(images.shape[0] // SUBJ_TILE):
        here = pl.ds(tile * SUBJ_TILE, SUBJ_TILE)
        for part in range(groups):
            rows = images[here, part * group * planes : (part + 1) * group * planes, :]
            rows = rows.reshape(SUBJ_TILE * group * planes, plane)
            rows = jnp.dot(order[...], rows, preferred_element_type=jnp.float32)
            inplane = jnp.dot(
                rows.astype(jnp.bfloat16), table[...], preferred_element_type=jnp.float32
            )
            for m in range(group):
                slabs = [
                    inplane[(m * planes + x) * SUBJ_TILE : (m * planes + x + 1) * SUBJ_TILE]
                    for x in range(planes)
                ]
                for x in range(planes):
                    total = slabs[x] * float(near[REACH])
                    for lag in range(1, REACH + 1):
                        sides = [slabs[k] for k in (x - lag, x + lag) if 0 <= k < planes]
                        if sides:
                            total = total + functools.reduce(jnp.add, sides) * float(
                                near[REACH + lag]
                            )
                    column = ((part * group + m) * per_vox + x % per_vox) * plane
                    target = (x // per_vox) * parts + column // width
                    chunk, first = column % width // size, column % size
                    out = outs[chunk]
                    out[target, here, first : first + plane] = total.astype(jnp.bfloat16)


def smooth(images, n_vox, parts, chunks):
    subjects, maps, planes, plane = images.shape
    per_vox = planes // n_vox
    width = maps * per_vox * plane // parts
    size = width // chunks
    assert size % plane == 0
    group = max(1, min(maps, 256 // (SUBJ_TILE * planes)))
    step = 32
    order = jnp.asarray(row_order(group, planes))
    table = jnp.asarray(plane_kernel(plane))
    return pl.pallas_call(
        functools.partial(smooth_kernel, group, planes, per_vox, parts, width),
        out_shape=[jax.ShapeDtypeStruct((n_vox * parts, subjects, size), jnp.bfloat16)] * chunks,
        grid=(subjects // step,),
        in_specs=[
            pl.BlockSpec((step, maps * planes, plane), lambda i: (i, 0, 0)),
            pl.BlockSpec(order.shape, lambda i: (0, 0)),
            pl.BlockSpec(table.shape, lambda i: (0, 0)),
        ],
        out_specs=[pl.BlockSpec((n_vox * parts, step, size), lambda i: (0, i, 0))] * chunks,
        compiler_params=params(VMEM_MOST),
        name="smooth",
    )(images.reshape(subjects, maps * planes, plane), order, table)


def moments_kernel(snps, slots, me, blocks, others, joined, out):
    rows = []
    half = len(slots) // 2
    for source in range(len(slots)):
        offset = jnp.bitwise_xor(me[0], source)
        index = 0
        for place, slot in enumerate(slots):
            index = index + jnp.where(offset == place, slot, 0)
        place = lax.rem(index, half)
        rows.append(jnp.where(index < half, blocks[place], others[place]))
    rows = jnp.concatenate(rows, axis=1)
    joined[...] = rows
    across = (((1,), (1,)), ((), ()))
    out[...] = jnp.zeros(out.shape, jnp.float32)
    out[:DPAD, : snps + DPAD] = lax.dot_general(
        rows[snps:], rows, across, preferred_element_type=jnp.float32
    )
    wide = rows[:snps].astype(jnp.float32)
    wide = wide * wide
    high = wide.astype(jnp.bfloat16)
    low = (wide - high.astype(jnp.float32)).astype(jnp.bfloat16)
    ones = jnp.ones((8, rows.shape[1]), jnp.bfloat16)
    squares = lax.dot_general(ones, high, across, preferred_element_type=jnp.float32)
    squares = squares + lax.dot_general(ones, low, across, preferred_element_type=jnp.float32)
    out[DPAD:, :snps] = squares


def moments(blocks, others, slots, me):
    count, rows, subjects = blocks.shape
    snps = rows - DPAD
    spread = -(-rows // LANES) * LANES
    outs = (
        result((rows, 2 * count * subjects), blocks.dtype),
        result((DPAD + 8, spread), jnp.float32),
    )
    kernel = functools.partial(moments_kernel, snps, slots)
    return call(kernel, "moments", outs, [me], [blocks, others], (), 2)


def eliminate(total, snps, design, guard):
    lane = lax.broadcasted_iota(jnp.int32, (DPAD, LANES), 1)
    row = lax.broadcasted_iota(jnp.int32, (DPAD, LANES), 0)
    shift = 32
    gram = total[:DPAD, snps : snps + LANES]
    work = jnp.where((row >= design) & (lane == row), 1.0, gram)
    work = jnp.where(lane == row + shift, 1.0, work)
    for k in range(design):
        pivot = work[k : k + 1, k : k + 1]
        line = work[k : k + 1, :] / pivot
        if guard:
            line = jnp.where(pivot > gram[k : k + 1, k : k + 1] * 2.0**-14, line, 0.0)
        work = jnp.where(row == k, line, work - work[:, k : k + 1] * line)
    solved = pltpu.roll(work, LANES - shift, 1)
    return jnp.where((lane < design) & (row < design), solved, 0.0)


def gene_fit(total, snps, design, guard):
    solved = eliminate(total, snps, design, guard)
    cross_gene = total[:DPAD, :snps]
    fitted = jnp.dot(
        solved[:, :DPAD], cross_gene, precision=HIGHEST, preferred_element_type=jnp.float32
    )
    square = total[DPAD : DPAD + 1, :snps]
    rss = square - jnp.sum(cross_gene * fitted, axis=0, keepdims=True)
    if guard:
        rss = jnp.maximum(rss, square * 2.0**-10) + 1e-30
    return solved, fitted, lax.rsqrt(rss)


def pair_kernel(snps, design, moment, coef, lines):
    _, fitted, scale = gene_fit(moment[...], snps, design, True)
    lines[...] = jnp.zeros(lines.shape, jnp.float32)
    lines[:DPAD, :] = fitted * scale
    lines[SCALE_LANE : SCALE_LANE + 1, :] = scale
    coef[...] = jnp.transpose(lines[...])


def pair_fit(moment, snps, design):
    kernel = functools.partial(pair_kernel, snps, design)
    scratch = [pltpu.VMEM((LANES, snps), jnp.float32)]
    return call(kernel, "pair_fit", result((snps, LANES), jnp.float32), [], [moment], scratch)


def cohort_kernel(snps, design, *refs):
    parts, (coef, inverse, lines) = refs[:-3], refs[-3:]
    moment = [part[...] for part in parts]
    solved, fitted, scale = gene_fit(tree_sum(moment), snps, design, False)
    inverse[...] = solved
    lines[...] = jnp.zeros(lines.shape, jnp.float32)
    lines[:DPAD, :] = fitted * -scale
    lines[SCALE_LANE : SCALE_LANE + 1, :] = scale
    for j in range(1, len(parts)):
        _, fit, own_scale = gene_fit(moment[j], snps, design, True)
        lines[j * STRIDE : j * STRIDE + DPAD, :] = fit * scale
        lines[SCALE_LANE + j : SCALE_LANE + j + 1, :] = scale / own_scale
    coef[...] = jnp.transpose(lines[...])


def cohort_fit(parts, snps, design):
    kernel = functools.partial(cohort_kernel, snps, design)
    outs = (result((snps, LANES), jnp.float32), result((DPAD, LANES), jnp.float32))
    scratch = [pltpu.VMEM((LANES, snps), jnp.float32)]
    return call(kernel, "cohort_fit", outs, [], parts, scratch)


def column_norm(sums, here):
    square = sums[SQUARE_ROW : SQUARE_ROW + 1, :]
    mean = jnp.sum(sums[:SITES, :], axis=0, keepdims=True) * (1.0 / here)
    spread = jnp.maximum(square - mean * mean * here, square * 2.0**-10)
    return jnp.sqrt(spread + 1e-30)


def sums_kernel(genes, columns, out):
    values = columns[...]
    wide = values.astype(jnp.float32)
    design = genes[genes.shape[0] - DPAD :, :]
    sums = jnp.dot(design, values, preferred_element_type=jnp.float32)
    square = jnp.sum(wide * wide, axis=0, keepdims=True)
    row = lax.broadcasted_iota(jnp.int32, sums.shape, 0)
    out[...] = jnp.where(row == SQUARE_ROW, square, sums)


def column_sums(genes, columns):
    outs = result((DPAD, columns.shape[1]), jnp.float32)
    return call(sums_kernel, "column_sums", outs, [], [genes, columns])


def products_kernel(here, first, me, genes, columns, coef, stats, own, *refs):
    far, held = refs[:-1], refs[-1]
    snps, width = held.shape
    held[...] = jnp.dot(
        genes[:snps, :],
        columns[:, first : first + width],
        preferred_element_type=jnp.float32,
    )
    cross_image = stats[:, first : first + width]
    over = 1.0 / column_norm(cross_image, here)
    size = own.shape[0]
    own[...] = held[pl.ds(pl.multiple_of(me[0] * size, size), size), :]
    for j, out in enumerate(far):
        place = pl.multiple_of(jnp.bitwise_xor(me[0], j + 1) * size, size)
        line = coef[pl.ds(place, size), :]
        fit = jnp.dot(
            line[:, :DPAD], cross_image, precision=HIGHEST, preferred_element_type=jnp.float32
        )
        scale = line[:, SCALE_LANE : SCALE_LANE + 1]
        out[...] = (scale * held[pl.ds(place, size), :] - fit) * over


def products(genes, columns, coef, stats, me, count, first, width):
    rows, here = genes.shape
    snps = rows - DPAD
    size = snps // count
    outs = (pltpu.HBM((size, width), jnp.float32),)
    outs += (result((size, width), jnp.float32),) * (count - 1)
    kernel = functools.partial(products_kernel, float(here), first)
    scratch = [pltpu.VMEM((snps, width), jnp.float32)]
    return call(kernel, "products", outs, [me], [genes, columns, coef, stats], scratch)


def base_kernel(here, first, me, own, coef, inverse, *refs):
    parts, (base, factors, stack) = refs[:-3], refs[-3:]
    stats = [part[:, first : first + own.shape[1]] for part in parts]
    row = lax.broadcasted_iota(jnp.int32, stats[0].shape, 0)
    total = tree_sum(stats)
    cross_image = jnp.where(row < SQUARE_ROW, total, 0.0)
    solved = jnp.dot(
        inverse[:, :DPAD], cross_image, precision=HIGHEST, preferred_element_type=jnp.float32
    )
    rss = total[SQUARE_ROW : SQUARE_ROW + 1, :] - jnp.sum(
        cross_image * solved, axis=0, keepdims=True
    )
    scale = lax.rsqrt(rss)
    stack[...] = jnp.zeros(stack.shape, jnp.float32)
    stack[:DPAD, :] = cross_image
    factors[...] = jnp.zeros(factors.shape, jnp.float32)
    for j in range(1, len(parts)):
        stack[j * STRIDE : j * STRIDE + DPAD, :] = jnp.where(row < SQUARE_ROW, stats[j], 0.0)
        factors[j : j + 1, :] = column_norm(stats[j], here) * scale
    size = own.shape[0]
    line = coef[pl.ds(pl.multiple_of(me[0] * size, size), size), :]
    terms = jnp.dot(line, stack[...], precision=HIGHEST, preferred_element_type=jnp.float32)
    base[...] = (line[:, SCALE_LANE : SCALE_LANE + 1] * own[...] + terms) * scale


def base_ratio(me, own, coef, inverse, parts, here, first):
    size, width = own.shape
    outs = (result((size, width), jnp.float32), result((8, width), jnp.float32))
    kernel = functools.partial(base_kernel, float(here), first)
    scratch = [pltpu.VMEM((LANES, width), jnp.float32)]
    return call(kernel, "base_ratio", outs, [me], [own, coef, inverse, *parts], scratch, 1)


def permute_xor(value, axes, bits):
    size = lax.axis_size(axes)
    return lax.ppermute(value, axes, [(i, i ^ bits) for i in range(size)])


def on_device(images, genotypes, covariates, site_codes):
    subjects, maps, planes, plane = images.shape
    n_vox, n_far, n_near = (lax.axis_size(name) for name in ("vox", "far", "near"))
    vox, far, near = (lax.axis_index(name) for name in ("vox", "far", "near"))
    snps = genotypes.shape[1]
    design = SITES + covariates.shape[1]
    per_vox = planes // n_vox
    count = n_vox * n_near
    here = count * subjects

    def exchange(value):
        value = lax.all_to_all(value, ("vox", "near"), 0, 0, tiled=True)
        return value.reshape(here, value.shape[2])

    tall = tall_design(genotypes, covariates, site_codes)
    other = n_near
    offsets = [o for o in range(count) if not o & other]
    blocks = [tall] + [permute_xor(tall, ("vox", "near"), o) for o in offsets[1:]]
    (smoothed,) = smooth(images, n_vox, n_near, 1)
    smoothed, *blocks = lax.optimization_barrier((smoothed, *blocks))
    columns = exchange(smoothed)
    blocks = jnp.stack(blocks)
    others = permute_xor(blocks, ("vox", "near"), other)
    order = offsets + [o | other for o in offsets]
    slots = tuple(order.index(o) for o in range(count))
    genes, moment = moments(blocks, others, slots, (vox * n_near + near)[None])
    pair_coef = pair_fit(moment, snps, design)
    moment_parts = [moment] + [permute_xor(moment, "far", j) for j in range(1, n_far)]
    columns, moment_parts = lax.optimization_barrier((columns, moment_parts))
    stats = column_sums(genes, columns)
    stat_parts = [stats] + [permute_xor(stats, "far", j) for j in range(1, n_far)]

    size = snps // n_far
    panel = size // n_near
    freedom = float(here * n_far - design - 1)

    def send(pieces):
        return [permute_xor(pieces[j - 1], "far", j) for j in range(1, n_far)]

    def panel_stats(index, coef, base, factors, pieces):
        first = index * panel
        line = lax.dynamic_slice_in_dim(coef, far * size + first, panel, 0)
        ratio = lax.dynamic_slice_in_dim(base, first, panel, 0)
        for j in range(1, n_far):
            piece = lax.dynamic_slice_in_dim(pieces[j - 1], first, panel, 0)
            weight = line[:, SCALE_LANE + j, None] * factors[None, j]
            ratio = ratio + piece.astype(jnp.float32) * weight
        return ratio * jnp.sqrt(freedom / (1.0 - ratio * ratio))

    owns, received = [], []
    width = columns.shape[1] // CHUNKS
    for chunk in range(CHUNKS):
        own, *pieces = products(
            genes, columns, pair_coef, stats, far[None], n_far, chunk * width, width
        )
        owns.append(own)
        received.append(send([piece.astype(jnp.float16) for piece in pieces]))
    coef, inverse = cohort_fit(moment_parts, snps, design)
    outs = []
    gate = None
    for chunk in range(CHUNKS):
        base, factors = base_ratio(
            far[None], owns[chunk], coef, inverse, stat_parts, here, chunk * width
        )
        if gate is not None:
            base, gate = lax.optimization_barrier((base, gate))
            outs[-1][0] = gate
        pieces = received[chunk]
        gate = panel_stats(jnp.bitwise_xor(near, 1), coef, base, factors, pieces)
        outs.append([gate, panel_stats(near, coef, base, factors, pieces)])
    outs = [
        (permute_xor((away * NARROW).astype(jnp.float16), "near", 1), home) for away, home in outs
    ]
    outs = [(away.astype(jnp.float32) * (1.0 / NARROW), home) for away, home in outs]
    outs = [
        jnp.where(near == 0, jnp.stack([home, away], 1), jnp.stack([away, home], 1))
        for away, home in outs
    ]
    return jnp.stack(outs, axis=2).reshape(panel, maps, per_vox, plane)


def solution(mesh):
    sizes = dict(mesh.shape)
    devices = mesh.devices.reshape(sizes["group"], sizes["vox"], sizes["snp"] // 2, 2)
    split = Mesh(devices, ("group", "vox", "far", "near"))
    owner = ("group", "vox", "far", "near")
    placed = (P(owner, None, None, None), P(owner, None), P(owner, None), P(owner))
    return jax.shard_map(
        on_device,
        mesh=split,
        in_specs=placed,
        out_specs=P(("group", "far", "near"), None, "vox", None),
        check_vma=False,
    )
```

```python
import functools

import jax
import jax.numpy as jnp
import ml_dtypes
import numpy as np
from jax import lax
from jax.experimental import pallas as pl
from jax.experimental.pallas import tpu as pltpu
from jax.sharding import Mesh
from jax.sharding import PartitionSpec as P

SY = 16
SZ = 16
SITES = 4
REACH = 2
DPAD = 24
LANES = 128
SUBJ_TILE = 16
HIGHEST = lax.Precision.HIGHEST
VMEM_MOST = 56 * 2**20
VMEM_BASE = 12 * 2**20
SQUARE_ROW = 20
CHUNKS = 2
NARROW = 2.0**-4
SCALE_LANE = DPAD
STRIDE = 32


def kernel_table(length):
    position = np.arange(length)
    offset = (position[:, None] - position[None, :]).astype(np.float32)
    weights = np.where(np.abs(offset) <= REACH, np.exp(-offset * offset / np.float32(2.0)), np.float32(0.0))
    total = sum(np.exp(-(k * k) / 2.0) for k in range(-REACH, REACH + 1))
    return (weights / np.float32(total)).astype(np.float32)


def plane_kernel(plane):
    row, depth = kernel_table(SY), kernel_table(SZ)
    table = row[:, None, :, None] * depth[None, :, None, :]
    return table.reshape(plane, plane).astype(ml_dtypes.bfloat16)


def row_order(maps, planes):
    rows = SUBJ_TILE * maps * planes
    source = np.arange(rows).reshape(SUBJ_TILE, maps * planes).T.reshape(-1)
    return np.eye(rows, dtype=np.float32)[source].astype(ml_dtypes.bfloat16)


def tree_sum(terms):
    while len(terms) > 1:
        terms = [terms[i] + terms[i + 1] for i in range(0, len(terms), 2)]
    return terms[0]


RESIDENT = 3 * 2**20
IN_VMEM = pl.BlockSpec(memory_space=pltpu.VMEM)
IN_SMEM = pl.BlockSpec(memory_space=pltpu.SMEM)


def params(extra=0):
    return pltpu.CompilerParams(vmem_limit_bytes=min(VMEM_MOST, VMEM_BASE + extra))


def size_of(value):
    return int(np.prod(value.shape)) * jnp.dtype(value.dtype).itemsize


def small(shape, dtype):
    return int(np.prod(shape)) * jnp.dtype(dtype).itemsize <= RESIDENT


def keep(value):
    if small(value.shape, value.dtype):
        return pltpu.with_memory_space_constraint(value, pltpu.VMEM)
    return value


def result(shape, dtype):
    if small(shape, dtype):
        return pltpu.VMEM(shape, dtype)
    return jax.ShapeDtypeStruct(shape, dtype)


def call(kernel, name, outs, scalars, arrays, scratch=(), moved=0):
    many = isinstance(outs, tuple)
    sizes = [size_of(value) for value in (*arrays, *(outs if many else (outs,)))]
    extra = 3 * sum(size for size in sizes if size > RESIDENT)
    return pl.pallas_call(
        kernel,
        out_shape=outs,
        in_specs=[IN_SMEM] * len(scalars) + [IN_VMEM] * len(arrays),
        out_specs=(IN_VMEM,) * len(outs) if many else IN_VMEM,
        scratch_shapes=list(scratch),
        compiler_params=params(extra),
        name=name,
    )(*scalars, *arrays[:moved], *[keep(value) for value in arrays[moved:]])


def tall_kernel(genotypes, codes, covariates, out, rows):
    snps = genotypes.shape[1]
    out[:snps, :] = jnp.transpose(genotypes[...])
    count = covariates.shape[0]
    site = lax.broadcasted_iota(jnp.int32, (SITES, codes.shape[1]), 0)
    rows[...] = jnp.zeros(rows.shape, jnp.float32)
    rows[:SITES, :] = (site == codes[...]).astype(jnp.float32)
    rows[SITES : SITES + count, :] = covariates[...].astype(jnp.float32)
    out[snps:, :] = rows[...].astype(jnp.bfloat16)


def tall_design(genotypes, covariates, site_codes):
    subjects, snps = genotypes.shape
    return pl.pallas_call(
        tall_kernel,
        out_shape=result((snps + DPAD, subjects), jnp.bfloat16),
        in_specs=[IN_VMEM] * 3,
        out_specs=IN_VMEM,
        scratch_shapes=[pltpu.VMEM((DPAD, subjects), jnp.float32)],
        compiler_params=params(VMEM_MOST),
        name="tall_design",
    )(genotypes, site_codes[None, :], covariates.T)


def smooth_kernel(group, planes, per_vox, parts, width, images, order, table, *outs):
    plane = table.shape[0]
    size = width // len(outs)
    groups = images.shape[1] // (group * planes)
    near = kernel_table(2 * REACH + 1)[REACH]
    for tile in range(images.shape[0] // SUBJ_TILE):
        here = pl.ds(tile * SUBJ_TILE, SUBJ_TILE)
        for part in range(groups):
            rows = images[here, part * group * planes : (part + 1) * group * planes, :]
            rows = rows.reshape(SUBJ_TILE * group * planes, plane)
            rows = jnp.dot(order[...], rows, preferred_element_type=jnp.float32)
            inplane = jnp.dot(
                rows.astype(jnp.bfloat16), table[...], preferred_element_type=jnp.float32
            )
            for m in range(group):
                slabs = [
                    inplane[(m * planes + x) * SUBJ_TILE : (m * planes + x + 1) * SUBJ_TILE]
                    for x in range(planes)
                ]
                for x in range(planes):
                    total = slabs[x] * float(near[REACH])
                    for lag in range(1, REACH + 1):
                        sides = [slabs[k] for k in (x - lag, x + lag) if 0 <= k < planes]
                        if sides:
                            total = total + functools.reduce(jnp.add, sides) * float(
                                near[REACH + lag]
                            )
                    column = ((part * group + m) * per_vox + x % per_vox) * plane
                    target = (x // per_vox) * parts + column // width
                    chunk, first = column % width // size, column % size
                    out = outs[chunk]
                    out[target, here, first : first + plane] = total.astype(jnp.bfloat16)


def smooth(images, n_vox, parts, chunks):
    subjects, maps, planes, plane = images.shape
    per_vox = planes // n_vox
    width = maps * per_vox * plane // parts
    size = width // chunks
    assert size % plane == 0
    group = max(1, min(maps, 256 // (SUBJ_TILE * planes)))
    step = 32
    order = jnp.asarray(row_order(group, planes))
    table = jnp.asarray(plane_kernel(plane))
    return pl.pallas_call(
        functools.partial(smooth_kernel, group, planes, per_vox, parts, width),
        out_shape=[jax.ShapeDtypeStruct((n_vox * parts, subjects, size), jnp.bfloat16)] * chunks,
        grid=(subjects // step,),
        in_specs=[
            pl.BlockSpec((step, maps * planes, plane), lambda i: (i, 0, 0)),
            pl.BlockSpec(order.shape, lambda i: (0, 0)),
            pl.BlockSpec(table.shape, lambda i: (0, 0)),
        ],
        out_specs=[pl.BlockSpec((n_vox * parts, step, size), lambda i: (0, i, 0))] * chunks,
        compiler_params=params(VMEM_MOST),
        name="smooth",
    )(images.reshape(subjects, maps * planes, plane), order, table)


def moments_kernel(snps, slots, me, blocks, others, joined, out):
    rows = []
    half = len(slots) // 2
    for source in range(len(slots)):
        offset = jnp.bitwise_xor(me[0], source)
        index = 0
        for place, slot in enumerate(slots):
            index = index + jnp.where(offset == place, slot, 0)
        place = lax.rem(index, half)
        rows.append(jnp.where(index < half, blocks[place], others[place]))
    rows = jnp.concatenate(rows, axis=1)
    joined[...] = rows
    across = (((1,), (1,)), ((), ()))
    out[...] = jnp.zeros(out.shape, jnp.float32)
    out[:DPAD, : snps + DPAD] = lax.dot_general(
        rows[snps:], rows, across, preferred_element_type=jnp.float32
    )
    wide = rows[:snps].astype(jnp.float32)
    wide = wide * wide
    high = wide.astype(jnp.bfloat16)
    low = (wide - high.astype(jnp.float32)).astype(jnp.bfloat16)
    ones = jnp.ones((8, rows.shape[1]), jnp.bfloat16)
    squares = lax.dot_general(ones, high, across, preferred_element_type=jnp.float32)
    squares = squares + lax.dot_general(ones, low, across, preferred_element_type=jnp.float32)
    out[DPAD:, :snps] = squares


def moments(blocks, others, slots, me):
    count, rows, subjects = blocks.shape
    snps = rows - DPAD
    spread = -(-rows // LANES) * LANES
    outs = (
        result((rows, 2 * count * subjects), blocks.dtype),
        pltpu.HBM((DPAD + 8, spread), jnp.float32),
    )
    kernel = functools.partial(moments_kernel, snps, slots)
    return call(kernel, "moments", outs, [me], [blocks, others], (), 2)


def eliminate(total, snps, design, guard):
    lane = lax.broadcasted_iota(jnp.int32, (DPAD, LANES), 1)
    row = lax.broadcasted_iota(jnp.int32, (DPAD, LANES), 0)
    shift = 32
    gram = total[:DPAD, snps : snps + LANES]
    work = jnp.where((row >= design) & (lane == row), 1.0, gram)
    work = jnp.where(lane == row + shift, 1.0, work)
    for k in range(design):
        pivot = work[k : k + 1, k : k + 1]
        line = work[k : k + 1, :] / pivot
        if guard:
            line = jnp.where(pivot > gram[k : k + 1, k : k + 1] * 2.0**-14, line, 0.0)
        work = jnp.where(row == k, line, work - work[:, k : k + 1] * line)
    solved = pltpu.roll(work, LANES - shift, 1)
    return jnp.where((lane < design) & (row < design), solved, 0.0)


def gene_fit(total, snps, design, guard):
    solved = eliminate(total, snps, design, guard)
    cross_gene = total[:DPAD, :snps]
    fitted = jnp.dot(
        solved[:, :DPAD], cross_gene, precision=HIGHEST, preferred_element_type=jnp.float32
    )
    square = total[DPAD : DPAD + 1, :snps]
    rss = square - jnp.sum(cross_gene * fitted, axis=0, keepdims=True)
    if guard:
        rss = jnp.maximum(rss, square * 2.0**-10) + 1e-30
    return solved, fitted, lax.rsqrt(rss)


def pair_kernel(snps, design, moment, coef, lines):
    _, fitted, scale = gene_fit(moment[...], snps, design, True)
    lines[...] = jnp.zeros(lines.shape, jnp.float32)
    lines[:DPAD, :] = fitted * scale
    lines[SCALE_LANE : SCALE_LANE + 1, :] = scale
    coef[...] = jnp.transpose(lines[...])


def pair_fit(moment, snps, design):
    kernel = functools.partial(pair_kernel, snps, design)
    scratch = [pltpu.VMEM((LANES, snps), jnp.float32)]
    return call(kernel, "pair_fit", result((snps, LANES), jnp.float32), [], [moment], scratch, 1)


def cohort_kernel(snps, design, *refs):
    parts, (coef, inverse, lines) = refs[:-3], refs[-3:]
    moment = [part[...] for part in parts]
    solved, fitted, scale = gene_fit(tree_sum(moment), snps, design, False)
    inverse[...] = solved
    lines[...] = jnp.zeros(lines.shape, jnp.float32)
    lines[:DPAD, :] = fitted * -scale
    lines[SCALE_LANE : SCALE_LANE + 1, :] = scale
    for j in range(1, len(parts)):
        _, fit, own_scale = gene_fit(moment[j], snps, design, True)
        lines[j * STRIDE : j * STRIDE + DPAD, :] = fit * scale
        lines[SCALE_LANE + j : SCALE_LANE + j + 1, :] = scale / own_scale
    coef[...] = jnp.transpose(lines[...])


def cohort_fit(parts, snps, design):
    kernel = functools.partial(cohort_kernel, snps, design)
    outs = (result((snps, LANES), jnp.float32), result((DPAD, LANES), jnp.float32))
    scratch = [pltpu.VMEM((LANES, snps), jnp.float32)]
    return call(kernel, "cohort_fit", outs, [], parts, scratch, len(parts))


def column_norm(sums, here):
    square = sums[SQUARE_ROW : SQUARE_ROW + 1, :]
    mean = jnp.sum(sums[:SITES, :], axis=0, keepdims=True) * (1.0 / here)
    spread = jnp.maximum(square - mean * mean * here, square * 2.0**-10)
    return jnp.sqrt(spread + 1e-30)


def sums_kernel(genes, columns, out):
    values = columns[...]
    wide = values.astype(jnp.float32)
    design = genes[genes.shape[0] - DPAD :, :]
    sums = jnp.dot(design, values, preferred_element_type=jnp.float32)
    square = jnp.sum(wide * wide, axis=0, keepdims=True)
    row = lax.broadcasted_iota(jnp.int32, sums.shape, 0)
    out[...] = jnp.where(row == SQUARE_ROW, square, sums)


def column_sums(genes, columns):
    outs = result((DPAD, columns.shape[1]), jnp.float32)
    return call(sums_kernel, "column_sums", outs, [], [genes, columns])


def products_kernel(here, first, me, genes, columns, coef, stats, own, *refs):
    far, held = refs[:-1], refs[-1]
    snps, width = held.shape
    held[...] = jnp.dot(
        genes[:snps, :],
        columns[:, first : first + width],
        preferred_element_type=jnp.float32,
    )
    cross_image = stats[:, first : first + width]
    over = 1.0 / column_norm(cross_image, here)
    size = own.shape[0]
    own[...] = held[pl.ds(pl.multiple_of(me[0] * size, size), size), :]
    for j, out in enumerate(far):
        place = pl.multiple_of(jnp.bitwise_xor(me[0], j + 1) * size, size)
        line = coef[pl.ds(place, size), :]
        fit = jnp.dot(
            line[:, :DPAD], cross_image, precision=HIGHEST, preferred_element_type=jnp.float32
        )
        scale = line[:, SCALE_LANE : SCALE_LANE + 1]
        out[...] = (scale * held[pl.ds(place, size), :] - fit) * over


def products(genes, columns, coef, stats, me, count, first, width):
    rows, here = genes.shape
    snps = rows - DPAD
    size = snps // count
    outs = (pltpu.HBM((size, width), jnp.float32),)
    outs += (result((size, width), jnp.float32),) * (count - 1)
    kernel = functools.partial(products_kernel, float(here), first)
    scratch = [pltpu.VMEM((snps, width), jnp.float32)]
    return call(kernel, "products", outs, [me], [genes, columns, coef, stats], scratch)


def base_kernel(here, first, me, own, coef, inverse, *refs):
    parts, (base, factors, stack) = refs[:-3], refs[-3:]
    stats = [part[:, first : first + own.shape[1]] for part in parts]
    row = lax.broadcasted_iota(jnp.int32, stats[0].shape, 0)
    total = tree_sum(stats)
    cross_image = jnp.where(row < SQUARE_ROW, total, 0.0)
    solved = jnp.dot(
        inverse[:, :DPAD], cross_image, precision=HIGHEST, preferred_element_type=jnp.float32
    )
    rss = total[SQUARE_ROW : SQUARE_ROW + 1, :] - jnp.sum(
        cross_image * solved, axis=0, keepdims=True
    )
    scale = lax.rsqrt(rss)
    stack[...] = jnp.zeros(stack.shape, jnp.float32)
    stack[:DPAD, :] = cross_image
    factors[...] = jnp.zeros(factors.shape, jnp.float32)
    for j in range(1, len(parts)):
        stack[j * STRIDE : j * STRIDE + DPAD, :] = jnp.where(row < SQUARE_ROW, stats[j], 0.0)
        factors[j : j + 1, :] = column_norm(stats[j], here) * scale
    size = own.shape[0]
    line = coef[pl.ds(pl.multiple_of(me[0] * size, size), size), :]
    terms = jnp.dot(line, stack[...], precision=HIGHEST, preferred_element_type=jnp.float32)
    base[...] = (line[:, SCALE_LANE : SCALE_LANE + 1] * own[...] + terms) * scale


def base_ratio(me, own, coef, inverse, parts, here, first):
    size, width = own.shape
    outs = (result((size, width), jnp.float32), result((8, width), jnp.float32))
    kernel = functools.partial(base_kernel, float(here), first)
    scratch = [pltpu.VMEM((LANES, width), jnp.float32)]
    return call(kernel, "base_ratio", outs, [me], [own, coef, inverse, *parts], scratch, 1)


def permute_xor(value, axes, bits):
    size = lax.axis_size(axes)
    return lax.ppermute(value, axes, [(i, i ^ bits) for i in range(size)])


def on_device(images, genotypes, covariates, site_codes):
    subjects, maps, planes, plane = images.shape
    n_vox, n_far, n_near = (lax.axis_size(name) for name in ("vox", "far", "near"))
    vox, far, near = (lax.axis_index(name) for name in ("vox", "far", "near"))
    snps = genotypes.shape[1]
    design = SITES + covariates.shape[1]
    per_vox = planes // n_vox
    count = n_vox * n_near
    here = count * subjects

    def exchange(value):
        value = lax.all_to_all(value, ("vox", "near"), 0, 0, tiled=True)
        return value.reshape(here, value.shape[2])

    tall = tall_design(genotypes, covariates, site_codes)
    other = n_near
    offsets = [o for o in range(count) if not o & other]
    blocks = [tall] + [permute_xor(tall, ("vox", "near"), o) for o in offsets[1:]]
    (smoothed,) = smooth(images, n_vox, n_near, 1)
    smoothed, *blocks = lax.optimization_barrier((smoothed, *blocks))
    columns = exchange(smoothed)
    blocks = jnp.stack(blocks)
    others = permute_xor(blocks, ("vox", "near"), other)
    order = offsets + [o | other for o in offsets]
    slots = tuple(order.index(o) for o in range(count))
    genes, moment = moments(blocks, others, slots, (vox * n_near + near)[None])
    pair_coef = pair_fit(moment, snps, design)
    moment_parts = [moment] + [permute_xor(moment, "far", j) for j in range(1, n_far)]
    columns, pair_coef, moment_parts = lax.optimization_barrier(
        (columns, pair_coef, moment_parts)
    )
    stats = column_sums(genes, columns)
    stat_parts = [stats] + [permute_xor(stats, "far", j) for j in range(1, n_far)]

    size = snps // n_far
    panel = size // n_near
    freedom = float(here * n_far - design - 1)

    def send(pieces):
        return [permute_xor(pieces[j - 1], "far", j) for j in range(1, n_far)]

    def panel_stats(index, coef, base, factors, pieces):
        first = index * panel
        line = lax.dynamic_slice_in_dim(coef, far * size + first, panel, 0)
        ratio = lax.dynamic_slice_in_dim(base, first, panel, 0)
        for j in range(1, n_far):
            piece = lax.dynamic_slice_in_dim(pieces[j - 1], first, panel, 0)
            weight = line[:, SCALE_LANE + j, None] * factors[None, j]
            ratio = ratio + piece.astype(jnp.float32) * weight
        return ratio * jnp.sqrt(freedom / (1.0 - ratio * ratio))

    owns, received = [], []
    width = columns.shape[1] // CHUNKS
    for chunk in range(CHUNKS):
        own, *pieces = products(
            genes, columns, pair_coef, stats, far[None], n_far, chunk * width, width
        )
        owns.append(own)
        pieces = [piece.astype(jnp.float16) for piece in pieces]
        if chunk == 0:
            pieces, stat_parts = lax.optimization_barrier((pieces, stat_parts))
        received.append(send(pieces))
    coef, inverse = cohort_fit(moment_parts, snps, design)
    outs = []
    gate = None
    for chunk in range(CHUNKS):
        base, factors = base_ratio(
            far[None], owns[chunk], coef, inverse, stat_parts, here, chunk * width
        )
        if gate is not None:
            base, gate = lax.optimization_barrier((base, gate))
            outs[-1][0] = gate
        pieces = received[chunk]
        gate = panel_stats(jnp.bitwise_xor(near, 1), coef, base, factors, pieces)
        outs.append([gate, panel_stats(near, coef, base, factors, pieces)])
    outs = [
        (permute_xor((away * NARROW).astype(jnp.float16), "near", 1), home) for away, home in outs
    ]
    outs = [(away.astype(jnp.float32) * (1.0 / NARROW), home) for away, home in outs]
    outs = [
        jnp.where(near == 0, jnp.stack([home, away], 1), jnp.stack([away, home], 1))
        for away, home in outs
    ]
    return jnp.stack(outs, axis=2).reshape(panel, maps, per_vox, plane)


def solution(mesh):
    sizes = dict(mesh.shape)
    devices = mesh.devices.reshape(sizes["group"], sizes["vox"], sizes["snp"] // 2, 2)
    split = Mesh(devices, ("group", "vox", "far", "near"))
    owner = ("group", "vox", "far", "near")
    placed = (P(owner, None, None, None), P(owner, None), P(owner, None), P(owner))
    return jax.shard_map(
        on_device,
        mesh=split,
        in_specs=placed,
        out_specs=P(("group", "far", "near"), None, "vox", None),
        check_vma=False,
    )
```

```python
import functools

import jax
import jax.numpy as jnp
import ml_dtypes
import numpy as np
from jax import lax
from jax.experimental import pallas as pl
from jax.experimental.pallas import tpu as pltpu
from jax.sharding import Mesh
from jax.sharding import PartitionSpec as P

SY = 16
SZ = 16
SITES = 4
REACH = 2
DPAD = 24
LANES = 128
SUBJ_TILE = 16
HIGHEST = lax.Precision.HIGHEST
VMEM_MOST = 56 * 2**20
VMEM_BASE = 12 * 2**20
SQUARE_ROW = 20
SCALE_LANE = DPAD
STRIDE = 32


def kernel_table(length):
    position = np.arange(length)
    offset = (position[:, None] - position[None, :]).astype(np.float32)
    weights = np.where(np.abs(offset) <= REACH, np.exp(-offset * offset / np.float32(2.0)), np.float32(0.0))
    total = sum(np.exp(-(k * k) / 2.0) for k in range(-REACH, REACH + 1))
    return (weights / np.float32(total)).astype(np.float32)


def plane_kernel(plane):
    row, depth = kernel_table(SY), kernel_table(SZ)
    table = row[:, None, :, None] * depth[None, :, None, :]
    return table.reshape(plane, plane).astype(ml_dtypes.bfloat16)


def row_order(maps, planes):
    rows = SUBJ_TILE * maps * planes
    source = np.arange(rows).reshape(SUBJ_TILE, maps * planes).T.reshape(-1)
    return np.eye(rows, dtype=np.float32)[source].astype(ml_dtypes.bfloat16)


def tree_sum(terms):
    while len(terms) > 1:
        terms = [terms[i] + terms[i + 1] for i in range(0, len(terms), 2)]
    return terms[0]


RESIDENT = 3 * 2**20
IN_VMEM = pl.BlockSpec(memory_space=pltpu.VMEM)
IN_SMEM = pl.BlockSpec(memory_space=pltpu.SMEM)


def params(extra=0):
    return pltpu.CompilerParams(vmem_limit_bytes=min(VMEM_MOST, VMEM_BASE + extra))


def size_of(value):
    return int(np.prod(value.shape)) * jnp.dtype(value.dtype).itemsize


def small(shape, dtype):
    return int(np.prod(shape)) * jnp.dtype(dtype).itemsize <= RESIDENT


def keep(value):
    if small(value.shape, value.dtype):
        return pltpu.with_memory_space_constraint(value, pltpu.VMEM)
    return value


def result(shape, dtype):
    if small(shape, dtype):
        return pltpu.VMEM(shape, dtype)
    return jax.ShapeDtypeStruct(shape, dtype)


def call(kernel, name, outs, scalars, arrays, scratch=(), moved=0):
    many = isinstance(outs, tuple)
    sizes = [size_of(value) for value in (*arrays, *(outs if many else (outs,)))]
    extra = 3 * sum(size for size in sizes if size > RESIDENT)
    return pl.pallas_call(
        kernel,
        out_shape=outs,
        in_specs=[IN_SMEM] * len(scalars) + [IN_VMEM] * len(arrays),
        out_specs=(IN_VMEM,) * len(outs) if many else IN_VMEM,
        scratch_shapes=list(scratch),
        compiler_params=params(extra),
        name=name,
    )(*scalars, *arrays[:moved], *[keep(value) for value in arrays[moved:]])


def tall_kernel(genotypes, codes, covariates, out, rows):
    snps = genotypes.shape[1]
    out[:snps, :] = jnp.transpose(genotypes[...])
    count = covariates.shape[0]
    site = lax.broadcasted_iota(jnp.int32, (SITES, codes.shape[1]), 0)
    rows[...] = jnp.zeros(rows.shape, jnp.float32)
    rows[:SITES, :] = (site == codes[...]).astype(jnp.float32)
    rows[SITES : SITES + count, :] = covariates[...].astype(jnp.float32)
    out[snps:, :] = rows[...].astype(jnp.bfloat16)


def tall_design(genotypes, covariates, site_codes):
    subjects, snps = genotypes.shape
    return pl.pallas_call(
        tall_kernel,
        out_shape=result((snps + DPAD, subjects), jnp.bfloat16),
        in_specs=[IN_VMEM] * 3,
        out_specs=IN_VMEM,
        scratch_shapes=[pltpu.VMEM((DPAD, subjects), jnp.float32)],
        compiler_params=params(VMEM_MOST),
        name="tall_design",
    )(genotypes, site_codes[None, :], covariates.T)


def smooth_kernel(group, planes, per_vox, parts, width, images, order, table, *outs):
    plane = table.shape[0]
    size = width // len(outs)
    groups = images.shape[1] // (group * planes)
    near = kernel_table(2 * REACH + 1)[REACH]
    for tile in range(images.shape[0] // SUBJ_TILE):
        here = pl.ds(tile * SUBJ_TILE, SUBJ_TILE)
        for part in range(groups):
            rows = images[here, part * group * planes : (part + 1) * group * planes, :]
            rows = rows.reshape(SUBJ_TILE * group * planes, plane)
            rows = jnp.dot(order[...], rows, preferred_element_type=jnp.float32)
            inplane = jnp.dot(
                rows.astype(jnp.bfloat16), table[...], preferred_element_type=jnp.float32
            )
            for m in range(group):
                slabs = [
                    inplane[(m * planes + x) * SUBJ_TILE : (m * planes + x + 1) * SUBJ_TILE]
                    for x in range(planes)
                ]
                for x in range(planes):
                    total = slabs[x] * float(near[REACH])
                    for lag in range(1, REACH + 1):
                        sides = [slabs[k] for k in (x - lag, x + lag) if 0 <= k < planes]
                        if sides:
                            total = total + functools.reduce(jnp.add, sides) * float(
                                near[REACH + lag]
                            )
                    column = ((part * group + m) * per_vox + x % per_vox) * plane
                    target = (x // per_vox) * parts + column // width
                    chunk, first = column % width // size, column % size
                    out = outs[chunk]
                    out[target, here, first : first + plane] = total.astype(jnp.bfloat16)


def smooth(images, n_vox, parts, chunks):
    subjects, maps, planes, plane = images.shape
    per_vox = planes // n_vox
    width = maps * per_vox * plane // parts
    size = width // chunks
    assert size % plane == 0
    group = max(1, min(maps, 256 // (SUBJ_TILE * planes)))
    step = 32
    order = jnp.asarray(row_order(group, planes))
    table = jnp.asarray(plane_kernel(plane))
    return pl.pallas_call(
        functools.partial(smooth_kernel, group, planes, per_vox, parts, width),
        out_shape=[jax.ShapeDtypeStruct((n_vox * parts, subjects, size), jnp.bfloat16)] * chunks,
        grid=(subjects // step,),
        in_specs=[
            pl.BlockSpec((step, maps * planes, plane), lambda i: (i, 0, 0)),
            pl.BlockSpec(order.shape, lambda i: (0, 0)),
            pl.BlockSpec(table.shape, lambda i: (0, 0)),
        ],
        out_specs=[pl.BlockSpec((n_vox * parts, step, size), lambda i: (0, i, 0))] * chunks,
        compiler_params=params(VMEM_MOST),
        name="smooth",
    )(images.reshape(subjects, maps * planes, plane), order, table)


def moments_kernel(snps, slots, me, blocks, others, joined, out):
    rows = []
    half = len(slots) // 2
    for source in range(len(slots)):
        offset = jnp.bitwise_xor(me[0], source)
        index = 0
        for place, slot in enumerate(slots):
            index = index + jnp.where(offset == place, slot, 0)
        place = lax.rem(index, half)
        rows.append(jnp.where(index < half, blocks[place], others[place]))
    rows = jnp.concatenate(rows, axis=1)
    joined[...] = rows
    across = (((1,), (1,)), ((), ()))
    out[...] = jnp.zeros(out.shape, jnp.float32)
    out[:DPAD, : snps + DPAD] = lax.dot_general(
        rows[snps:], rows, across, preferred_element_type=jnp.float32
    )
    wide = rows[:snps].astype(jnp.float32)
    wide = wide * wide
    high = wide.astype(jnp.bfloat16)
    low = (wide - high.astype(jnp.float32)).astype(jnp.bfloat16)
    ones = jnp.ones((8, rows.shape[1]), jnp.bfloat16)
    squares = lax.dot_general(ones, high, across, preferred_element_type=jnp.float32)
    squares = squares + lax.dot_general(ones, low, across, preferred_element_type=jnp.float32)
    out[DPAD:, :snps] = squares


def moments(blocks, others, slots, me):
    count, rows, subjects = blocks.shape
    snps = rows - DPAD
    spread = -(-rows // LANES) * LANES
    outs = (
        result((rows, 2 * count * subjects), blocks.dtype),
        pltpu.HBM((DPAD + 8, spread), jnp.float32),
    )
    kernel = functools.partial(moments_kernel, snps, slots)
    return call(kernel, "moments", outs, [me], [blocks, others], (), 2)


def eliminate(total, snps, design, guard):
    lane = lax.broadcasted_iota(jnp.int32, (DPAD, LANES), 1)
    row = lax.broadcasted_iota(jnp.int32, (DPAD, LANES), 0)
    shift = 32
    gram = total[:DPAD, snps : snps + LANES]
    work = jnp.where((row >= design) & (lane == row), 1.0, gram)
    work = jnp.where(lane == row + shift, 1.0, work)
    for k in range(design):
        pivot = work[k : k + 1, k : k + 1]
        line = work[k : k + 1, :] / pivot
        if guard:
            line = jnp.where(pivot > gram[k : k + 1, k : k + 1] * 2.0**-14, line, 0.0)
        work = jnp.where(row == k, line, work - work[:, k : k + 1] * line)
    solved = pltpu.roll(work, LANES - shift, 1)
    return jnp.where((lane < design) & (row < design), solved, 0.0)


def gene_fit(total, snps, design, guard):
    solved = eliminate(total, snps, design, guard)
    cross_gene = total[:DPAD, :snps]
    fitted = jnp.dot(
        solved[:, :DPAD], cross_gene, precision=HIGHEST, preferred_element_type=jnp.float32
    )
    square = total[DPAD : DPAD + 1, :snps]
    rss = square - jnp.sum(cross_gene * fitted, axis=0, keepdims=True)
    if guard:
        rss = jnp.maximum(rss, square * 2.0**-10) + 1e-30
    return solved, fitted, lax.rsqrt(rss)


def pair_kernel(snps, design, moment, coef, lines):
    _, fitted, scale = gene_fit(moment[...], snps, design, True)
    lines[...] = jnp.zeros(lines.shape, jnp.float32)
    lines[:DPAD, :] = fitted * scale
    lines[SCALE_LANE : SCALE_LANE + 1, :] = scale
    coef[...] = jnp.transpose(lines[...])


def pair_fit(moment, snps, design):
    kernel = functools.partial(pair_kernel, snps, design)
    scratch = [pltpu.VMEM((LANES, snps), jnp.float32)]
    return call(kernel, "pair_fit", result((snps, LANES), jnp.float32), [], [moment], scratch, 1)


def cohort_kernel(snps, design, *refs):
    parts, (coef, inverse, lines) = refs[:-3], refs[-3:]
    moment = [part[...] for part in parts]
    solved, fitted, scale = gene_fit(tree_sum(moment), snps, design, False)
    inverse[...] = solved
    lines[...] = jnp.zeros(lines.shape, jnp.float32)
    lines[:DPAD, :] = fitted * -scale
    lines[SCALE_LANE : SCALE_LANE + 1, :] = scale
    for j in range(len(parts)):
        _, fit, own_scale = gene_fit(moment[j], snps, design, True)
        lane = SCALE_LANE + 1 + j
        lines[lane : lane + 1, :] = scale / own_scale
        if j:
            lines[j * STRIDE : j * STRIDE + DPAD, :] = fit * scale
    coef[...] = jnp.transpose(lines[...])


def cohort_fit(parts, snps, design):
    kernel = functools.partial(cohort_kernel, snps, design)
    outs = (result((snps, LANES), jnp.float32), result((DPAD, LANES), jnp.float32))
    scratch = [pltpu.VMEM((LANES, snps), jnp.float32)]
    return call(kernel, "cohort_fit", outs, [], parts, scratch, len(parts))


def column_norm(sums, here):
    square = sums[SQUARE_ROW : SQUARE_ROW + 1, :]
    mean = jnp.sum(sums[:SITES, :], axis=0, keepdims=True) * (1.0 / here)
    spread = jnp.maximum(square - mean * mean * here, square * 2.0**-10)
    return jnp.sqrt(spread + 1e-30)


def sums_kernel(genes, columns, out):
    values = columns[...]
    wide = values.astype(jnp.float32)
    design = genes[genes.shape[0] - DPAD :, :]
    sums = jnp.dot(design, values, preferred_element_type=jnp.float32)
    square = jnp.sum(wide * wide, axis=0, keepdims=True)
    row = lax.broadcasted_iota(jnp.int32, sums.shape, 0)
    out[...] = jnp.where(row == SQUARE_ROW, square, sums)


def column_sums(genes, columns):
    outs = result((DPAD, columns.shape[1]), jnp.float32)
    return call(sums_kernel, "column_sums", outs, [], [genes, columns])


def products_kernel(here, offsets, far, near, genes, columns, coef, stats, *refs):
    outs, held = list(refs[:-1]), refs[-1]
    size = held.shape[0]
    panel = outs[0].shape[0]
    cross_image = stats[...]
    over = 1.0 / column_norm(cross_image, here)
    for j in offsets:
        block = pl.multiple_of(jnp.bitwise_xor(far[0], j) * size, size)
        held[...] = jnp.dot(
            genes[pl.ds(block, size), :], columns[...], preferred_element_type=jnp.float32
        )
        for k in range(size // panel):
            place = pl.multiple_of(jnp.bitwise_xor(near[0], k) * panel, panel)
            sums = held[pl.ds(place, panel), :]
            out = outs.pop(0)
            if j == 0 and k == 0:
                out[...] = sums
                continue
            line = coef[pl.ds(block + place, panel), :]
            fit = jnp.dot(
                line[:, :DPAD], cross_image, precision=HIGHEST, preferred_element_type=jnp.float32
            )
            out[...] = (line[:, SCALE_LANE : SCALE_LANE + 1] * sums - fit) * over


def products(genes, columns, coef, stats, far, near, offsets, size, count):
    here, width = columns.shape
    panel = size // count
    outs = [result((panel, width), jnp.float32) for _ in range(len(offsets) * count)]
    if 0 in offsets:
        outs[0] = pltpu.HBM((panel, width), jnp.float32)
    kernel = functools.partial(products_kernel, float(here), tuple(offsets))
    scratch = [pltpu.VMEM((size, width), jnp.float32)]
    arrays = [genes, columns, coef, stats]
    return call(kernel, "products", tuple(outs), [far, near], arrays, scratch)


def base_half(here, line, inverse, stats, extra, factors, stack):
    row = lax.broadcasted_iota(jnp.int32, stats[0].shape, 0)
    total = tree_sum(stats)
    known = row < SQUARE_ROW
    cross_image = jnp.where(known, total, 0.0)
    solved = jnp.dot(
        inverse[:, :DPAD], cross_image, precision=HIGHEST, preferred_element_type=jnp.float32
    )
    rss = total[SQUARE_ROW : SQUARE_ROW + 1, :] - jnp.sum(
        cross_image * solved, axis=0, keepdims=True
    )
    scale = lax.rsqrt(rss)
    stack[:DPAD, :] = cross_image
    factors[...] = jnp.zeros(factors.shape, jnp.float32)
    for j, stat in enumerate(stats):
        factors[j : j + 1, :] = column_norm(stat, here) * scale
        if j:
            stack[j * STRIDE : j * STRIDE + DPAD, :] = jnp.where(known, stat, 0.0)
    terms = jnp.dot(line, stack[...], precision=HIGHEST, preferred_element_type=jnp.float32)
    return (terms + extra) * scale


def base_kernel(here, place, own, coef, inverse, pair_coef, *refs):
    parts, (home, home_factors, away, away_factors, stack) = refs[:-5], refs[-5:]
    count = len(parts) // 2
    stack[...] = jnp.zeros(stack.shape, jnp.float32)
    panel = own.shape[0]
    rows = pl.ds(pl.multiple_of(place[0] * panel, panel), panel)
    line = coef[rows, :]
    stats = [part[...] for part in parts[:count]]
    extra = line[:, SCALE_LANE : SCALE_LANE + 1] * own[...]
    home[...] = base_half(here, line, inverse, stats, extra, home_factors, stack)
    stats = [part[...] for part in parts[count:]]
    row = lax.broadcasted_iota(jnp.int32, stats[0].shape, 0)
    extra = jnp.dot(
        pair_coef[rows, :][:, :DPAD],
        jnp.where(row < SQUARE_ROW, stats[0], 0.0),
        precision=HIGHEST,
        preferred_element_type=jnp.float32,
    )
    extra = line[:, SCALE_LANE + 1 : SCALE_LANE + 2] * extra
    away[...] = base_half(here, line, inverse, stats, extra, away_factors, stack)


def base_ratio(place, own, coef, inverse, pair_coef, parts, here):
    panel, width = own.shape
    outs = (result((panel, width), jnp.float32), result((8, width), jnp.float32)) * 2
    kernel = functools.partial(base_kernel, float(here))
    scratch = [pltpu.VMEM((LANES, width), jnp.float32)]
    arrays = [own, coef, inverse, pair_coef, *parts]
    return call(kernel, "base_ratio", outs, [place], arrays, scratch, 1)


def permute_xor(value, axes, bits):
    size = lax.axis_size(axes)
    return lax.ppermute(value, axes, [(i, i ^ bits) for i in range(size)])


def on_device(images, genotypes, covariates, site_codes):
    subjects, maps, planes, plane = images.shape
    n_vox, n_far, n_near = (lax.axis_size(name) for name in ("vox", "far", "near"))
    vox, far, near = (lax.axis_index(name) for name in ("vox", "far", "near"))
    snps = genotypes.shape[1]
    design = SITES + covariates.shape[1]
    per_vox = planes // n_vox
    count = n_vox * n_near
    here = count * subjects

    def exchange(value):
        value = lax.all_to_all(value, ("vox", "near"), 0, 0, tiled=True)
        return value.reshape(here, value.shape[2])

    tall = tall_design(genotypes, covariates, site_codes)
    other = n_near
    offsets = [o for o in range(count) if not o & other]
    blocks = [tall] + [permute_xor(tall, ("vox", "near"), o) for o in offsets[1:]]
    (smoothed,) = smooth(images, n_vox, n_near, 1)
    smoothed, *blocks = lax.optimization_barrier((smoothed, *blocks))
    columns = exchange(smoothed)
    blocks = jnp.stack(blocks)
    others = permute_xor(blocks, ("vox", "near"), other)
    order = offsets + [o | other for o in offsets]
    slots = tuple(order.index(o) for o in range(count))
    genes, moment = moments(blocks, others, slots, (vox * n_near + near)[None])
    pair_coef = pair_fit(moment, snps, design)
    moment_parts = [moment] + [permute_xor(moment, "far", j) for j in range(1, n_far)]
    coef, inverse = cohort_fit(moment_parts, snps, design)
    columns, pair_coef, coef, inverse = lax.optimization_barrier(
        (columns, pair_coef, coef, inverse)
    )
    stats = column_sums(genes, columns)
    stat_parts = [stats] + [permute_xor(stats, "far", j) for j in range(1, n_far)]

    size = snps // n_far
    panel = size // n_near
    freedom = float(here * n_far - design - 1)
    line = ("far", "near")
    where = [far[None], near[None]]

    def shrink(pieces):
        return [piece.astype(jnp.float16) for piece in pieces]

    sent = products(
        genes, columns, pair_coef, stats, *where, list(range(1, n_far)), size, n_near
    )
    sent = shrink(sent)
    sent, stat_parts = lax.optimization_barrier((sent, stat_parts))
    own, *rest = products(genes, columns, pair_coef, stats, *where, [0], size, n_near)
    sent = [own, *shrink(rest), *sent]
    pieces = [None] + [permute_xor(sent[k], line, k) for k in range(1, n_far * n_near)]
    away_parts = permute_xor(jnp.stack(stat_parts), "near", 1)
    away_parts = [away_parts[j] for j in range(n_far)]

    place = far * n_near + near
    columns_scale = lax.dynamic_slice_in_dim(coef, place * panel, panel, 0)

    home, home_factors, away, away_factors = base_ratio(
        place[None], own, coef, inverse, pair_coef, stat_parts + away_parts, here
    )

    def t_of(ratio, factors, offset):
        for j in range(n_far):
            piece = pieces[j * n_near + offset]
            if piece is not None:
                weight = columns_scale[:, SCALE_LANE + 1 + j, None] * factors[None, j]
                ratio = ratio + piece.astype(jnp.float32) * weight
        return ratio * jnp.sqrt(freedom / (1.0 - ratio * ratio))

    home = t_of(home, home_factors, 0)
    away = t_of(away, away_factors, 1)
    both = jnp.where(near == 0, jnp.stack([home, away], 1), jnp.stack([away, home], 1))
    return both.reshape(panel, maps, per_vox, plane)


def solution(mesh):
    sizes = dict(mesh.shape)
    devices = mesh.devices.reshape(sizes["group"], sizes["vox"], sizes["snp"] // 2, 2)
    split = Mesh(devices, ("group", "vox", "far", "near"))
    owner = ("group", "vox", "far", "near")
    placed = (P(owner, None, None, None), P(owner, None), P(owner, None), P(owner))
    return jax.shard_map(
        on_device,
        mesh=split,
        in_specs=placed,
        out_specs=P(("group", "far", "near"), None, "vox", None),
        check_vma=False,
    )
```

```python
import functools

import jax
import jax.numpy as jnp
import ml_dtypes
import numpy as np
from jax import lax
from jax.experimental import pallas as pl
from jax.experimental.pallas import tpu as pltpu
from jax.sharding import Mesh
from jax.sharding import PartitionSpec as P

SY = 16
SZ = 16
SITES = 4
REACH = 2
DPAD = 24
LANES = 128
SUBJ_TILE = 16
HIGHEST = lax.Precision.HIGHEST
VMEM_MOST = 56 * 2**20
VMEM_BASE = 12 * 2**20
SQUARE_ROW = 20
SCALE_LANE = DPAD
STRIDE = 32


def kernel_table(length):
    position = np.arange(length)
    offset = (position[:, None] - position[None, :]).astype(np.float32)
    weights = np.where(np.abs(offset) <= REACH, np.exp(-offset * offset / np.float32(2.0)), np.float32(0.0))
    total = sum(np.exp(-(k * k) / 2.0) for k in range(-REACH, REACH + 1))
    return (weights / np.float32(total)).astype(np.float32)


def plane_kernel(plane):
    row, depth = kernel_table(SY), kernel_table(SZ)
    table = row[:, None, :, None] * depth[None, :, None, :]
    return table.reshape(plane, plane).astype(ml_dtypes.bfloat16)


def row_order(maps, planes):
    rows = SUBJ_TILE * maps * planes
    source = np.arange(rows).reshape(SUBJ_TILE, maps * planes).T.reshape(-1)
    return np.eye(rows, dtype=np.float32)[source].astype(ml_dtypes.bfloat16)


def tree_sum(terms):
    while len(terms) > 1:
        terms = [terms[i] + terms[i + 1] for i in range(0, len(terms), 2)]
    return terms[0]


RESIDENT = 3 * 2**20
IN_VMEM = pl.BlockSpec(memory_space=pltpu.VMEM)
IN_SMEM = pl.BlockSpec(memory_space=pltpu.SMEM)


def params(extra=0):
    return pltpu.CompilerParams(vmem_limit_bytes=min(VMEM_MOST, VMEM_BASE + extra))


def size_of(value):
    return int(np.prod(value.shape)) * jnp.dtype(value.dtype).itemsize


def small(shape, dtype):
    return int(np.prod(shape)) * jnp.dtype(dtype).itemsize <= RESIDENT


def keep(value):
    if small(value.shape, value.dtype):
        return pltpu.with_memory_space_constraint(value, pltpu.VMEM)
    return value


def result(shape, dtype):
    if small(shape, dtype):
        return pltpu.VMEM(shape, dtype)
    return jax.ShapeDtypeStruct(shape, dtype)


def call(kernel, name, outs, scalars, arrays, scratch=(), moved=0):
    many = isinstance(outs, tuple)
    sizes = [size_of(value) for value in (*arrays, *(outs if many else (outs,)))]
    extra = 3 * sum(size for size in sizes if size > RESIDENT)
    return pl.pallas_call(
        kernel,
        out_shape=outs,
        in_specs=[IN_SMEM] * len(scalars) + [IN_VMEM] * len(arrays),
        out_specs=(IN_VMEM,) * len(outs) if many else IN_VMEM,
        scratch_shapes=list(scratch),
        compiler_params=params(extra),
        name=name,
    )(*scalars, *arrays[:moved], *[keep(value) for value in arrays[moved:]])


def tall_kernel(genotypes, codes, covariates, out, rows):
    snps = genotypes.shape[1]
    out[:snps, :] = jnp.transpose(genotypes[...])
    count = covariates.shape[0]
    site = lax.broadcasted_iota(jnp.int32, (SITES, codes.shape[1]), 0)
    rows[...] = jnp.zeros(rows.shape, jnp.float32)
    rows[:SITES, :] = (site == codes[...]).astype(jnp.float32)
    rows[SITES : SITES + count, :] = covariates[...].astype(jnp.float32)
    out[snps:, :] = rows[...].astype(jnp.bfloat16)


def tall_design(genotypes, covariates, site_codes):
    subjects, snps = genotypes.shape
    return pl.pallas_call(
        tall_kernel,
        out_shape=result((snps + DPAD, subjects), jnp.bfloat16),
        in_specs=[IN_VMEM] * 3,
        out_specs=IN_VMEM,
        scratch_shapes=[pltpu.VMEM((DPAD, subjects), jnp.float32)],
        compiler_params=params(VMEM_MOST),
        name="tall_design",
    )(genotypes, site_codes[None, :], covariates.T)


def smooth_kernel(group, planes, per_vox, parts, width, images, order, table, *outs):
    plane = table.shape[0]
    size = width // len(outs)
    groups = images.shape[1] // (group * planes)
    near = kernel_table(2 * REACH + 1)[REACH]
    for tile in range(images.shape[0] // SUBJ_TILE):
        here = pl.ds(tile * SUBJ_TILE, SUBJ_TILE)
        for part in range(groups):
            rows = images[here, part * group * planes : (part + 1) * group * planes, :]
            rows = rows.reshape(SUBJ_TILE * group * planes, plane)
            rows = jnp.dot(order[...], rows, preferred_element_type=jnp.float32)
            inplane = jnp.dot(
                rows.astype(jnp.bfloat16), table[...], preferred_element_type=jnp.float32
            )
            for m in range(group):
                slabs = [
                    inplane[(m * planes + x) * SUBJ_TILE : (m * planes + x + 1) * SUBJ_TILE]
                    for x in range(planes)
                ]
                for x in range(planes):
                    total = slabs[x] * float(near[REACH])
                    for lag in range(1, REACH + 1):
                        sides = [slabs[k] for k in (x - lag, x + lag) if 0 <= k < planes]
                        if sides:
                            total = total + functools.reduce(jnp.add, sides) * float(
                                near[REACH + lag]
                            )
                    column = ((part * group + m) * per_vox + x % per_vox) * plane
                    target = (x // per_vox) * parts + column // width
                    chunk, first = column % width // size, column % size
                    out = outs[chunk]
                    out[target, here, first : first + plane] = total.astype(jnp.bfloat16)


def smooth(images, n_vox, parts, chunks):
    subjects, maps, planes, plane = images.shape
    per_vox = planes // n_vox
    width = maps * per_vox * plane // parts
    size = width // chunks
    assert size % plane == 0
    group = max(1, min(maps, 256 // (SUBJ_TILE * planes)))
    step = 32
    order = jnp.asarray(row_order(group, planes))
    table = jnp.asarray(plane_kernel(plane))
    return pl.pallas_call(
        functools.partial(smooth_kernel, group, planes, per_vox, parts, width),
        out_shape=[jax.ShapeDtypeStruct((n_vox * parts, subjects, size), jnp.bfloat16)] * chunks,
        grid=(subjects // step,),
        in_specs=[
            pl.BlockSpec((step, maps * planes, plane), lambda i: (i, 0, 0)),
            pl.BlockSpec(order.shape, lambda i: (0, 0)),
            pl.BlockSpec(table.shape, lambda i: (0, 0)),
        ],
        out_specs=[pl.BlockSpec((n_vox * parts, step, size), lambda i: (0, i, 0))] * chunks,
        compiler_params=params(VMEM_MOST),
        name="smooth",
    )(images.reshape(subjects, maps * planes, plane), order, table)


def moments_kernel(snps, slots, me, blocks, others, joined, out):
    rows = []
    half = len(slots) // 2
    for source in range(len(slots)):
        offset = jnp.bitwise_xor(me[0], source)
        index = 0
        for place, slot in enumerate(slots):
            index = index + jnp.where(offset == place, slot, 0)
        place = lax.rem(index, half)
        rows.append(jnp.where(index < half, blocks[place], others[place]))
    rows = jnp.concatenate(rows, axis=1)
    joined[...] = rows
    across = (((1,), (1,)), ((), ()))
    out[...] = jnp.zeros(out.shape, jnp.float32)
    out[:DPAD, : snps + DPAD] = lax.dot_general(
        rows[snps:], rows, across, preferred_element_type=jnp.float32
    )
    wide = rows[:snps].astype(jnp.float32)
    wide = wide * wide
    high = wide.astype(jnp.bfloat16)
    low = (wide - high.astype(jnp.float32)).astype(jnp.bfloat16)
    ones = jnp.ones((8, rows.shape[1]), jnp.bfloat16)
    squares = lax.dot_general(ones, high, across, preferred_element_type=jnp.float32)
    squares = squares + lax.dot_general(ones, low, across, preferred_element_type=jnp.float32)
    out[DPAD:, :snps] = squares


def moments(blocks, others, slots, me):
    count, rows, subjects = blocks.shape
    snps = rows - DPAD
    spread = -(-rows // LANES) * LANES
    outs = (
        result((rows, 2 * count * subjects), blocks.dtype),
        pltpu.HBM((DPAD + 8, spread), jnp.float32),
    )
    kernel = functools.partial(moments_kernel, snps, slots)
    return call(kernel, "moments", outs, [me], [blocks, others], (), 2)


def eliminate(total, snps, design, guard):
    lane = lax.broadcasted_iota(jnp.int32, (DPAD, LANES), 1)
    row = lax.broadcasted_iota(jnp.int32, (DPAD, LANES), 0)
    shift = 32
    gram = total[:DPAD, snps : snps + LANES]
    work = jnp.where((row >= design) & (lane == row), 1.0, gram)
    work = jnp.where(lane == row + shift, 1.0, work)
    for k in range(design):
        pivot = work[k : k + 1, k : k + 1]
        line = work[k : k + 1, :] / pivot
        if guard:
            line = jnp.where(pivot > gram[k : k + 1, k : k + 1] * 2.0**-14, line, 0.0)
        work = jnp.where(row == k, line, work - work[:, k : k + 1] * line)
    solved = pltpu.roll(work, LANES - shift, 1)
    return jnp.where((lane < design) & (row < design), solved, 0.0)


def gene_fit(total, snps, design, guard):
    solved = eliminate(total, snps, design, guard)
    cross_gene = total[:DPAD, :snps]
    fitted = jnp.dot(
        solved[:, :DPAD], cross_gene, precision=HIGHEST, preferred_element_type=jnp.float32
    )
    square = total[DPAD : DPAD + 1, :snps]
    rss = square - jnp.sum(cross_gene * fitted, axis=0, keepdims=True)
    if guard:
        rss = jnp.maximum(rss, square * 2.0**-10) + 1e-30
    return solved, fitted, lax.rsqrt(rss)


def pair_kernel(snps, design, moment, coef, lines):
    _, fitted, scale = gene_fit(moment[...], snps, design, True)
    lines[...] = jnp.zeros(lines.shape, jnp.float32)
    lines[:DPAD, :] = fitted * scale
    lines[SCALE_LANE : SCALE_LANE + 1, :] = scale
    coef[...] = jnp.transpose(lines[...])


def pair_fit(moment, snps, design):
    kernel = functools.partial(pair_kernel, snps, design)
    scratch = [pltpu.VMEM((LANES, snps), jnp.float32)]
    return call(kernel, "pair_fit", result((snps, LANES), jnp.float32), [], [moment], scratch, 1)


def cohort_kernel(snps, design, *refs):
    parts, (coef, inverse, lines) = refs[:-3], refs[-3:]
    moment = [part[...] for part in parts]
    solved, fitted, scale = gene_fit(tree_sum(moment), snps, design, False)
    inverse[...] = solved
    lines[...] = jnp.zeros(lines.shape, jnp.float32)
    lines[:DPAD, :] = fitted * -scale
    lines[SCALE_LANE : SCALE_LANE + 1, :] = scale
    for j in range(len(parts)):
        _, fit, own_scale = gene_fit(moment[j], snps, design, True)
        lane = SCALE_LANE + 1 + j
        lines[lane : lane + 1, :] = scale / own_scale
        if j:
            lines[j * STRIDE : j * STRIDE + DPAD, :] = fit * scale
    coef[...] = jnp.transpose(lines[...])


def cohort_fit(parts, snps, design):
    kernel = functools.partial(cohort_kernel, snps, design)
    outs = (pltpu.HBM((snps, LANES), jnp.float32), pltpu.HBM((DPAD, LANES), jnp.float32))
    scratch = [pltpu.VMEM((LANES, snps), jnp.float32)]
    return call(kernel, "cohort_fit", outs, [], parts, scratch, len(parts))


def column_norm(sums, here):
    square = sums[SQUARE_ROW : SQUARE_ROW + 1, :]
    mean = jnp.sum(sums[:SITES, :], axis=0, keepdims=True) * (1.0 / here)
    spread = jnp.maximum(square - mean * mean * here, square * 2.0**-10)
    return jnp.sqrt(spread + 1e-30)


def sums_kernel(genes, columns, out):
    values = columns[...]
    wide = values.astype(jnp.float32)
    design = genes[genes.shape[0] - DPAD :, :]
    sums = jnp.dot(design, values, preferred_element_type=jnp.float32)
    square = jnp.sum(wide * wide, axis=0, keepdims=True)
    row = lax.broadcasted_iota(jnp.int32, sums.shape, 0)
    out[...] = jnp.where(row == SQUARE_ROW, square, sums)


def column_sums(genes, columns):
    outs = result((DPAD, columns.shape[1]), jnp.float32)
    return call(sums_kernel, "column_sums", outs, [], [genes, columns])


def products_kernel(here, offsets, far, near, genes, columns, coef, stats, *refs):
    outs, held = list(refs[:-1]), refs[-1]
    size = held.shape[0]
    panel = outs[0].shape[0]
    cross_image = stats[...]
    over = 1.0 / column_norm(cross_image, here)
    for j in offsets:
        block = pl.multiple_of(jnp.bitwise_xor(far[0], j) * size, size)
        held[...] = jnp.dot(
            genes[pl.ds(block, size), :], columns[...], preferred_element_type=jnp.float32
        )
        for k in range(size // panel):
            place = pl.multiple_of(jnp.bitwise_xor(near[0], k) * panel, panel)
            sums = held[pl.ds(place, panel), :]
            out = outs.pop(0)
            if j == 0 and k == 0:
                out[...] = sums
                continue
            line = coef[pl.ds(block + place, panel), :]
            fit = jnp.dot(
                line[:, :DPAD], cross_image, precision=HIGHEST, preferred_element_type=jnp.float32
            )
            out[...] = (line[:, SCALE_LANE : SCALE_LANE + 1] * sums - fit) * over


def products(genes, columns, coef, stats, far, near, offsets, size, count):
    here, width = columns.shape
    panel = size // count
    outs = [result((panel, width), jnp.float32) for _ in range(len(offsets) * count)]
    if 0 in offsets:
        outs[0] = pltpu.HBM((panel, width), jnp.float32)
    kernel = functools.partial(products_kernel, float(here), tuple(offsets))
    scratch = [pltpu.VMEM((size, width), jnp.float32)]
    arrays = [genes, columns, coef, stats]
    return call(kernel, "products", tuple(outs), [far, near], arrays, scratch)


def base_half(here, line, inverse, stats, extra, factors, stack):
    row = lax.broadcasted_iota(jnp.int32, stats[0].shape, 0)
    total = tree_sum(stats)
    known = row < SQUARE_ROW
    cross_image = jnp.where(known, total, 0.0)
    solved = jnp.dot(
        inverse[:, :DPAD], cross_image, precision=HIGHEST, preferred_element_type=jnp.float32
    )
    rss = total[SQUARE_ROW : SQUARE_ROW + 1, :] - jnp.sum(
        cross_image * solved, axis=0, keepdims=True
    )
    scale = lax.rsqrt(rss)
    stack[:DPAD, :] = cross_image
    factors[...] = jnp.zeros(factors.shape, jnp.float32)
    for j, stat in enumerate(stats):
        factors[j : j + 1, :] = column_norm(stat, here) * scale
        if j:
            stack[j * STRIDE : j * STRIDE + DPAD, :] = jnp.where(known, stat, 0.0)
    terms = jnp.dot(line, stack[...], precision=HIGHEST, preferred_element_type=jnp.float32)
    return (terms + extra) * scale


def base_kernel(here, place, own, coef, inverse, pair_coef, *refs):
    parts, (home, home_factors, away, away_factors, stack) = refs[:-5], refs[-5:]
    count = len(parts) // 2
    stack[...] = jnp.zeros(stack.shape, jnp.float32)
    panel = own.shape[0]
    rows = pl.ds(pl.multiple_of(place[0] * panel, panel), panel)
    line = coef[rows, :]
    stats = [part[...] for part in parts[:count]]
    extra = line[:, SCALE_LANE : SCALE_LANE + 1] * own[...]
    home[...] = base_half(here, line, inverse, stats, extra, home_factors, stack)
    stats = [part[...] for part in parts[count:]]
    row = lax.broadcasted_iota(jnp.int32, stats[0].shape, 0)
    extra = jnp.dot(
        pair_coef[rows, :][:, :DPAD],
        jnp.where(row < SQUARE_ROW, stats[0], 0.0),
        precision=HIGHEST,
        preferred_element_type=jnp.float32,
    )
    extra = line[:, SCALE_LANE + 1 : SCALE_LANE + 2] * extra
    away[...] = base_half(here, line, inverse, stats, extra, away_factors, stack)


def base_ratio(place, own, coef, inverse, pair_coef, parts, here):
    panel, width = own.shape
    outs = (result((panel, width), jnp.float32), result((8, width), jnp.float32)) * 2
    kernel = functools.partial(base_kernel, float(here))
    scratch = [pltpu.VMEM((LANES, width), jnp.float32)]
    arrays = [own, coef, inverse, pair_coef, *parts]
    return call(kernel, "base_ratio", outs, [place], arrays, scratch, len(arrays))


def permute_xor(value, axes, bits):
    size = lax.axis_size(axes)
    return lax.ppermute(value, axes, [(i, i ^ bits) for i in range(size)])


def on_device(images, genotypes, covariates, site_codes):
    subjects, maps, planes, plane = images.shape
    n_vox, n_far, n_near = (lax.axis_size(name) for name in ("vox", "far", "near"))
    vox, far, near = (lax.axis_index(name) for name in ("vox", "far", "near"))
    snps = genotypes.shape[1]
    design = SITES + covariates.shape[1]
    per_vox = planes // n_vox
    count = n_vox * n_near
    here = count * subjects

    def exchange(value):
        value = lax.all_to_all(value, ("vox", "near"), 0, 0, tiled=True)
        return value.reshape(here, value.shape[2])

    tall = tall_design(genotypes, covariates, site_codes)
    other = n_near
    offsets = [o for o in range(count) if not o & other]
    blocks = [tall] + [permute_xor(tall, ("vox", "near"), o) for o in offsets[1:]]
    (smoothed,) = smooth(images, n_vox, n_near, 1)
    smoothed, *blocks = lax.optimization_barrier((smoothed, *blocks))
    columns = exchange(smoothed)
    blocks = jnp.stack(blocks)
    others = permute_xor(blocks, ("vox", "near"), other)
    order = offsets + [o | other for o in offsets]
    slots = tuple(order.index(o) for o in range(count))
    genes, moment = moments(blocks, others, slots, (vox * n_near + near)[None])
    pair_coef = pair_fit(moment, snps, design)
    moment_parts = [moment] + [permute_xor(moment, "far", j) for j in range(1, n_far)]
    coef, inverse = cohort_fit(moment_parts, snps, design)
    columns, pair_coef, coef, inverse = lax.optimization_barrier(
        (columns, pair_coef, coef, inverse)
    )
    stats = column_sums(genes, columns)
    stat_parts = [stats] + [permute_xor(stats, "far", j) for j in range(1, n_far)]

    size = snps // n_far
    panel = size // n_near
    freedom = float(here * n_far - design - 1)
    line = ("far", "near")
    where = [far[None], near[None]]

    def shrink(pieces):
        return [piece.astype(jnp.float16) for piece in pieces]

    own, *sent = products(
        genes, columns, pair_coef, stats, *where, list(range(n_far)), size, n_near
    )
    away_parts = [permute_xor(stats, "near", 1)]
    sent, stat_parts, away_parts = lax.optimization_barrier(
        (shrink(sent), stat_parts, away_parts)
    )
    pieces = [None]
    pieces += [permute_xor(sent[k - 1], line, k) for k in range(1, n_far * n_near)]
    away_parts += [permute_xor(part, "near", 1) for part in stat_parts[1:]]
    place = far * n_near + near
    columns_scale = lax.dynamic_slice_in_dim(coef, place * panel, panel, 0)

    home, home_factors, away, away_factors = base_ratio(
        place[None], own, coef, inverse, pair_coef, stat_parts + away_parts, here
    )

    def t_of(ratio, factors, offset):
        for j in range(n_far):
            piece = pieces[j * n_near + offset]
            if piece is not None:
                weight = columns_scale[:, SCALE_LANE + 1 + j, None] * factors[None, j]
                ratio = ratio + piece.astype(jnp.float32) * weight
        return ratio * jnp.sqrt(freedom / (1.0 - ratio * ratio))

    home = t_of(home, home_factors, 0)
    away = t_of(away, away_factors, 1)
    both = jnp.where(near == 0, jnp.stack([home, away], 1), jnp.stack([away, home], 1))
    return both.reshape(panel, maps, per_vox, plane)


def solution(mesh):
    sizes = dict(mesh.shape)
    devices = mesh.devices.reshape(sizes["group"], sizes["vox"], sizes["snp"] // 2, 2)
    split = Mesh(devices, ("group", "vox", "far", "near"))
    owner = ("group", "vox", "far", "near")
    placed = (P(owner, None, None, None), P(owner, None), P(owner, None), P(owner))
    return jax.shard_map(
        on_device,
        mesh=split,
        in_specs=placed,
        out_specs=P(("group", "far", "near"), None, "vox", None),
        check_vma=False,
    )
```

```python
import functools

import jax
import jax.numpy as jnp
import ml_dtypes
import numpy as np
from jax import lax
from jax.experimental import pallas as pl
from jax.experimental.pallas import tpu as pltpu
from jax.sharding import Mesh
from jax.sharding import PartitionSpec as P

SY = 16
SZ = 16
SITES = 4
REACH = 2
DPAD = 24
LANES = 128
SUBJ_TILE = 16
HIGHEST = lax.Precision.HIGHEST
VMEM_MOST = 56 * 2**20
VMEM_BASE = 12 * 2**20
SQUARE_ROW = 20
WIDE = 2.0**8
SCALE_LANE = DPAD
STRIDE = 32


def kernel_table(length):
    position = np.arange(length)
    offset = (position[:, None] - position[None, :]).astype(np.float32)
    weights = np.where(np.abs(offset) <= REACH, np.exp(-offset * offset / np.float32(2.0)), np.float32(0.0))
    total = sum(np.exp(-(k * k) / 2.0) for k in range(-REACH, REACH + 1))
    return (weights / np.float32(total)).astype(np.float32)


def plane_kernel(plane):
    row, depth = kernel_table(SY), kernel_table(SZ)
    table = row[:, None, :, None] * depth[None, :, None, :]
    return table.reshape(plane, plane).astype(ml_dtypes.bfloat16)


def row_order(maps, planes):
    rows = SUBJ_TILE * maps * planes
    source = np.arange(rows).reshape(SUBJ_TILE, maps * planes).T.reshape(-1)
    return np.eye(rows, dtype=np.float32)[source].astype(ml_dtypes.bfloat16)


def tree_sum(terms):
    while len(terms) > 1:
        terms = [terms[i] + terms[i + 1] for i in range(0, len(terms), 2)]
    return terms[0]


RESIDENT = 3 * 2**20
IN_VMEM = pl.BlockSpec(memory_space=pltpu.VMEM)
IN_SMEM = pl.BlockSpec(memory_space=pltpu.SMEM)


def params(extra=0):
    return pltpu.CompilerParams(vmem_limit_bytes=min(VMEM_MOST, VMEM_BASE + extra))


def size_of(value):
    return int(np.prod(value.shape)) * jnp.dtype(value.dtype).itemsize


def small(shape, dtype):
    return int(np.prod(shape)) * jnp.dtype(dtype).itemsize <= RESIDENT


def keep(value):
    if small(value.shape, value.dtype):
        return pltpu.with_memory_space_constraint(value, pltpu.VMEM)
    return value


def result(shape, dtype):
    if small(shape, dtype):
        return pltpu.VMEM(shape, dtype)
    return jax.ShapeDtypeStruct(shape, dtype)


def call(kernel, name, outs, scalars, arrays, scratch=(), moved=0):
    many = isinstance(outs, tuple)
    sizes = [size_of(value) for value in (*arrays, *(outs if many else (outs,)))]
    extra = 3 * sum(size for size in sizes if size > RESIDENT)
    return pl.pallas_call(
        kernel,
        out_shape=outs,
        in_specs=[IN_SMEM] * len(scalars) + [IN_VMEM] * len(arrays),
        out_specs=(IN_VMEM,) * len(outs) if many else IN_VMEM,
        scratch_shapes=list(scratch),
        compiler_params=params(extra),
        name=name,
    )(*scalars, *arrays[:moved], *[keep(value) for value in arrays[moved:]])


def tall_kernel(genotypes, codes, covariates, out, rows):
    snps = genotypes.shape[1]
    out[:snps, :] = jnp.transpose(genotypes[...])
    count = covariates.shape[0]
    site = lax.broadcasted_iota(jnp.int32, (SITES, codes.shape[1]), 0)
    rows[...] = jnp.zeros(rows.shape, jnp.float32)
    rows[:SITES, :] = (site == codes[...]).astype(jnp.float32)
    rows[SITES : SITES + count, :] = covariates[...].astype(jnp.float32)
    out[snps:, :] = rows[...].astype(jnp.bfloat16)


def tall_design(genotypes, covariates, site_codes):
    subjects, snps = genotypes.shape
    return pl.pallas_call(
        tall_kernel,
        out_shape=result((snps + DPAD, subjects), jnp.bfloat16),
        in_specs=[IN_VMEM] * 3,
        out_specs=IN_VMEM,
        scratch_shapes=[pltpu.VMEM((DPAD, subjects), jnp.float32)],
        compiler_params=params(VMEM_MOST),
        name="tall_design",
    )(genotypes, site_codes[None, :], covariates.T)


def smooth_kernel(group, planes, per_vox, parts, width, images, order, table, *outs):
    plane = table.shape[0]
    size = width // len(outs)
    groups = images.shape[1] // (group * planes)
    near = kernel_table(2 * REACH + 1)[REACH]
    for tile in range(images.shape[0] // SUBJ_TILE):
        here = pl.ds(tile * SUBJ_TILE, SUBJ_TILE)
        for part in range(groups):
            rows = images[here, part * group * planes : (part + 1) * group * planes, :]
            rows = rows.reshape(SUBJ_TILE * group * planes, plane)
            rows = jnp.dot(order[...], rows, preferred_element_type=jnp.float32)
            inplane = jnp.dot(
                rows.astype(jnp.bfloat16), table[...], preferred_element_type=jnp.float32
            )
            for m in range(group):
                slabs = [
                    inplane[(m * planes + x) * SUBJ_TILE : (m * planes + x + 1) * SUBJ_TILE]
                    for x in range(planes)
                ]
                for x in range(planes):
                    total = slabs[x] * float(near[REACH])
                    for lag in range(1, REACH + 1):
                        sides = [slabs[k] for k in (x - lag, x + lag) if 0 <= k < planes]
                        if sides:
                            total = total + functools.reduce(jnp.add, sides) * float(
                                near[REACH + lag]
                            )
                    column = ((part * group + m) * per_vox + x % per_vox) * plane
                    target = (x // per_vox) * parts + column // width
                    chunk, first = column % width // size, column % size
                    out = outs[chunk]
                    out[target, here, first : first + plane] = total.astype(jnp.bfloat16)


def smooth(images, n_vox, parts, chunks):
    subjects, maps, planes, plane = images.shape
    per_vox = planes // n_vox
    width = maps * per_vox * plane // parts
    size = width // chunks
    assert size % plane == 0
    group = max(1, min(maps, 256 // (SUBJ_TILE * planes)))
    step = 32
    order = jnp.asarray(row_order(group, planes))
    table = jnp.asarray(plane_kernel(plane))
    return pl.pallas_call(
        functools.partial(smooth_kernel, group, planes, per_vox, parts, width),
        out_shape=[jax.ShapeDtypeStruct((n_vox * parts, subjects, size), jnp.bfloat16)] * chunks,
        grid=(subjects // step,),
        in_specs=[
            pl.BlockSpec((step, maps * planes, plane), lambda i: (i, 0, 0)),
            pl.BlockSpec(order.shape, lambda i: (0, 0)),
            pl.BlockSpec(table.shape, lambda i: (0, 0)),
        ],
        out_specs=[pl.BlockSpec((n_vox * parts, step, size), lambda i: (0, i, 0))] * chunks,
        compiler_params=params(VMEM_MOST),
        name="smooth",
    )(images.reshape(subjects, maps * planes, plane), order, table)


def moments_kernel(snps, slots, me, blocks, others, joined, out):
    rows = []
    half = len(slots) // 2
    for source in range(len(slots)):
        offset = jnp.bitwise_xor(me[0], source)
        index = 0
        for place, slot in enumerate(slots):
            index = index + jnp.where(offset == place, slot, 0)
        place = lax.rem(index, half)
        rows.append(jnp.where(index < half, blocks[place], others[place]))
    rows = jnp.concatenate(rows, axis=1)
    joined[...] = rows
    across = (((1,), (1,)), ((), ()))
    out[...] = jnp.zeros(out.shape, jnp.float32)
    out[:DPAD, : snps + DPAD] = lax.dot_general(
        rows[snps:], rows, across, preferred_element_type=jnp.float32
    )
    wide = rows[:snps].astype(jnp.float32)
    wide = wide * wide
    high = wide.astype(jnp.bfloat16)
    low = (wide - high.astype(jnp.float32)).astype(jnp.bfloat16)
    ones = jnp.ones((8, rows.shape[1]), jnp.bfloat16)
    squares = lax.dot_general(ones, high, across, preferred_element_type=jnp.float32)
    squares = squares + lax.dot_general(ones, low, across, preferred_element_type=jnp.float32)
    out[DPAD:, :snps] = squares


def moments(blocks, others, slots, me):
    count, rows, subjects = blocks.shape
    snps = rows - DPAD
    spread = -(-rows // LANES) * LANES
    outs = (
        result((rows, 2 * count * subjects), blocks.dtype),
        pltpu.HBM((DPAD + 8, spread), jnp.float32),
    )
    kernel = functools.partial(moments_kernel, snps, slots)
    return call(kernel, "moments", outs, [me], [blocks, others], (), 2)


def eliminate(total, snps, design, guard):
    lane = lax.broadcasted_iota(jnp.int32, (DPAD, LANES), 1)
    row = lax.broadcasted_iota(jnp.int32, (DPAD, LANES), 0)
    shift = 32
    gram = total[:DPAD, snps : snps + LANES]
    work = jnp.where((row >= design) & (lane == row), 1.0, gram)
    work = jnp.where(lane == row + shift, 1.0, work)
    for k in range(design):
        pivot = work[k : k + 1, k : k + 1]
        line = work[k : k + 1, :] / pivot
        if guard:
            line = jnp.where(pivot > gram[k : k + 1, k : k + 1] * 2.0**-14, line, 0.0)
        work = jnp.where(row == k, line, work - work[:, k : k + 1] * line)
    solved = pltpu.roll(work, LANES - shift, 1)
    return jnp.where((lane < design) & (row < design), solved, 0.0)


def gene_fit(total, snps, design, guard):
    solved = eliminate(total, snps, design, guard)
    cross_gene = total[:DPAD, :snps]
    fitted = jnp.dot(
        solved[:, :DPAD], cross_gene, precision=HIGHEST, preferred_element_type=jnp.float32
    )
    square = total[DPAD : DPAD + 1, :snps]
    rss = square - jnp.sum(cross_gene * fitted, axis=0, keepdims=True)
    if guard:
        rss = jnp.maximum(rss, square * 2.0**-10) + 1e-30
    return solved, fitted, lax.rsqrt(rss)


def pair_kernel(snps, design, moment, coef, lines):
    _, fitted, scale = gene_fit(moment[...], snps, design, True)
    lines[...] = jnp.zeros(lines.shape, jnp.float32)
    lines[:DPAD, :] = fitted * scale
    lines[SCALE_LANE : SCALE_LANE + 1, :] = scale
    coef[...] = jnp.transpose(lines[...])


def pair_fit(moment, snps, design):
    kernel = functools.partial(pair_kernel, snps, design)
    scratch = [pltpu.VMEM((LANES, snps), jnp.float32)]
    return call(kernel, "pair_fit", result((snps, LANES), jnp.float32), [], [moment], scratch, 1)


def cohort_kernel(snps, design, *refs):
    parts, (coef, inverse, lines) = refs[:-3], refs[-3:]
    moment = [part[...] for part in parts]
    solved, fitted, scale = gene_fit(tree_sum(moment), snps, design, False)
    inverse[...] = solved
    lines[...] = jnp.zeros(lines.shape, jnp.float32)
    lines[:DPAD, :] = fitted * -scale
    lines[SCALE_LANE : SCALE_LANE + 1, :] = scale
    for j in range(len(parts)):
        _, fit, own_scale = gene_fit(moment[j], snps, design, True)
        lane = SCALE_LANE + 1 + j
        lines[lane : lane + 1, :] = scale / own_scale
        if j:
            lines[j * STRIDE : j * STRIDE + DPAD, :] = fit * scale
    coef[...] = jnp.transpose(lines[...])


def cohort_fit(parts, snps, design):
    kernel = functools.partial(cohort_kernel, snps, design)
    outs = (pltpu.HBM((snps, LANES), jnp.float32), pltpu.HBM((DPAD, LANES), jnp.float32))
    scratch = [pltpu.VMEM((LANES, snps), jnp.float32)]
    return call(kernel, "cohort_fit", outs, [], parts, scratch, len(parts))


def column_norm(sums, here):
    square = sums[SQUARE_ROW : SQUARE_ROW + 1, :]
    mean = jnp.sum(sums[:SITES, :], axis=0, keepdims=True) * (1.0 / here)
    spread = jnp.maximum(square - mean * mean * here, square * 2.0**-10)
    return jnp.sqrt(spread + 1e-30)


def sums_kernel(genes, columns, out):
    values = columns[...]
    wide = values.astype(jnp.float32)
    design = genes[genes.shape[0] - DPAD :, :]
    sums = jnp.dot(design, values, preferred_element_type=jnp.float32)
    square = jnp.sum(wide * wide, axis=0, keepdims=True)
    row = lax.broadcasted_iota(jnp.int32, sums.shape, 0)
    out[...] = jnp.where(row == SQUARE_ROW, square, sums)


def column_sums(genes, columns):
    outs = result((DPAD, columns.shape[1]), jnp.float32)
    return call(sums_kernel, "column_sums", outs, [], [genes, columns])


def far_kernel(here, count, far, near, genes, columns, coef, stats, *refs):
    outs, held = list(refs[:-1]), refs[-1]
    size = held.shape[0]
    panel = outs[0].shape[0]
    cross_image = stats[...]
    over = 1.0 / column_norm(cross_image, here)
    for j in range(1, count):
        block = pl.multiple_of(jnp.bitwise_xor(far[0], j) * size, size)
        held[...] = jnp.dot(
            genes[pl.ds(block, size), :], columns[...], preferred_element_type=jnp.float32
        )
        for k in range(size // panel):
            place = pl.multiple_of(jnp.bitwise_xor(near[0], k) * panel, panel)
            line = coef[pl.ds(block + place, panel), :]
            fit = jnp.dot(
                line[:, :DPAD], cross_image, precision=HIGHEST, preferred_element_type=jnp.float32
            )
            scale = line[:, SCALE_LANE : SCALE_LANE + 1]
            outs.pop(0)[...] = (scale * held[pl.ds(place, panel), :] - fit) * over


def far_products(genes, columns, coef, stats, far, near, n_far, n_near):
    here, width = columns.shape
    size = (genes.shape[0] - DPAD) // n_far
    outs = (result((size // n_near, width), jnp.float32),) * ((n_far - 1) * n_near)
    kernel = functools.partial(far_kernel, float(here), n_far)
    scratch = [pltpu.VMEM((size, width), jnp.float32)]
    return call(kernel, "far_products", outs, [far, near], [genes, columns, coef, stats], scratch)


def base_kernel(here, count, far, near, genes, columns, coef, inverse, *refs):
    parts, (home, away, factors, stack, held) = refs[:-5], refs[-5:]
    stats = [part[...] for part in parts]
    row = lax.broadcasted_iota(jnp.int32, stats[0].shape, 0)
    total = tree_sum(stats)
    known = row < SQUARE_ROW
    cross_image = jnp.where(known, total, 0.0)
    solved = jnp.dot(
        inverse[:, :DPAD], cross_image, precision=HIGHEST, preferred_element_type=jnp.float32
    )
    rss = total[SQUARE_ROW : SQUARE_ROW + 1, :] - jnp.sum(
        cross_image * solved, axis=0, keepdims=True
    )
    scale = lax.rsqrt(rss)
    stack[...] = jnp.zeros(stack.shape, jnp.float32)
    stack[:DPAD, :] = cross_image
    factors[...] = jnp.zeros(factors.shape, jnp.float32)
    for j in range(1, len(stats)):
        factors[j : j + 1, :] = column_norm(stats[j], here) * scale
        stack[j * STRIDE : j * STRIDE + DPAD, :] = jnp.where(known, stats[j], 0.0)
    size = held.shape[0]
    block = pl.ds(pl.multiple_of(far[0] * size, size), size)
    line = coef[block, :]
    sums = jnp.dot(genes[block, :], columns[...], preferred_element_type=jnp.float32)
    terms = jnp.dot(line, stack[...], precision=HIGHEST, preferred_element_type=jnp.float32)
    held[...] = (line[:, SCALE_LANE : SCALE_LANE + 1] * sums + terms) * scale
    panel = size // count
    for k, out in enumerate((home, away)):
        place = pl.multiple_of(jnp.bitwise_xor(near[0], k) * panel, panel)
        out[...] = held[pl.ds(place, panel), :] * (WIDE if k else 1.0)


def base_ratio(genes, columns, coef, inverse, parts, far, near, n_far, n_near):
    here, width = columns.shape
    size = (genes.shape[0] - DPAD) // n_far
    outs = (result((size // n_near, width), jnp.float32),) * 2
    outs += (result((8, width), jnp.float32),)
    kernel = functools.partial(base_kernel, float(here), n_near)
    scratch = [pltpu.VMEM((LANES, width), jnp.float32), pltpu.VMEM((size, width), jnp.float32)]
    arrays = [coef, inverse, genes, columns, *parts]
    kernel = functools.partial(reorder, kernel)
    return call(kernel, "base_ratio", outs, [far, near], arrays, scratch, 2)


def reorder(kernel, far, near, coef, inverse, genes, columns, *refs):
    kernel(far, near, genes, columns, coef, inverse, *refs)


def permute_xor(value, axes, bits):
    size = lax.axis_size(axes)
    return lax.ppermute(value, axes, [(i, i ^ bits) for i in range(size)])


def on_device(images, genotypes, covariates, site_codes):
    subjects, maps, planes, plane = images.shape
    n_vox, n_far, n_near = (lax.axis_size(name) for name in ("vox", "far", "near"))
    vox, far, near = (lax.axis_index(name) for name in ("vox", "far", "near"))
    snps = genotypes.shape[1]
    design = SITES + covariates.shape[1]
    per_vox = planes // n_vox
    count = n_vox * n_near
    here = count * subjects

    def exchange(value):
        value = lax.all_to_all(value, ("vox", "near"), 0, 0, tiled=True)
        return value.reshape(here, value.shape[2])

    tall = tall_design(genotypes, covariates, site_codes)
    other = n_near
    offsets = [o for o in range(count) if not o & other]
    blocks = [tall] + [permute_xor(tall, ("vox", "near"), o) for o in offsets[1:]]
    (smoothed,) = smooth(images, n_vox, n_near, 1)
    smoothed, *blocks = lax.optimization_barrier((smoothed, *blocks))
    columns = exchange(smoothed)
    blocks = jnp.stack(blocks)
    others = permute_xor(blocks, ("vox", "near"), other)
    order = offsets + [o | other for o in offsets]
    slots = tuple(order.index(o) for o in range(count))
    genes, moment = moments(blocks, others, slots, (vox * n_near + near)[None])
    pair_coef = pair_fit(moment, snps, design)
    moment_parts = [moment] + [permute_xor(moment, "far", j) for j in range(1, n_far)]
    coef, inverse = cohort_fit(moment_parts, snps, design)
    columns, pair_coef, coef, inverse = lax.optimization_barrier(
        (columns, pair_coef, coef, inverse)
    )
    stats = column_sums(genes, columns)
    stat_parts = [stats] + [permute_xor(stats, "far", j) for j in range(1, n_far)]

    size = snps // n_far
    panel = size // n_near
    freedom = float(here * n_far - design - 1)
    line = ("far", "near")
    where = [far[None], near[None], n_far, n_near]
    sent = far_products(genes, columns, pair_coef, stats, *where)
    sent = [piece.astype(jnp.float16) for piece in sent]
    sent, stat_parts = lax.optimization_barrier((sent, stat_parts))
    pieces = {
        k: permute_xor(sent[k - n_near], line, k) for k in range(n_near, n_far * n_near)
    }
    home, away, factors = base_ratio(genes, columns, coef, inverse, stat_parts, *where)
    away = permute_xor(away.astype(jnp.float16), "near", 1)
    away = away.astype(jnp.float32) * (1.0 / WIDE)
    away_factors = permute_xor(factors, "near", 1)
    place = far * n_near + near
    columns_scale = lax.dynamic_slice_in_dim(coef, place * panel, panel, 0)

    def t_of(ratio, factors, offset):
        for j in range(1, n_far):
            weight = columns_scale[:, SCALE_LANE + 1 + j, None] * factors[None, j]
            ratio = ratio + pieces[j * n_near + offset].astype(jnp.float32) * weight
        return ratio * jnp.sqrt(freedom / (1.0 - ratio * ratio))

    home = t_of(home, factors, 0)
    away = t_of(away, away_factors, 1)
    both = jnp.where(near == 0, jnp.stack([home, away], 1), jnp.stack([away, home], 1))
    return both.reshape(panel, maps, per_vox, plane)


def solution(mesh):
    sizes = dict(mesh.shape)
    devices = mesh.devices.reshape(sizes["group"], sizes["vox"], sizes["snp"] // 2, 2)
    split = Mesh(devices, ("group", "vox", "far", "near"))
    owner = ("group", "vox", "far", "near")
    placed = (P(owner, None, None, None), P(owner, None), P(owner, None), P(owner))
    return jax.shard_map(
        on_device,
        mesh=split,
        in_specs=placed,
        out_specs=P(("group", "far", "near"), None, "vox", None),
        check_vma=False,
    )
```

```python
import functools

import jax
import jax.numpy as jnp
import ml_dtypes
import numpy as np
from jax import lax
from jax.experimental import pallas as pl
from jax.experimental.pallas import tpu as pltpu
from jax.sharding import Mesh
from jax.sharding import PartitionSpec as P

SY = 16
SZ = 16
SITES = 4
REACH = 2
DPAD = 24
LANES = 128
SUBJ_TILE = 16
HIGHEST = lax.Precision.HIGHEST
VMEM_MOST = 56 * 2**20
VMEM_BASE = 12 * 2**20
SQUARE_ROW = 20
WIDE = 2.0**8
SCALE_LANE = DPAD
STRIDE = 32


def kernel_table(length):
    position = np.arange(length)
    offset = (position[:, None] - position[None, :]).astype(np.float32)
    weights = np.where(np.abs(offset) <= REACH, np.exp(-offset * offset / np.float32(2.0)), np.float32(0.0))
    total = sum(np.exp(-(k * k) / 2.0) for k in range(-REACH, REACH + 1))
    return (weights / np.float32(total)).astype(np.float32)


def plane_kernel(plane):
    row, depth = kernel_table(SY), kernel_table(SZ)
    table = row[:, None, :, None] * depth[None, :, None, :]
    return table.reshape(plane, plane).astype(ml_dtypes.bfloat16)


def row_order(maps, planes):
    rows = SUBJ_TILE * maps * planes
    source = np.arange(rows).reshape(SUBJ_TILE, maps * planes).T.reshape(-1)
    return np.eye(rows, dtype=np.float32)[source].astype(ml_dtypes.bfloat16)


def tree_sum(terms):
    while len(terms) > 1:
        terms = [terms[i] + terms[i + 1] for i in range(0, len(terms), 2)]
    return terms[0]


RESIDENT = 3 * 2**20
IN_VMEM = pl.BlockSpec(memory_space=pltpu.VMEM)
IN_SMEM = pl.BlockSpec(memory_space=pltpu.SMEM)


def params(extra=0):
    return pltpu.CompilerParams(vmem_limit_bytes=min(VMEM_MOST, VMEM_BASE + extra))


def size_of(value):
    return int(np.prod(value.shape)) * jnp.dtype(value.dtype).itemsize


def small(shape, dtype):
    return int(np.prod(shape)) * jnp.dtype(dtype).itemsize <= RESIDENT


def keep(value):
    if small(value.shape, value.dtype):
        return pltpu.with_memory_space_constraint(value, pltpu.VMEM)
    return value


def result(shape, dtype):
    if small(shape, dtype):
        return pltpu.VMEM(shape, dtype)
    return jax.ShapeDtypeStruct(shape, dtype)


def call(kernel, name, outs, scalars, arrays, scratch=(), moved=0):
    many = isinstance(outs, tuple)
    sizes = [size_of(value) for value in (*arrays, *(outs if many else (outs,)))]
    extra = 3 * sum(size for size in sizes if size > RESIDENT)
    return pl.pallas_call(
        kernel,
        out_shape=outs,
        in_specs=[IN_SMEM] * len(scalars) + [IN_VMEM] * len(arrays),
        out_specs=(IN_VMEM,) * len(outs) if many else IN_VMEM,
        scratch_shapes=list(scratch),
        compiler_params=params(extra),
        name=name,
    )(*scalars, *arrays[:moved], *[keep(value) for value in arrays[moved:]])


def tall_kernel(genotypes, codes, covariates, out, rows):
    snps = genotypes.shape[1]
    out[:snps, :] = jnp.transpose(genotypes[...])
    count = covariates.shape[0]
    site = lax.broadcasted_iota(jnp.int32, (SITES, codes.shape[1]), 0)
    rows[...] = jnp.zeros(rows.shape, jnp.float32)
    rows[:SITES, :] = (site == codes[...]).astype(jnp.float32)
    rows[SITES : SITES + count, :] = covariates[...].astype(jnp.float32)
    out[snps:, :] = rows[...].astype(jnp.bfloat16)


def tall_design(genotypes, covariates, site_codes):
    subjects, snps = genotypes.shape
    return pl.pallas_call(
        tall_kernel,
        out_shape=result((snps + DPAD, subjects), jnp.bfloat16),
        in_specs=[IN_VMEM] * 3,
        out_specs=IN_VMEM,
        scratch_shapes=[pltpu.VMEM((DPAD, subjects), jnp.float32)],
        compiler_params=params(VMEM_MOST),
        name="tall_design",
    )(genotypes, site_codes[None, :], covariates.T)


def smooth_kernel(group, planes, per_vox, parts, width, images, order, table, *outs):
    plane = table.shape[0]
    size = width // len(outs)
    groups = images.shape[1] // (group * planes)
    near = kernel_table(2 * REACH + 1)[REACH]
    for tile in range(images.shape[0] // SUBJ_TILE):
        here = pl.ds(tile * SUBJ_TILE, SUBJ_TILE)
        for part in range(groups):
            rows = images[here, part * group * planes : (part + 1) * group * planes, :]
            rows = rows.reshape(SUBJ_TILE * group * planes, plane)
            rows = jnp.dot(order[...], rows, preferred_element_type=jnp.float32)
            inplane = jnp.dot(
                rows.astype(jnp.bfloat16), table[...], preferred_element_type=jnp.float32
            )
            for m in range(group):
                slabs = [
                    inplane[(m * planes + x) * SUBJ_TILE : (m * planes + x + 1) * SUBJ_TILE]
                    for x in range(planes)
                ]
                for x in range(planes):
                    total = slabs[x] * float(near[REACH])
                    for lag in range(1, REACH + 1):
                        sides = [slabs[k] for k in (x - lag, x + lag) if 0 <= k < planes]
                        if sides:
                            total = total + functools.reduce(jnp.add, sides) * float(
                                near[REACH + lag]
                            )
                    column = ((part * group + m) * per_vox + x % per_vox) * plane
                    target = (x // per_vox) * parts + column // width
                    chunk, first = column % width // size, column % size
                    out = outs[chunk]
                    out[target, here, first : first + plane] = total.astype(jnp.bfloat16)


def smooth(images, n_vox, parts, chunks):
    subjects, maps, planes, plane = images.shape
    per_vox = planes // n_vox
    width = maps * per_vox * plane // parts
    size = width // chunks
    assert size % plane == 0
    group = max(1, min(maps, 256 // (SUBJ_TILE * planes)))
    step = min(subjects, 64)
    order = jnp.asarray(row_order(group, planes))
    table = jnp.asarray(plane_kernel(plane))
    return pl.pallas_call(
        functools.partial(smooth_kernel, group, planes, per_vox, parts, width),
        out_shape=[jax.ShapeDtypeStruct((n_vox * parts, subjects, size), jnp.bfloat16)] * chunks,
        grid=(subjects // step,),
        in_specs=[
            pl.BlockSpec((step, maps * planes, plane), lambda i: (i, 0, 0)),
            pl.BlockSpec(order.shape, lambda i: (0, 0)),
            pl.BlockSpec(table.shape, lambda i: (0, 0)),
        ],
        out_specs=[pl.BlockSpec((n_vox * parts, step, size), lambda i: (0, i, 0))] * chunks,
        compiler_params=params(VMEM_MOST),
        name="smooth",
    )(images.reshape(subjects, maps * planes, plane), order, table)


def moments_kernel(snps, slots, me, blocks, others, joined, out):
    rows = []
    half = len(slots) // 2
    for source in range(len(slots)):
        offset = jnp.bitwise_xor(me[0], source)
        index = 0
        for place, slot in enumerate(slots):
            index = index + jnp.where(offset == place, slot, 0)
        place = lax.rem(index, half)
        rows.append(jnp.where(index < half, blocks[place], others[place]))
    rows = jnp.concatenate(rows, axis=1)
    joined[...] = rows
    across = (((1,), (1,)), ((), ()))
    out[...] = jnp.zeros(out.shape, jnp.float32)
    out[:DPAD, : snps + DPAD] = lax.dot_general(
        rows[snps:], rows, across, preferred_element_type=jnp.float32
    )
    wide = rows[:snps].astype(jnp.float32)
    wide = wide * wide
    high = wide.astype(jnp.bfloat16)
    low = (wide - high.astype(jnp.float32)).astype(jnp.bfloat16)
    ones = jnp.ones((8, rows.shape[1]), jnp.bfloat16)
    squares = lax.dot_general(ones, high, across, preferred_element_type=jnp.float32)
    squares = squares + lax.dot_general(ones, low, across, preferred_element_type=jnp.float32)
    out[DPAD:, :snps] = squares


def moments(blocks, others, slots, me):
    count, rows, subjects = blocks.shape
    snps = rows - DPAD
    spread = -(-rows // LANES) * LANES
    outs = (
        result((rows, 2 * count * subjects), blocks.dtype),
        pltpu.HBM((DPAD + 8, spread), jnp.float32),
    )
    kernel = functools.partial(moments_kernel, snps, slots)
    return call(kernel, "moments", outs, [me], [blocks, others], (), 2)


def eliminate(total, snps, design, guard):
    lane = lax.broadcasted_iota(jnp.int32, (DPAD, LANES), 1)
    row = lax.broadcasted_iota(jnp.int32, (DPAD, LANES), 0)
    shift = 32
    gram = total[:DPAD, snps : snps + LANES]
    work = jnp.where((row >= design) & (lane == row), 1.0, gram)
    work = jnp.where(lane == row + shift, 1.0, work)
    for k in range(design):
        pivot = work[k : k + 1, k : k + 1]
        line = work[k : k + 1, :] / pivot
        if guard:
            line = jnp.where(pivot > gram[k : k + 1, k : k + 1] * 2.0**-14, line, 0.0)
        work = jnp.where(row == k, line, work - work[:, k : k + 1] * line)
    solved = pltpu.roll(work, LANES - shift, 1)
    return jnp.where((lane < design) & (row < design), solved, 0.0)


def gene_fit(total, snps, design, guard):
    solved = eliminate(total, snps, design, guard)
    cross_gene = total[:DPAD, :snps]
    fitted = jnp.dot(
        solved[:, :DPAD], cross_gene, precision=HIGHEST, preferred_element_type=jnp.float32
    )
    square = total[DPAD : DPAD + 1, :snps]
    rss = square - jnp.sum(cross_gene * fitted, axis=0, keepdims=True)
    if guard:
        rss = jnp.maximum(rss, square * 2.0**-10) + 1e-30
    return solved, fitted, lax.rsqrt(rss)


def pair_kernel(snps, design, moment, coef, lines):
    _, fitted, scale = gene_fit(moment[...], snps, design, True)
    lines[...] = jnp.zeros(lines.shape, jnp.float32)
    lines[:DPAD, :] = fitted * scale
    lines[SCALE_LANE : SCALE_LANE + 1, :] = scale
    coef[...] = jnp.transpose(lines[...])


def pair_fit(moment, snps, design):
    kernel = functools.partial(pair_kernel, snps, design)
    scratch = [pltpu.VMEM((LANES, snps), jnp.float32)]
    return call(kernel, "pair_fit", result((snps, LANES), jnp.float32), [], [moment], scratch, 1)


def cohort_kernel(snps, design, *refs):
    parts, (coef, inverse, lines) = refs[:-3], refs[-3:]
    moment = [part[...] for part in parts]
    solved, fitted, scale = gene_fit(tree_sum(moment), snps, design, False)
    inverse[...] = solved
    lines[...] = jnp.zeros(lines.shape, jnp.float32)
    lines[:DPAD, :] = fitted * -scale
    lines[SCALE_LANE : SCALE_LANE + 1, :] = scale
    for j in range(len(parts)):
        _, fit, own_scale = gene_fit(moment[j], snps, design, True)
        lane = SCALE_LANE + 1 + j
        lines[lane : lane + 1, :] = scale / own_scale
        if j:
            lines[j * STRIDE : j * STRIDE + DPAD, :] = fit * scale
    coef[...] = jnp.transpose(lines[...])


def cohort_fit(parts, snps, design):
    kernel = functools.partial(cohort_kernel, snps, design)
    outs = (pltpu.HBM((snps, LANES), jnp.float32), pltpu.HBM((DPAD, LANES), jnp.float32))
    scratch = [pltpu.VMEM((LANES, snps), jnp.float32)]
    return call(kernel, "cohort_fit", outs, [], parts, scratch, len(parts))


def column_norm(sums, here):
    square = sums[SQUARE_ROW : SQUARE_ROW + 1, :]
    mean = jnp.sum(sums[:SITES, :], axis=0, keepdims=True) * (1.0 / here)
    spread = jnp.maximum(square - mean * mean * here, square * 2.0**-10)
    return jnp.sqrt(spread + 1e-30)


def sums_kernel(genes, columns, out):
    values = columns[...]
    wide = values.astype(jnp.float32)
    design = genes[genes.shape[0] - DPAD :, :]
    sums = jnp.dot(design, values, preferred_element_type=jnp.float32)
    square = jnp.sum(wide * wide, axis=0, keepdims=True)
    row = lax.broadcasted_iota(jnp.int32, sums.shape, 0)
    out[...] = jnp.where(row == SQUARE_ROW, square, sums)


def column_sums(genes, columns):
    outs = result((DPAD, columns.shape[1]), jnp.float32)
    return call(sums_kernel, "column_sums", outs, [], [genes, columns])


def far_kernel(here, count, far, near, genes, columns, coef, stats, *refs):
    outs, held = list(refs[:-1]), refs[-1]
    size = held.shape[0]
    panel = outs[0].shape[0]
    cross_image = stats[...]
    over = 1.0 / column_norm(cross_image, here)
    for j in range(1, count):
        block = pl.multiple_of(jnp.bitwise_xor(far[0], j) * size, size)
        held[...] = jnp.dot(
            genes[pl.ds(block, size), :], columns[...], preferred_element_type=jnp.float32
        )
        for k in range(size // panel):
            place = pl.multiple_of(jnp.bitwise_xor(near[0], k) * panel, panel)
            line = coef[pl.ds(block + place, panel), :]
            fit = jnp.dot(
                line[:, :DPAD], cross_image, precision=HIGHEST, preferred_element_type=jnp.float32
            )
            scale = line[:, SCALE_LANE : SCALE_LANE + 1]
            outs.pop(0)[...] = (scale * held[pl.ds(place, panel), :] - fit) * over


def far_products(genes, columns, coef, stats, far, near, n_far, n_near):
    here, width = columns.shape
    size = (genes.shape[0] - DPAD) // n_far
    outs = (result((size // n_near, width), jnp.float32),) * ((n_far - 1) * n_near)
    kernel = functools.partial(far_kernel, float(here), n_far)
    scratch = [pltpu.VMEM((size, width), jnp.float32)]
    return call(kernel, "far_products", outs, [far, near], [genes, columns, coef, stats], scratch)


def base_kernel(here, count, far, near, genes, columns, coef, inverse, *refs):
    parts, (home, away, factors, stack, held) = refs[:-5], refs[-5:]
    stats = [part[...] for part in parts]
    row = lax.broadcasted_iota(jnp.int32, stats[0].shape, 0)
    total = tree_sum(stats)
    known = row < SQUARE_ROW
    cross_image = jnp.where(known, total, 0.0)
    solved = jnp.dot(
        inverse[:, :DPAD], cross_image, precision=HIGHEST, preferred_element_type=jnp.float32
    )
    rss = total[SQUARE_ROW : SQUARE_ROW + 1, :] - jnp.sum(
        cross_image * solved, axis=0, keepdims=True
    )
    scale = lax.rsqrt(rss)
    stack[...] = jnp.zeros(stack.shape, jnp.float32)
    stack[:DPAD, :] = cross_image
    factors[...] = jnp.zeros(factors.shape, jnp.float32)
    for j in range(1, len(stats)):
        factors[j : j + 1, :] = column_norm(stats[j], here) * scale
        stack[j * STRIDE : j * STRIDE + DPAD, :] = jnp.where(known, stats[j], 0.0)
    size = held.shape[0]
    block = pl.ds(pl.multiple_of(far[0] * size, size), size)
    line = coef[block, :]
    sums = jnp.dot(genes[block, :], columns[...], preferred_element_type=jnp.float32)
    terms = jnp.dot(line, stack[...], precision=HIGHEST, preferred_element_type=jnp.float32)
    held[...] = (line[:, SCALE_LANE : SCALE_LANE + 1] * sums + terms) * scale
    panel = size // count
    for k, out in enumerate((home, away)):
        place = pl.multiple_of(jnp.bitwise_xor(near[0], k) * panel, panel)
        out[...] = held[pl.ds(place, panel), :] * (WIDE if k else 1.0)


def base_ratio(genes, columns, coef, inverse, parts, far, near, n_far, n_near):
    here, width = columns.shape
    size = (genes.shape[0] - DPAD) // n_far
    outs = (result((size // n_near, width), jnp.float32),) * 2
    outs += (result((8, width), jnp.float32),)
    kernel = functools.partial(base_kernel, float(here), n_near)
    scratch = [pltpu.VMEM((LANES, width), jnp.float32), pltpu.VMEM((size, width), jnp.float32)]
    arrays = [coef, inverse, genes, columns, *parts]
    kernel = functools.partial(reorder, kernel)
    return call(kernel, "base_ratio", outs, [far, near], arrays, scratch, 2)


def reorder(kernel, far, near, coef, inverse, genes, columns, *refs):
    kernel(far, near, genes, columns, coef, inverse, *refs)


def permute_xor(value, axes, bits):
    size = lax.axis_size(axes)
    return lax.ppermute(value, axes, [(i, i ^ bits) for i in range(size)])


def on_device(images, genotypes, covariates, site_codes):
    subjects, maps, planes, plane = images.shape
    n_vox, n_far, n_near = (lax.axis_size(name) for name in ("vox", "far", "near"))
    vox, far, near = (lax.axis_index(name) for name in ("vox", "far", "near"))
    snps = genotypes.shape[1]
    design = SITES + covariates.shape[1]
    per_vox = planes // n_vox
    count = n_vox * n_near
    here = count * subjects

    def exchange(value):
        value = lax.all_to_all(value, ("vox", "near"), 0, 0, tiled=True)
        return value.reshape(here, value.shape[2])

    tall = tall_design(genotypes, covariates, site_codes)
    other = n_near
    offsets = [o for o in range(count) if not o & other]
    blocks = [tall] + [permute_xor(tall, ("vox", "near"), o) for o in offsets[1:]]
    (smoothed,) = smooth(images, n_vox, n_near, 1)
    smoothed, *blocks = lax.optimization_barrier((smoothed, *blocks))
    columns = exchange(smoothed)
    blocks = jnp.stack(blocks)
    others = permute_xor(blocks, ("vox", "near"), other)
    order = offsets + [o | other for o in offsets]
    slots = tuple(order.index(o) for o in range(count))
    genes, moment = moments(blocks, others, slots, (vox * n_near + near)[None])
    pair_coef = pair_fit(moment, snps, design)
    moment_parts = [moment] + [permute_xor(moment, "far", j) for j in range(1, n_far)]
    coef, inverse = cohort_fit(moment_parts, snps, design)
    columns, pair_coef, coef, inverse = lax.optimization_barrier(
        (columns, pair_coef, coef, inverse)
    )
    stats = column_sums(genes, columns)
    stat_parts = [stats] + [permute_xor(stats, "far", j) for j in range(1, n_far)]

    size = snps // n_far
    panel = size // n_near
    freedom = float(here * n_far - design - 1)
    line = ("far", "near")
    where = [far[None], near[None], n_far, n_near]
    sent = far_products(genes, columns, pair_coef, stats, *where)
    sent, stat_parts = lax.optimization_barrier((sent, stat_parts))
    sent = [piece.astype(jnp.float16) for piece in sent]
    pieces = {
        k: permute_xor(sent[k - n_near], line, k) for k in range(n_near, n_far * n_near)
    }
    home, away, factors = base_ratio(genes, columns, coef, inverse, stat_parts, *where)
    away = permute_xor(away.astype(jnp.float16), "near", 1)
    away = away.astype(jnp.float32) * (1.0 / WIDE)
    away_factors = permute_xor(factors, "near", 1)
    place = far * n_near + near
    columns_scale = lax.dynamic_slice_in_dim(coef, place * panel, panel, 0)

    def t_of(ratio, factors, offset):
        for j in range(1, n_far):
            weight = columns_scale[:, SCALE_LANE + 1 + j, None] * factors[None, j]
            ratio = ratio + pieces[j * n_near + offset].astype(jnp.float32) * weight
        return ratio * jnp.sqrt(freedom / (1.0 - ratio * ratio))

    first = [k for k in pieces if k % n_near]
    *taken, home = lax.optimization_barrier((*[pieces[k] for k in first], home))
    pieces.update(zip(first, taken))
    home = t_of(home, factors, 0)
    away = t_of(away, away_factors, 1)
    both = jnp.where(near == 0, jnp.stack([home, away], 1), jnp.stack([away, home], 1))
    return both.reshape(panel, maps, per_vox, plane)


def solution(mesh):
    sizes = dict(mesh.shape)
    devices = mesh.devices.reshape(sizes["group"], sizes["vox"], sizes["snp"] // 2, 2)
    split = Mesh(devices, ("group", "vox", "far", "near"))
    owner = ("group", "vox", "far", "near")
    placed = (P(owner, None, None, None), P(owner, None), P(owner, None), P(owner))
    return jax.shard_map(
        on_device,
        mesh=split,
        in_specs=placed,
        out_specs=P(("group", "far", "near"), None, "vox", None),
        check_vma=False,
    )
```

```python
import functools

import jax
import jax.numpy as jnp
import ml_dtypes
import numpy as np
from jax import lax
from jax.experimental import pallas as pl
from jax.experimental.pallas import tpu as pltpu
from jax.sharding import Mesh
from jax.sharding import PartitionSpec as P

SY = 16
SZ = 16
SITES = 4
REACH = 2
DPAD = 24
LANES = 128
SUBJ_TILE = 16
HIGHEST = lax.Precision.HIGHEST
VMEM_MOST = 56 * 2**20
VMEM_BASE = 12 * 2**20
SQUARE_ROW = 20
WIDE = 2.0**8
SCALE_LANE = DPAD
STRIDE = 32


def kernel_table(length):
    position = np.arange(length)
    offset = (position[:, None] - position[None, :]).astype(np.float32)
    weights = np.where(np.abs(offset) <= REACH, np.exp(-offset * offset / np.float32(2.0)), np.float32(0.0))
    total = sum(np.exp(-(k * k) / 2.0) for k in range(-REACH, REACH + 1))
    return (weights / np.float32(total)).astype(np.float32)


def plane_kernel(plane):
    row, depth = kernel_table(SY), kernel_table(SZ)
    table = row[:, None, :, None] * depth[None, :, None, :]
    return table.reshape(plane, plane).astype(ml_dtypes.bfloat16)


def row_order(maps, planes):
    rows = SUBJ_TILE * maps * planes
    source = np.arange(rows).reshape(SUBJ_TILE, maps * planes).T.reshape(-1)
    return np.eye(rows, dtype=np.float32)[source].astype(ml_dtypes.bfloat16)


def tree_sum(terms):
    while len(terms) > 1:
        terms = [terms[i] + terms[i + 1] for i in range(0, len(terms), 2)]
    return terms[0]


RESIDENT = 3 * 2**20
IN_VMEM = pl.BlockSpec(memory_space=pltpu.VMEM)
IN_SMEM = pl.BlockSpec(memory_space=pltpu.SMEM)


def params(extra=0):
    return pltpu.CompilerParams(vmem_limit_bytes=min(VMEM_MOST, VMEM_BASE + extra))


def size_of(value):
    return int(np.prod(value.shape)) * jnp.dtype(value.dtype).itemsize


def small(shape, dtype):
    return int(np.prod(shape)) * jnp.dtype(dtype).itemsize <= RESIDENT


def keep(value):
    if small(value.shape, value.dtype):
        return pltpu.with_memory_space_constraint(value, pltpu.VMEM)
    return value


def result(shape, dtype):
    if small(shape, dtype):
        return pltpu.VMEM(shape, dtype)
    return jax.ShapeDtypeStruct(shape, dtype)


def call(kernel, name, outs, scalars, arrays, scratch=(), moved=0):
    many = isinstance(outs, tuple)
    sizes = [size_of(value) for value in (*arrays, *(outs if many else (outs,)))]
    extra = 3 * sum(size for size in sizes if size > RESIDENT)
    return pl.pallas_call(
        kernel,
        out_shape=outs,
        in_specs=[IN_SMEM] * len(scalars) + [IN_VMEM] * len(arrays),
        out_specs=(IN_VMEM,) * len(outs) if many else IN_VMEM,
        scratch_shapes=list(scratch),
        compiler_params=params(extra),
        name=name,
    )(*scalars, *arrays[:moved], *[keep(value) for value in arrays[moved:]])


def tall_kernel(genotypes, codes, covariates, out, rows):
    snps = genotypes.shape[1]
    out[:snps, :] = jnp.transpose(genotypes[...])
    count = covariates.shape[0]
    site = lax.broadcasted_iota(jnp.int32, (SITES, codes.shape[1]), 0)
    rows[...] = jnp.zeros(rows.shape, jnp.float32)
    rows[:SITES, :] = (site == codes[...]).astype(jnp.float32)
    rows[SITES : SITES + count, :] = covariates[...].astype(jnp.float32)
    out[snps:, :] = rows[...].astype(jnp.bfloat16)


def tall_design(genotypes, covariates, site_codes):
    subjects, snps = genotypes.shape
    return pl.pallas_call(
        tall_kernel,
        out_shape=result((snps + DPAD, subjects), jnp.bfloat16),
        in_specs=[IN_VMEM] * 3,
        out_specs=IN_VMEM,
        scratch_shapes=[pltpu.VMEM((DPAD, subjects), jnp.float32)],
        compiler_params=params(VMEM_MOST),
        name="tall_design",
    )(genotypes, site_codes[None, :], covariates.T)


def smooth_kernel(group, planes, per_vox, parts, width, images, order, table, *outs):
    plane = table.shape[0]
    size = width // len(outs)
    groups = images.shape[1] // (group * planes)
    near = kernel_table(2 * REACH + 1)[REACH]
    for tile in range(images.shape[0] // SUBJ_TILE):
        here = pl.ds(tile * SUBJ_TILE, SUBJ_TILE)
        for part in range(groups):
            rows = images[here, part * group * planes : (part + 1) * group * planes, :]
            rows = rows.reshape(SUBJ_TILE * group * planes, plane)
            rows = jnp.dot(order[...], rows, preferred_element_type=jnp.float32)
            inplane = jnp.dot(
                rows.astype(jnp.bfloat16), table[...], preferred_element_type=jnp.float32
            )
            for m in range(group):
                slabs = [
                    inplane[(m * planes + x) * SUBJ_TILE : (m * planes + x + 1) * SUBJ_TILE]
                    for x in range(planes)
                ]
                for x in range(planes):
                    total = slabs[x] * float(near[REACH])
                    for lag in range(1, REACH + 1):
                        sides = [slabs[k] for k in (x - lag, x + lag) if 0 <= k < planes]
                        if sides:
                            total = total + functools.reduce(jnp.add, sides) * float(
                                near[REACH + lag]
                            )
                    column = ((part * group + m) * per_vox + x % per_vox) * plane
                    target = (x // per_vox) * parts + column // width
                    chunk, first = column % width // size, column % size
                    out = outs[chunk]
                    out[target, here, first : first + plane] = total.astype(jnp.bfloat16)


def smooth(images, n_vox, parts, chunks):
    subjects, maps, planes, plane = images.shape
    per_vox = planes // n_vox
    width = maps * per_vox * plane // parts
    size = width // chunks
    assert size % plane == 0
    group = max(1, min(maps, 256 // (SUBJ_TILE * planes)))
    step = min(subjects, 64)
    order = jnp.asarray(row_order(group, planes))
    table = jnp.asarray(plane_kernel(plane))
    return pl.pallas_call(
        functools.partial(smooth_kernel, group, planes, per_vox, parts, width),
        out_shape=[jax.ShapeDtypeStruct((n_vox * parts, subjects, size), jnp.bfloat16)] * chunks,
        grid=(subjects // step,),
        in_specs=[
            pl.BlockSpec((step, maps * planes, plane), lambda i: (i, 0, 0)),
            pl.BlockSpec(order.shape, lambda i: (0, 0)),
            pl.BlockSpec(table.shape, lambda i: (0, 0)),
        ],
        out_specs=[pl.BlockSpec((n_vox * parts, step, size), lambda i: (0, i, 0))] * chunks,
        compiler_params=params(VMEM_MOST),
        name="smooth",
    )(images.reshape(subjects, maps * planes, plane), order, table)


def moments_kernel(snps, slots, me, blocks, others, joined, out):
    rows = []
    half = len(slots) // 2
    for source in range(len(slots)):
        offset = jnp.bitwise_xor(me[0], source)
        index = 0
        for place, slot in enumerate(slots):
            index = index + jnp.where(offset == place, slot, 0)
        place = lax.rem(index, half)
        rows.append(jnp.where(index < half, blocks[place], others[place]))
    rows = jnp.concatenate(rows, axis=1)
    joined[...] = rows
    across = (((1,), (1,)), ((), ()))
    out[...] = jnp.zeros(out.shape, jnp.float32)
    out[:DPAD, : snps + DPAD] = lax.dot_general(
        rows[snps:], rows, across, preferred_element_type=jnp.float32
    )
    wide = rows[:snps].astype(jnp.float32)
    wide = wide * wide
    high = wide.astype(jnp.bfloat16)
    low = (wide - high.astype(jnp.float32)).astype(jnp.bfloat16)
    ones = jnp.ones((8, rows.shape[1]), jnp.bfloat16)
    squares = lax.dot_general(ones, high, across, preferred_element_type=jnp.float32)
    squares = squares + lax.dot_general(ones, low, across, preferred_element_type=jnp.float32)
    out[DPAD:, :snps] = squares


def moments(blocks, others, slots, me):
    count, rows, subjects = blocks.shape
    snps = rows - DPAD
    spread = -(-rows // LANES) * LANES
    outs = (
        result((rows, 2 * count * subjects), blocks.dtype),
        pltpu.HBM((DPAD + 8, spread), jnp.float32),
    )
    kernel = functools.partial(moments_kernel, snps, slots)
    return call(kernel, "moments", outs, [me], [blocks, others], (), 2)


def eliminate(total, snps, design, guard):
    lane = lax.broadcasted_iota(jnp.int32, (DPAD, LANES), 1)
    row = lax.broadcasted_iota(jnp.int32, (DPAD, LANES), 0)
    shift = 32
    gram = total[:DPAD, snps : snps + LANES]
    work = jnp.where((row >= design) & (lane == row), 1.0, gram)
    work = jnp.where(lane == row + shift, 1.0, work)
    for k in range(design):
        pivot = work[k : k + 1, k : k + 1]
        line = work[k : k + 1, :] / pivot
        if guard:
            line = jnp.where(pivot > gram[k : k + 1, k : k + 1] * 2.0**-14, line, 0.0)
        work = jnp.where(row == k, line, work - work[:, k : k + 1] * line)
    solved = pltpu.roll(work, LANES - shift, 1)
    return jnp.where((lane < design) & (row < design), solved, 0.0)


def gene_fit(total, snps, design, guard):
    solved = eliminate(total, snps, design, guard)
    cross_gene = total[:DPAD, :snps]
    fitted = jnp.dot(
        solved[:, :DPAD], cross_gene, precision=HIGHEST, preferred_element_type=jnp.float32
    )
    square = total[DPAD : DPAD + 1, :snps]
    rss = square - jnp.sum(cross_gene * fitted, axis=0, keepdims=True)
    if guard:
        rss = jnp.maximum(rss, square * 2.0**-10) + 1e-30
    return solved, fitted, lax.rsqrt(rss)


def pair_kernel(snps, design, moment, coef, lines):
    _, fitted, scale = gene_fit(moment[...], snps, design, True)
    lines[...] = jnp.zeros(lines.shape, jnp.float32)
    lines[:DPAD, :] = fitted * scale
    lines[SCALE_LANE : SCALE_LANE + 1, :] = scale
    coef[...] = jnp.transpose(lines[...])


def pair_fit(moment, snps, design):
    kernel = functools.partial(pair_kernel, snps, design)
    scratch = [pltpu.VMEM((LANES, snps), jnp.float32)]
    return call(kernel, "pair_fit", result((snps, LANES), jnp.float32), [], [moment], scratch, 1)


def cohort_kernel(snps, design, *refs):
    parts, (coef, inverse, lines) = refs[:-3], refs[-3:]
    moment = [part[...] for part in parts]
    solved, fitted, scale = gene_fit(tree_sum(moment), snps, design, False)
    inverse[...] = solved
    lines[...] = jnp.zeros(lines.shape, jnp.float32)
    lines[:DPAD, :] = fitted * -scale
    lines[SCALE_LANE : SCALE_LANE + 1, :] = scale
    for j in range(1, len(parts)):
        _, fit, own_scale = gene_fit(moment[j], snps, design, True)
        lane = SCALE_LANE + 1 + j
        lines[lane : lane + 1, :] = scale / own_scale
        lines[j * STRIDE : j * STRIDE + DPAD, :] = fit * scale
    coef[...] = jnp.transpose(lines[...])


def cohort_fit(parts, snps, design):
    kernel = functools.partial(cohort_kernel, snps, design)
    outs = (pltpu.HBM((snps, LANES), jnp.float32), pltpu.HBM((DPAD, LANES), jnp.float32))
    scratch = [pltpu.VMEM((LANES, snps), jnp.float32)]
    return call(kernel, "cohort_fit", outs, [], parts, scratch, len(parts))


def column_norm(sums, here):
    square = sums[SQUARE_ROW : SQUARE_ROW + 1, :]
    mean = jnp.sum(sums[:SITES, :], axis=0, keepdims=True) * (1.0 / here)
    spread = jnp.maximum(square - mean * mean * here, square * 2.0**-10)
    return jnp.sqrt(spread + 1e-30)


def sums_kernel(genes, columns, out):
    values = columns[...]
    wide = values.astype(jnp.float32)
    design = genes[genes.shape[0] - DPAD :, :]
    sums = jnp.dot(design, values, preferred_element_type=jnp.float32)
    square = jnp.sum(wide * wide, axis=0, keepdims=True)
    row = lax.broadcasted_iota(jnp.int32, sums.shape, 0)
    out[...] = jnp.where(row == SQUARE_ROW, square, sums)


def column_sums(genes, columns):
    outs = result((DPAD, columns.shape[1]), jnp.float32)
    return call(sums_kernel, "column_sums", outs, [], [genes, columns])


def far_kernel(here, count, far, near, genes, columns, coef, stats, *refs):
    outs, held = list(refs[:-1]), refs[-1]
    size = held.shape[0]
    panel = outs[0].shape[0]
    cross_image = stats[...]
    over = 1.0 / column_norm(cross_image, here)
    for j in range(1, count):
        block = pl.multiple_of(jnp.bitwise_xor(far[0], j) * size, size)
        held[...] = jnp.dot(
            genes[pl.ds(block, size), :], columns[...], preferred_element_type=jnp.float32
        )
        for k in range(size // panel):
            place = pl.multiple_of(jnp.bitwise_xor(near[0], k) * panel, panel)
            line = coef[pl.ds(block + place, panel), :]
            fit = jnp.dot(
                line[:, :DPAD], cross_image, precision=HIGHEST, preferred_element_type=jnp.float32
            )
            scale = line[:, SCALE_LANE : SCALE_LANE + 1]
            outs.pop(0)[...] = (scale * held[pl.ds(place, panel), :] - fit) * over


def far_products(genes, columns, coef, stats, far, near, n_far, n_near):
    here, width = columns.shape
    size = (genes.shape[0] - DPAD) // n_far
    outs = (result((size // n_near, width), jnp.float32),) * ((n_far - 1) * n_near)
    kernel = functools.partial(far_kernel, float(here), n_far)
    scratch = [pltpu.VMEM((size, width), jnp.float32)]
    return call(kernel, "far_products", outs, [far, near], [genes, columns, coef, stats], scratch)


def base_kernel(here, count, far, near, genes, columns, coef, inverse, *refs):
    parts, (home, away, factors, stack, held) = refs[:-5], refs[-5:]
    stats = [part[...] for part in parts]
    row = lax.broadcasted_iota(jnp.int32, stats[0].shape, 0)
    total = tree_sum(stats)
    known = row < SQUARE_ROW
    cross_image = jnp.where(known, total, 0.0)
    solved = jnp.dot(
        inverse[:, :DPAD], cross_image, precision=HIGHEST, preferred_element_type=jnp.float32
    )
    rss = total[SQUARE_ROW : SQUARE_ROW + 1, :] - jnp.sum(
        cross_image * solved, axis=0, keepdims=True
    )
    scale = lax.rsqrt(rss)
    stack[...] = jnp.zeros(stack.shape, jnp.float32)
    stack[:DPAD, :] = cross_image
    factors[...] = jnp.zeros(factors.shape, jnp.float32)
    for j in range(1, len(stats)):
        factors[j : j + 1, :] = column_norm(stats[j], here) * scale
        stack[j * STRIDE : j * STRIDE + DPAD, :] = jnp.where(known, stats[j], 0.0)
    size = held.shape[0]
    block = pl.ds(pl.multiple_of(far[0] * size, size), size)
    line = coef[block, :]
    sums = jnp.dot(genes[block, :], columns[...], preferred_element_type=jnp.float32)
    terms = jnp.dot(line, stack[...], precision=HIGHEST, preferred_element_type=jnp.float32)
    held[...] = (line[:, SCALE_LANE : SCALE_LANE + 1] * sums + terms) * scale
    panel = size // count
    for k, out in enumerate((home, away)):
        place = pl.multiple_of(jnp.bitwise_xor(near[0], k) * panel, panel)
        out[...] = held[pl.ds(place, panel), :] * (WIDE if k else 1.0)


def base_ratio(genes, columns, coef, inverse, parts, far, near, n_far, n_near):
    here, width = columns.shape
    size = (genes.shape[0] - DPAD) // n_far
    outs = (result((size // n_near, width), jnp.float32),) * 2
    outs += (result((8, width), jnp.float32),)
    kernel = functools.partial(base_kernel, float(here), n_near)
    scratch = [pltpu.VMEM((LANES, width), jnp.float32), pltpu.VMEM((size, width), jnp.float32)]
    arrays = [coef, inverse, genes, columns, *parts]
    kernel = functools.partial(reorder, kernel)
    return call(kernel, "base_ratio", outs, [far, near], arrays, scratch, 2)


def reorder(kernel, far, near, coef, inverse, genes, columns, *refs):
    kernel(far, near, genes, columns, coef, inverse, *refs)


def permute_xor(value, axes, bits):
    size = lax.axis_size(axes)
    return lax.ppermute(value, axes, [(i, i ^ bits) for i in range(size)])


def on_device(images, genotypes, covariates, site_codes):
    subjects, maps, planes, plane = images.shape
    n_vox, n_far, n_near = (lax.axis_size(name) for name in ("vox", "far", "near"))
    vox, far, near = (lax.axis_index(name) for name in ("vox", "far", "near"))
    snps = genotypes.shape[1]
    design = SITES + covariates.shape[1]
    per_vox = planes // n_vox
    count = n_vox * n_near
    here = count * subjects

    def exchange(value):
        value = lax.all_to_all(value, ("vox", "near"), 0, 0, tiled=True)
        return value.reshape(here, value.shape[2])

    tall = tall_design(genotypes, covariates, site_codes)
    other = n_near
    offsets = [o for o in range(count) if not o & other]
    blocks = [tall] + [permute_xor(tall, ("vox", "near"), o) for o in offsets[1:]]
    (smoothed,) = smooth(images, n_vox, n_near, 1)
    smoothed, *blocks = lax.optimization_barrier((smoothed, *blocks))
    columns = exchange(smoothed)
    blocks = jnp.stack(blocks)
    others = permute_xor(blocks, ("vox", "near"), other)
    order = offsets + [o | other for o in offsets]
    slots = tuple(order.index(o) for o in range(count))
    genes, moment = moments(blocks, others, slots, (vox * n_near + near)[None])
    pair_coef = pair_fit(moment, snps, design)
    moment_parts = [moment] + [permute_xor(moment, "far", j) for j in range(1, n_far)]
    coef, inverse = cohort_fit(moment_parts, snps, design)
    columns, pair_coef, coef, inverse = lax.optimization_barrier(
        (columns, pair_coef, coef, inverse)
    )
    stats = column_sums(genes, columns)
    stat_parts = [stats] + [permute_xor(stats, "far", j) for j in range(1, n_far)]

    size = snps // n_far
    panel = size // n_near
    freedom = float(here * n_far - design - 1)
    line = ("far", "near")
    where = [far[None], near[None], n_far, n_near]
    sent = list(far_products(genes, columns, pair_coef, stats, *where))
    sent[0] = sent[0].astype(jnp.float16)
    sent, stat_parts = lax.optimization_barrier((sent, stat_parts))
    sent = [piece.astype(jnp.float16) for piece in sent]
    pieces = {
        k: permute_xor(sent[k - n_near], line, k) for k in range(n_near, n_far * n_near)
    }
    home, away, factors = base_ratio(genes, columns, coef, inverse, stat_parts, *where)
    away = permute_xor(away.astype(jnp.float16), "near", 1)
    away = away.astype(jnp.float32) * (1.0 / WIDE)
    away_factors = permute_xor(factors, "near", 1)
    place = far * n_near + near
    columns_scale = lax.dynamic_slice_in_dim(coef, place * panel, panel, 0)

    def t_of(ratio, factors, offset):
        for j in range(1, n_far):
            weight = columns_scale[:, SCALE_LANE + 1 + j, None] * factors[None, j]
            ratio = ratio + pieces[j * n_near + offset].astype(jnp.float32) * weight
        return ratio * jnp.sqrt(freedom / (1.0 - ratio * ratio))

    home = t_of(home, factors, 0)
    away_factors, home = lax.optimization_barrier((away_factors, home))
    away = t_of(away, away_factors, 1)
    both = jnp.where(near == 0, jnp.stack([home, away], 1), jnp.stack([away, home], 1))
    return both.reshape(panel, maps, per_vox, plane)


def solution(mesh):
    sizes = dict(mesh.shape)
    devices = mesh.devices.reshape(sizes["group"], sizes["vox"], sizes["snp"] // 2, 2)
    split = Mesh(devices, ("group", "vox", "far", "near"))
    owner = ("group", "vox", "far", "near")
    placed = (P(owner, None, None, None), P(owner, None), P(owner, None), P(owner))
    return jax.shard_map(
        on_device,
        mesh=split,
        in_specs=placed,
        out_specs=P(("group", "far", "near"), None, "vox", None),
        check_vma=False,
    )
```

```python
import functools

import jax
import jax.numpy as jnp
import ml_dtypes
import numpy as np
from jax import lax
from jax.experimental import pallas as pl
from jax.experimental.pallas import tpu as pltpu
from jax.sharding import Mesh
from jax.sharding import PartitionSpec as P

SY = 16
SZ = 16
SITES = 4
REACH = 2
DPAD = 24
LANES = 128
SUBJ_TILE = 16
HIGHEST = lax.Precision.HIGHEST
VMEM_MOST = 56 * 2**20
VMEM_BASE = 12 * 2**20
SQUARE_ROW = 20
WIDE = 2.0**8
SCALE_LANE = DPAD
STRIDE = 32


def kernel_table(length):
    position = np.arange(length)
    offset = (position[:, None] - position[None, :]).astype(np.float32)
    weights = np.where(np.abs(offset) <= REACH, np.exp(-offset * offset / np.float32(2.0)), np.float32(0.0))
    total = sum(np.exp(-(k * k) / 2.0) for k in range(-REACH, REACH + 1))
    return (weights / np.float32(total)).astype(np.float32)


def plane_kernel(plane):
    row, depth = kernel_table(SY), kernel_table(SZ)
    table = row[:, None, :, None] * depth[None, :, None, :]
    return table.reshape(plane, plane).astype(ml_dtypes.bfloat16)


def row_order(maps, planes):
    rows = SUBJ_TILE * maps * planes
    source = np.arange(rows).reshape(SUBJ_TILE, maps * planes).T.reshape(-1)
    return np.eye(rows, dtype=np.float32)[source].astype(ml_dtypes.bfloat16)


def tree_sum(terms):
    while len(terms) > 1:
        terms = [terms[i] + terms[i + 1] for i in range(0, len(terms), 2)]
    return terms[0]


RESIDENT = 3 * 2**20
IN_VMEM = pl.BlockSpec(memory_space=pltpu.VMEM)
IN_SMEM = pl.BlockSpec(memory_space=pltpu.SMEM)


def params(extra=0):
    return pltpu.CompilerParams(vmem_limit_bytes=min(VMEM_MOST, VMEM_BASE + extra))


def size_of(value):
    return int(np.prod(value.shape)) * jnp.dtype(value.dtype).itemsize


def small(shape, dtype):
    return int(np.prod(shape)) * jnp.dtype(dtype).itemsize <= RESIDENT


def keep(value):
    if small(value.shape, value.dtype):
        return pltpu.with_memory_space_constraint(value, pltpu.VMEM)
    return value


def result(shape, dtype):
    if small(shape, dtype):
        return pltpu.VMEM(shape, dtype)
    return jax.ShapeDtypeStruct(shape, dtype)


def call(kernel, name, outs, scalars, arrays, scratch=(), moved=0):
    many = isinstance(outs, tuple)
    sizes = [size_of(value) for value in (*arrays, *(outs if many else (outs,)))]
    extra = 3 * sum(size for size in sizes if size > RESIDENT)
    return pl.pallas_call(
        kernel,
        out_shape=outs,
        in_specs=[IN_SMEM] * len(scalars) + [IN_VMEM] * len(arrays),
        out_specs=(IN_VMEM,) * len(outs) if many else IN_VMEM,
        scratch_shapes=list(scratch),
        compiler_params=params(extra),
        name=name,
    )(*scalars, *arrays[:moved], *[keep(value) for value in arrays[moved:]])


def tall_kernel(genotypes, codes, covariates, out, rows):
    snps = genotypes.shape[1]
    out[:snps, :] = jnp.transpose(genotypes[...])
    count = covariates.shape[0]
    site = lax.broadcasted_iota(jnp.int32, (SITES, codes.shape[1]), 0)
    rows[...] = jnp.zeros(rows.shape, jnp.float32)
    rows[:SITES, :] = (site == codes[...]).astype(jnp.float32)
    rows[SITES : SITES + count, :] = covariates[...].astype(jnp.float32)
    out[snps:, :] = rows[...].astype(jnp.bfloat16)


def tall_design(genotypes, covariates, site_codes):
    subjects, snps = genotypes.shape
    return pl.pallas_call(
        tall_kernel,
        out_shape=result((snps + DPAD, subjects), jnp.bfloat16),
        in_specs=[IN_VMEM] * 3,
        out_specs=IN_VMEM,
        scratch_shapes=[pltpu.VMEM((DPAD, subjects), jnp.float32)],
        compiler_params=params(VMEM_MOST),
        name="tall_design",
    )(genotypes, site_codes[None, :], covariates.T)


def smooth_kernel(group, planes, per_vox, parts, width, images, order, table, *outs):
    plane = table.shape[0]
    size = width // len(outs)
    groups = images.shape[1] // (group * planes)
    near = kernel_table(2 * REACH + 1)[REACH]
    for tile in range(images.shape[0] // SUBJ_TILE):
        here = pl.ds(tile * SUBJ_TILE, SUBJ_TILE)
        for part in range(groups):
            rows = images[here, part * group * planes : (part + 1) * group * planes, :]
            rows = rows.reshape(SUBJ_TILE * group * planes, plane)
            rows = jnp.dot(order[...], rows, preferred_element_type=jnp.float32)
            inplane = jnp.dot(
                rows.astype(jnp.bfloat16), table[...], preferred_element_type=jnp.float32
            )
            for m in range(group):
                slabs = [
                    inplane[(m * planes + x) * SUBJ_TILE : (m * planes + x + 1) * SUBJ_TILE]
                    for x in range(planes)
                ]
                for x in range(planes):
                    total = slabs[x] * float(near[REACH])
                    for lag in range(1, REACH + 1):
                        sides = [slabs[k] for k in (x - lag, x + lag) if 0 <= k < planes]
                        if sides:
                            total = total + functools.reduce(jnp.add, sides) * float(
                                near[REACH + lag]
                            )
                    column = ((part * group + m) * per_vox + x % per_vox) * plane
                    target = (x // per_vox) * parts + column // width
                    chunk, first = column % width // size, column % size
                    out = outs[chunk]
                    out[target, here, first : first + plane] = total.astype(jnp.bfloat16)


def smooth(images, n_vox, parts, chunks):
    subjects, maps, planes, plane = images.shape
    per_vox = planes // n_vox
    width = maps * per_vox * plane // parts
    size = width // chunks
    assert size % plane == 0
    group = max(1, min(maps, 256 // (SUBJ_TILE * planes)))
    step = min(subjects, 64)
    order = jnp.asarray(row_order(group, planes))
    table = jnp.asarray(plane_kernel(plane))
    return pl.pallas_call(
        functools.partial(smooth_kernel, group, planes, per_vox, parts, width),
        out_shape=[jax.ShapeDtypeStruct((n_vox * parts, subjects, size), jnp.bfloat16)] * chunks,
        grid=(subjects // step,),
        in_specs=[
            pl.BlockSpec((step, maps * planes, plane), lambda i: (i, 0, 0)),
            pl.BlockSpec(order.shape, lambda i: (0, 0)),
            pl.BlockSpec(table.shape, lambda i: (0, 0)),
        ],
        out_specs=[pl.BlockSpec((n_vox * parts, step, size), lambda i: (0, i, 0))] * chunks,
        compiler_params=params(VMEM_MOST),
        name="smooth",
    )(images.reshape(subjects, maps * planes, plane), order, table)


def moments_kernel(snps, slots, me, blocks, others, joined, out):
    rows = []
    half = len(slots) // 2
    for source in range(len(slots)):
        offset = jnp.bitwise_xor(me[0], source)
        index = 0
        for place, slot in enumerate(slots):
            index = index + jnp.where(offset == place, slot, 0)
        place = lax.rem(index, half)
        rows.append(jnp.where(index < half, blocks[place], others[place]))
    rows = jnp.concatenate(rows, axis=1)
    joined[...] = rows
    across = (((1,), (1,)), ((), ()))
    out[...] = jnp.zeros(out.shape, jnp.float32)
    out[:DPAD, : snps + DPAD] = lax.dot_general(
        rows[snps:], rows, across, preferred_element_type=jnp.float32
    )
    wide = rows[:snps].astype(jnp.float32)
    wide = wide * wide
    high = wide.astype(jnp.bfloat16)
    low = (wide - high.astype(jnp.float32)).astype(jnp.bfloat16)
    ones = jnp.ones((8, rows.shape[1]), jnp.bfloat16)
    squares = lax.dot_general(ones, high, across, preferred_element_type=jnp.float32)
    squares = squares + lax.dot_general(ones, low, across, preferred_element_type=jnp.float32)
    out[DPAD:, :snps] = squares


def moments(blocks, others, slots, me):
    count, rows, subjects = blocks.shape
    snps = rows - DPAD
    spread = -(-rows // LANES) * LANES
    outs = (
        result((rows, 2 * count * subjects), blocks.dtype),
        pltpu.HBM((DPAD + 8, spread), jnp.float32),
    )
    kernel = functools.partial(moments_kernel, snps, slots)
    return call(kernel, "moments", outs, [me], [blocks, others], (), 2)


def eliminate(total, snps, design, guard):
    lane = lax.broadcasted_iota(jnp.int32, (DPAD, LANES), 1)
    row = lax.broadcasted_iota(jnp.int32, (DPAD, LANES), 0)
    shift = 32
    gram = total[:DPAD, snps : snps + LANES]
    work = jnp.where((row >= design) & (lane == row), 1.0, gram)
    work = jnp.where(lane == row + shift, 1.0, work)
    for k in range(design):
        pivot = work[k : k + 1, k : k + 1]
        line = work[k : k + 1, :] / pivot
        if guard:
            line = jnp.where(pivot > gram[k : k + 1, k : k + 1] * 2.0**-14, line, 0.0)
        work = jnp.where(row == k, line, work - work[:, k : k + 1] * line)
    solved = pltpu.roll(work, LANES - shift, 1)
    return jnp.where((lane < design) & (row < design), solved, 0.0)


def gene_fit(total, snps, design, guard):
    solved = eliminate(total, snps, design, guard)
    cross_gene = total[:DPAD, :snps]
    fitted = jnp.dot(
        solved[:, :DPAD], cross_gene, precision=HIGHEST, preferred_element_type=jnp.float32
    )
    square = total[DPAD : DPAD + 1, :snps]
    rss = square - jnp.sum(cross_gene * fitted, axis=0, keepdims=True)
    if guard:
        rss = jnp.maximum(rss, square * 2.0**-10) + 1e-30
    return solved, fitted, lax.rsqrt(rss)


def pair_kernel(snps, design, moment, coef, lines):
    _, fitted, scale = gene_fit(moment[...], snps, design, True)
    lines[...] = jnp.zeros(lines.shape, jnp.float32)
    lines[:DPAD, :] = fitted * scale
    lines[SCALE_LANE : SCALE_LANE + 1, :] = scale
    coef[...] = jnp.transpose(lines[...])


def pair_fit(moment, snps, design):
    kernel = functools.partial(pair_kernel, snps, design)
    scratch = [pltpu.VMEM((LANES, snps), jnp.float32)]
    return call(kernel, "pair_fit", result((snps, LANES), jnp.float32), [], [moment], scratch, 1)


def cohort_lines(moments, snps, design, lines):
    solved, fitted, scale = gene_fit(tree_sum(moments), snps, design, False)
    lines[...] = jnp.zeros(lines.shape, jnp.float32)
    lines[:DPAD, :] = fitted * -scale
    lines[SCALE_LANE : SCALE_LANE + 1, :] = scale
    for j in range(1, len(moments)):
        _, fit, own_scale = gene_fit(moments[j], snps, design, True)
        lane = SCALE_LANE + 1 + j
        lines[lane : lane + 1, :] = scale / own_scale
        lines[j * STRIDE : j * STRIDE + DPAD, :] = fit * scale
    return solved


def column_norm(sums, here):
    square = sums[SQUARE_ROW : SQUARE_ROW + 1, :]
    mean = jnp.sum(sums[:SITES, :], axis=0, keepdims=True) * (1.0 / here)
    spread = jnp.maximum(square - mean * mean * here, square * 2.0**-10)
    return jnp.sqrt(spread + 1e-30)


def sums_kernel(genes, columns, out):
    values = columns[...]
    wide = values.astype(jnp.float32)
    design = genes[genes.shape[0] - DPAD :, :]
    sums = jnp.dot(design, values, preferred_element_type=jnp.float32)
    square = jnp.sum(wide * wide, axis=0, keepdims=True)
    row = lax.broadcasted_iota(jnp.int32, sums.shape, 0)
    out[...] = jnp.where(row == SQUARE_ROW, square, sums)


def column_sums(genes, columns):
    outs = result((DPAD, columns.shape[1]), jnp.float32)
    return call(sums_kernel, "column_sums", outs, [], [genes, columns])


def far_kernel(here, count, far, near, genes, columns, coef, stats, *refs):
    outs, held = list(refs[:-1]), refs[-1]
    size = held.shape[0]
    panel = outs[0].shape[0]
    cross_image = stats[...]
    over = 1.0 / column_norm(cross_image, here)
    for j in range(1, count):
        block = pl.multiple_of(jnp.bitwise_xor(far[0], j) * size, size)
        held[...] = jnp.dot(
            genes[pl.ds(block, size), :], columns[...], preferred_element_type=jnp.float32
        )
        for k in range(size // panel):
            place = pl.multiple_of(jnp.bitwise_xor(near[0], k) * panel, panel)
            line = coef[pl.ds(block + place, panel), :]
            fit = jnp.dot(
                line[:, :DPAD], cross_image, precision=HIGHEST, preferred_element_type=jnp.float32
            )
            scale = line[:, SCALE_LANE : SCALE_LANE + 1]
            outs.pop(0)[...] = (scale * held[pl.ds(place, panel), :] - fit) * over


def far_products(genes, columns, coef, stats, far, near, n_far, n_near):
    here, width = columns.shape
    size = (genes.shape[0] - DPAD) // n_far
    outs = (result((size // n_near, width), jnp.float32),) * ((n_far - 1) * n_near)
    kernel = functools.partial(far_kernel, float(here), n_far)
    scratch = [pltpu.VMEM((size, width), jnp.float32)]
    return call(kernel, "far_products", outs, [far, near], [genes, columns, coef, stats], scratch)


def base_kernel(here, design, count, far, near, genes, columns, *refs):
    parts, (home, away, factors, weights, stack, held, lines, coef) = refs[:-8], refs[-8:]
    n_far = len(parts) // 2
    size = held.shape[0]
    snps = size * n_far
    block = pl.ds(pl.multiple_of(far[0] * size, size), size)
    moments = [
        jnp.concatenate([part[:, block], part[:, snps : snps + LANES]], axis=1)
        for part in parts[:n_far]
    ]
    inverse = cohort_lines(moments, size, design, lines)
    coef[...] = jnp.transpose(lines[...])
    stats = [part[...] for part in parts[n_far:]]
    row = lax.broadcasted_iota(jnp.int32, stats[0].shape, 0)
    total = tree_sum(stats)
    known = row < SQUARE_ROW
    cross_image = jnp.where(known, total, 0.0)
    solved = jnp.dot(
        inverse[:, :DPAD], cross_image, precision=HIGHEST, preferred_element_type=jnp.float32
    )
    rss = total[SQUARE_ROW : SQUARE_ROW + 1, :] - jnp.sum(
        cross_image * solved, axis=0, keepdims=True
    )
    scale = lax.rsqrt(rss)
    stack[...] = jnp.zeros(stack.shape, jnp.float32)
    stack[:DPAD, :] = cross_image
    factors[...] = jnp.zeros(factors.shape, jnp.float32)
    for j in range(1, len(stats)):
        factors[j : j + 1, :] = column_norm(stats[j], here) * scale
        stack[j * STRIDE : j * STRIDE + DPAD, :] = jnp.where(known, stats[j], 0.0)
    line = coef[...]
    sums = jnp.dot(genes[block, :], columns[...], preferred_element_type=jnp.float32)
    terms = jnp.dot(line, stack[...], precision=HIGHEST, preferred_element_type=jnp.float32)
    held[...] = (line[:, SCALE_LANE : SCALE_LANE + 1] * sums + terms) * scale
    panel = size // count
    for k, out in enumerate((home, away)):
        place = pl.ds(pl.multiple_of(jnp.bitwise_xor(near[0], k) * panel, panel), panel)
        out[...] = held[place, :] * (WIDE if k else 1.0)
        if k == 0:
            weights[...] = coef[place, :]


def base_ratio(genes, columns, moments, parts, far, near, n_far, n_near, design):
    here, width = columns.shape
    size = (genes.shape[0] - DPAD) // n_far
    outs = (result((size // n_near, width), jnp.float32),) * 2
    outs += (result((8, width), jnp.float32), result((size // n_near, LANES), jnp.float32))
    kernel = functools.partial(base_kernel, float(here), design, n_near)
    scratch = [
        pltpu.VMEM((LANES, width), jnp.float32),
        pltpu.VMEM((size, width), jnp.float32),
        pltpu.VMEM((LANES, size), jnp.float32),
        pltpu.VMEM((size, LANES), jnp.float32),
    ]
    arrays = [genes, columns, *moments, *parts]
    return call(kernel, "base_ratio", outs, [far, near], arrays, scratch)


def permute_xor(value, axes, bits):
    size = lax.axis_size(axes)
    return lax.ppermute(value, axes, [(i, i ^ bits) for i in range(size)])


def on_device(images, genotypes, covariates, site_codes):
    subjects, maps, planes, plane = images.shape
    n_vox, n_far, n_near = (lax.axis_size(name) for name in ("vox", "far", "near"))
    vox, far, near = (lax.axis_index(name) for name in ("vox", "far", "near"))
    snps = genotypes.shape[1]
    design = SITES + covariates.shape[1]
    per_vox = planes // n_vox
    count = n_vox * n_near
    here = count * subjects

    def exchange(value):
        value = lax.all_to_all(value, ("vox", "near"), 0, 0, tiled=True)
        return value.reshape(here, value.shape[2])

    tall = tall_design(genotypes, covariates, site_codes)
    other = n_near
    offsets = [o for o in range(count) if not o & other]
    blocks = [tall] + [permute_xor(tall, ("vox", "near"), o) for o in offsets[1:]]
    (smoothed,) = smooth(images, n_vox, n_near, 1)
    smoothed, *blocks = lax.optimization_barrier((smoothed, *blocks))
    columns = exchange(smoothed)
    blocks = jnp.stack(blocks)
    others = permute_xor(blocks, ("vox", "near"), other)
    order = offsets + [o | other for o in offsets]
    slots = tuple(order.index(o) for o in range(count))
    genes, moment = moments(blocks, others, slots, (vox * n_near + near)[None])
    pair_coef = pair_fit(moment, snps, design)
    moment_parts = [moment] + [permute_xor(moment, "far", j) for j in range(1, n_far)]
    columns, pair_coef, moment_parts = lax.optimization_barrier(
        (columns, pair_coef, moment_parts)
    )
    stats = column_sums(genes, columns)
    stat_parts = [stats] + [permute_xor(stats, "far", j) for j in range(1, n_far)]

    size = snps // n_far
    panel = size // n_near
    freedom = float(here * n_far - design - 1)
    line = ("far", "near")
    where = [far[None], near[None], n_far, n_near]
    sent = list(far_products(genes, columns, pair_coef, stats, *where))
    sent[0] = sent[0].astype(jnp.float16)
    sent, stat_parts = lax.optimization_barrier((sent, stat_parts))
    sent = [piece.astype(jnp.float16) for piece in sent]
    pieces = {
        k: permute_xor(sent[k - n_near], line, k) for k in range(n_near, n_far * n_near)
    }
    home, away, factors, weights = base_ratio(
        genes, columns, moment_parts, stat_parts, *where, design
    )
    away = permute_xor(away.astype(jnp.float16), "near", 1)
    away = away.astype(jnp.float32) * (1.0 / WIDE)
    away_factors = permute_xor(factors, "near", 1)

    def t_of(ratio, factors, offset):
        for j in range(1, n_far):
            weight = weights[:, SCALE_LANE + 1 + j, None] * factors[None, j]
            ratio = ratio + pieces[j * n_near + offset].astype(jnp.float32) * weight
        return ratio * jnp.sqrt(freedom / (1.0 - ratio * ratio))

    home = t_of(home, factors, 0)
    away_factors, home = lax.optimization_barrier((away_factors, home))
    away = t_of(away, away_factors, 1)
    both = jnp.where(near == 0, jnp.stack([home, away], 1), jnp.stack([away, home], 1))
    return both.reshape(panel, maps, per_vox, plane)


def solution(mesh):
    sizes = dict(mesh.shape)
    devices = mesh.devices.reshape(sizes["group"], sizes["vox"], sizes["snp"] // 2, 2)
    split = Mesh(devices, ("group", "vox", "far", "near"))
    owner = ("group", "vox", "far", "near")
    placed = (P(owner, None, None, None), P(owner, None), P(owner, None), P(owner))
    return jax.shard_map(
        on_device,
        mesh=split,
        in_specs=placed,
        out_specs=P(("group", "far", "near"), None, "vox", None),
        check_vma=False,
    )
```

```python
import functools

import jax
import jax.numpy as jnp
import ml_dtypes
import numpy as np
from jax import lax
from jax.experimental import pallas as pl
from jax.experimental.pallas import tpu as pltpu
from jax.sharding import Mesh
from jax.sharding import PartitionSpec as P

SY = 16
SZ = 16
SITES = 4
REACH = 2
DPAD = 24
LANES = 128
SUBJ_TILE = 16
HIGHEST = lax.Precision.HIGHEST
VMEM_MOST = 56 * 2**20
VMEM_BASE = 12 * 2**20
SQUARE_ROW = 20
WIDE = 2.0**8
SCALE_LANE = DPAD
STRIDE = 32


def kernel_table(length):
    position = np.arange(length)
    offset = (position[:, None] - position[None, :]).astype(np.float32)
    weights = np.where(np.abs(offset) <= REACH, np.exp(-offset * offset / np.float32(2.0)), np.float32(0.0))
    total = sum(np.exp(-(k * k) / 2.0) for k in range(-REACH, REACH + 1))
    return (weights / np.float32(total)).astype(np.float32)


def plane_kernel(plane):
    row, depth = kernel_table(SY), kernel_table(SZ)
    table = row[:, None, :, None] * depth[None, :, None, :]
    return table.reshape(plane, plane).astype(ml_dtypes.bfloat16)


def row_order(maps, planes):
    rows = SUBJ_TILE * maps * planes
    source = np.arange(rows).reshape(SUBJ_TILE, maps * planes).T.reshape(-1)
    return np.eye(rows, dtype=np.float32)[source].astype(ml_dtypes.bfloat16)


def tree_sum(terms):
    while len(terms) > 1:
        terms = [terms[i] + terms[i + 1] for i in range(0, len(terms), 2)]
    return terms[0]


RESIDENT = 3 * 2**20
IN_VMEM = pl.BlockSpec(memory_space=pltpu.VMEM)
IN_SMEM = pl.BlockSpec(memory_space=pltpu.SMEM)


def params(extra=0):
    return pltpu.CompilerParams(vmem_limit_bytes=min(VMEM_MOST, VMEM_BASE + extra))


def size_of(value):
    return int(np.prod(value.shape)) * jnp.dtype(value.dtype).itemsize


def small(shape, dtype):
    return int(np.prod(shape)) * jnp.dtype(dtype).itemsize <= RESIDENT


def keep(value):
    if small(value.shape, value.dtype):
        return pltpu.with_memory_space_constraint(value, pltpu.VMEM)
    return value


def result(shape, dtype):
    if small(shape, dtype):
        return pltpu.VMEM(shape, dtype)
    return jax.ShapeDtypeStruct(shape, dtype)


def call(kernel, name, outs, scalars, arrays, scratch=(), moved=0):
    many = isinstance(outs, tuple)
    sizes = [size_of(value) for value in (*arrays, *(outs if many else (outs,)))]
    extra = 3 * sum(size for size in sizes if size > RESIDENT)
    return pl.pallas_call(
        kernel,
        out_shape=outs,
        in_specs=[IN_SMEM] * len(scalars) + [IN_VMEM] * len(arrays),
        out_specs=(IN_VMEM,) * len(outs) if many else IN_VMEM,
        scratch_shapes=list(scratch),
        compiler_params=params(extra),
        name=name,
    )(*scalars, *arrays[:moved], *[keep(value) for value in arrays[moved:]])


def tall_kernel(genotypes, codes, covariates, out, rows):
    snps = genotypes.shape[1]
    out[:snps, :] = jnp.transpose(genotypes[...])
    count = covariates.shape[0]
    site = lax.broadcasted_iota(jnp.int32, (SITES, codes.shape[1]), 0)
    rows[...] = jnp.zeros(rows.shape, jnp.float32)
    rows[:SITES, :] = (site == codes[...]).astype(jnp.float32)
    rows[SITES : SITES + count, :] = covariates[...].astype(jnp.float32)
    out[snps:, :] = rows[...].astype(jnp.bfloat16)


def tall_design(genotypes, covariates, site_codes):
    subjects, snps = genotypes.shape
    return pl.pallas_call(
        tall_kernel,
        out_shape=result((snps + DPAD, subjects), jnp.bfloat16),
        in_specs=[IN_VMEM] * 3,
        out_specs=IN_VMEM,
        scratch_shapes=[pltpu.VMEM((DPAD, subjects), jnp.float32)],
        compiler_params=params(VMEM_MOST),
        name="tall_design",
    )(genotypes, site_codes[None, :], covariates.T)


def smooth_kernel(group, planes, per_vox, parts, width, images, order, table, *outs):
    plane = table.shape[0]
    size = width // len(outs)
    groups = images.shape[1] // (group * planes)
    near = kernel_table(2 * REACH + 1)[REACH]
    for tile in range(images.shape[0] // SUBJ_TILE):
        here = pl.ds(tile * SUBJ_TILE, SUBJ_TILE)
        for part in range(groups):
            rows = images[here, part * group * planes : (part + 1) * group * planes, :]
            rows = rows.reshape(SUBJ_TILE * group * planes, plane)
            rows = jnp.dot(order[...], rows, preferred_element_type=jnp.float32)
            inplane = jnp.dot(
                rows.astype(jnp.bfloat16), table[...], preferred_element_type=jnp.float32
            )
            for m in range(group):
                slabs = [
                    inplane[(m * planes + x) * SUBJ_TILE : (m * planes + x + 1) * SUBJ_TILE]
                    for x in range(planes)
                ]
                for x in range(planes):
                    total = slabs[x] * float(near[REACH])
                    for lag in range(1, REACH + 1):
                        sides = [slabs[k] for k in (x - lag, x + lag) if 0 <= k < planes]
                        if sides:
                            total = total + functools.reduce(jnp.add, sides) * float(
                                near[REACH + lag]
                            )
                    column = ((part * group + m) * per_vox + x % per_vox) * plane
                    target = (x // per_vox) * parts + column // width
                    chunk, first = column % width // size, column % size
                    out = outs[chunk]
                    out[target, here, first : first + plane] = total.astype(jnp.bfloat16)


def smooth(images, n_vox, parts, chunks):
    subjects, maps, planes, plane = images.shape
    per_vox = planes // n_vox
    width = maps * per_vox * plane // parts
    size = width // chunks
    assert size % plane == 0
    group = max(1, min(maps, 256 // (SUBJ_TILE * planes)))
    step = min(subjects, 64)
    order = jnp.asarray(row_order(group, planes))
    table = jnp.asarray(plane_kernel(plane))
    return pl.pallas_call(
        functools.partial(smooth_kernel, group, planes, per_vox, parts, width),
        out_shape=[jax.ShapeDtypeStruct((n_vox * parts, subjects, size), jnp.bfloat16)] * chunks,
        grid=(subjects // step,),
        in_specs=[
            pl.BlockSpec((step, maps * planes, plane), lambda i: (i, 0, 0)),
            pl.BlockSpec(order.shape, lambda i: (0, 0)),
            pl.BlockSpec(table.shape, lambda i: (0, 0)),
        ],
        out_specs=[pl.BlockSpec((n_vox * parts, step, size), lambda i: (0, i, 0))] * chunks,
        compiler_params=params(VMEM_MOST),
        name="smooth",
    )(images.reshape(subjects, maps * planes, plane), order, table)


def moments_kernel(snps, slots, me, blocks, others, joined, out):
    rows = []
    half = len(slots) // 2
    for source in range(len(slots)):
        offset = jnp.bitwise_xor(me[0], source)
        index = 0
        for place, slot in enumerate(slots):
            index = index + jnp.where(offset == place, slot, 0)
        place = lax.rem(index, half)
        rows.append(jnp.where(index < half, blocks[place], others[place]))
    rows = jnp.concatenate(rows, axis=1)
    joined[...] = rows
    across = (((1,), (1,)), ((), ()))
    out[...] = jnp.zeros(out.shape, jnp.float32)
    out[:DPAD, : snps + DPAD] = lax.dot_general(
        rows[snps:], rows, across, preferred_element_type=jnp.float32
    )
    wide = rows[:snps].astype(jnp.float32)
    wide = wide * wide
    high = wide.astype(jnp.bfloat16)
    low = (wide - high.astype(jnp.float32)).astype(jnp.bfloat16)
    ones = jnp.ones((8, rows.shape[1]), jnp.bfloat16)
    squares = lax.dot_general(ones, high, across, preferred_element_type=jnp.float32)
    squares = squares + lax.dot_general(ones, low, across, preferred_element_type=jnp.float32)
    out[DPAD:, :snps] = squares


def moments(blocks, others, slots, me):
    count, rows, subjects = blocks.shape
    snps = rows - DPAD
    spread = -(-rows // LANES) * LANES
    outs = (
        result((rows, 2 * count * subjects), blocks.dtype),
        pltpu.HBM((DPAD + 8, spread), jnp.float32),
    )
    kernel = functools.partial(moments_kernel, snps, slots)
    return call(kernel, "moments", outs, [me], [blocks, others], (), 2)


def eliminate(total, snps, design, guard):
    lane = lax.broadcasted_iota(jnp.int32, (DPAD, LANES), 1)
    row = lax.broadcasted_iota(jnp.int32, (DPAD, LANES), 0)
    shift = 32
    gram = total[:DPAD, snps : snps + LANES]
    work = jnp.where((row >= design) & (lane == row), 1.0, gram)
    work = jnp.where(lane == row + shift, 1.0, work)
    for k in range(design):
        pivot = work[k : k + 1, k : k + 1]
        line = work[k : k + 1, :] / pivot
        if guard:
            line = jnp.where(pivot > gram[k : k + 1, k : k + 1] * 2.0**-14, line, 0.0)
        work = jnp.where(row == k, line, work - work[:, k : k + 1] * line)
    solved = pltpu.roll(work, LANES - shift, 1)
    return jnp.where((lane < design) & (row < design), solved, 0.0)


def gene_fit(total, snps, design, guard):
    solved = eliminate(total, snps, design, guard)
    cross_gene = total[:DPAD, :snps]
    fitted = jnp.dot(
        solved[:, :DPAD], cross_gene, precision=HIGHEST, preferred_element_type=jnp.float32
    )
    square = total[DPAD : DPAD + 1, :snps]
    rss = square - jnp.sum(cross_gene * fitted, axis=0, keepdims=True)
    if guard:
        rss = jnp.maximum(rss, square * 2.0**-10) + 1e-30
    return solved, fitted, lax.rsqrt(rss)


def pair_kernel(snps, design, moment, coef, lines):
    _, fitted, scale = gene_fit(moment[...], snps, design, True)
    lines[...] = jnp.zeros(lines.shape, jnp.float32)
    lines[:DPAD, :] = fitted * scale
    lines[SCALE_LANE : SCALE_LANE + 1, :] = scale
    coef[...] = jnp.transpose(lines[...])


def pair_fit(moment, snps, design):
    kernel = functools.partial(pair_kernel, snps, design)
    scratch = [pltpu.VMEM((LANES, snps), jnp.float32)]
    return call(kernel, "pair_fit", result((snps, LANES), jnp.float32), [], [moment], scratch, 1)


def cohort_lines(moments, snps, design, lines):
    solved, fitted, scale = gene_fit(tree_sum(moments), snps, design, False)
    lines[...] = jnp.zeros(lines.shape, jnp.float32)
    lines[:DPAD, :] = fitted * -scale
    lines[SCALE_LANE : SCALE_LANE + 1, :] = scale
    for j in range(1, len(moments)):
        _, fit, own_scale = gene_fit(moments[j], snps, design, True)
        lane = SCALE_LANE + 1 + j
        lines[lane : lane + 1, :] = scale / own_scale
        lines[j * STRIDE : j * STRIDE + DPAD, :] = fit * scale
    return solved


def column_norm(sums, here):
    square = sums[SQUARE_ROW : SQUARE_ROW + 1, :]
    mean = jnp.sum(sums[:SITES, :], axis=0, keepdims=True) * (1.0 / here)
    spread = jnp.maximum(square - mean * mean * here, square * 2.0**-10)
    return jnp.sqrt(spread + 1e-30)


def sums_kernel(genes, columns, out):
    values = columns[...]
    wide = values.astype(jnp.float32)
    design = genes[genes.shape[0] - DPAD :, :]
    sums = jnp.dot(design, values, preferred_element_type=jnp.float32)
    square = jnp.sum(wide * wide, axis=0, keepdims=True)
    row = lax.broadcasted_iota(jnp.int32, sums.shape, 0)
    out[...] = jnp.where(row == SQUARE_ROW, square, sums)


def column_sums(genes, columns):
    outs = result((DPAD, columns.shape[1]), jnp.float32)
    return call(sums_kernel, "column_sums", outs, [], [genes, columns])


def far_kernel(here, count, far, near, genes, columns, coef, stats, *refs):
    outs, held = list(refs[:-1]), refs[-1]
    size = held.shape[0]
    panel = outs[0].shape[0]
    cross_image = stats[...]
    over = 1.0 / column_norm(cross_image, here)
    for j in range(1, count):
        block = pl.multiple_of(jnp.bitwise_xor(far[0], j) * size, size)
        held[...] = jnp.dot(
            genes[pl.ds(block, size), :], columns[...], preferred_element_type=jnp.float32
        )
        for k in range(size // panel):
            place = pl.multiple_of(jnp.bitwise_xor(near[0], k) * panel, panel)
            line = coef[pl.ds(block + place, panel), :]
            fit = jnp.dot(
                line[:, :DPAD], cross_image, precision=HIGHEST, preferred_element_type=jnp.float32
            )
            scale = line[:, SCALE_LANE : SCALE_LANE + 1]
            outs.pop(0)[...] = (scale * held[pl.ds(place, panel), :] - fit) * over


def far_products(genes, columns, coef, stats, far, near, n_far, n_near):
    here, width = columns.shape
    size = (genes.shape[0] - DPAD) // n_far
    outs = (result((size // n_near, width), jnp.float32),) * ((n_far - 1) * n_near)
    kernel = functools.partial(far_kernel, float(here), n_far)
    scratch = [pltpu.VMEM((size, width), jnp.float32)]
    return call(kernel, "far_products", outs, [far, near], [genes, columns, coef, stats], scratch)


def base_kernel(here, design, count, far, near, genes, columns, *refs):
    parts, (home, away, factors, weights, stack, held, lines, coef) = refs[:-8], refs[-8:]
    n_far = len(parts) // 2
    size = held.shape[0]
    snps = size * n_far
    block = pl.ds(pl.multiple_of(far[0] * size, size), size)
    moments = [
        jnp.concatenate([part[:, block], part[:, snps : snps + LANES]], axis=1)
        for part in parts[:n_far]
    ]
    inverse = cohort_lines(moments, size, design, lines)
    coef[...] = jnp.transpose(lines[...])
    stats = [part[...] for part in parts[n_far:]]
    row = lax.broadcasted_iota(jnp.int32, stats[0].shape, 0)
    total = tree_sum(stats)
    known = row < SQUARE_ROW
    cross_image = jnp.where(known, total, 0.0)
    solved = jnp.dot(
        inverse[:, :DPAD], cross_image, precision=HIGHEST, preferred_element_type=jnp.float32
    )
    rss = total[SQUARE_ROW : SQUARE_ROW + 1, :] - jnp.sum(
        cross_image * solved, axis=0, keepdims=True
    )
    scale = lax.rsqrt(rss)
    stack[...] = jnp.zeros(stack.shape, jnp.float32)
    stack[:DPAD, :] = cross_image
    factors[...] = jnp.zeros(factors.shape, jnp.float32)
    for j in range(1, len(stats)):
        factors[j : j + 1, :] = column_norm(stats[j], here) * scale
        stack[j * STRIDE : j * STRIDE + DPAD, :] = jnp.where(known, stats[j], 0.0)
    line = coef[...]
    sums = jnp.dot(genes[block, :], columns[...], preferred_element_type=jnp.float32)
    terms = jnp.dot(line, stack[...], precision=HIGHEST, preferred_element_type=jnp.float32)
    held[...] = (line[:, SCALE_LANE : SCALE_LANE + 1] * sums + terms) * scale
    panel = size // count
    for k, out in enumerate((home, away)):
        place = pl.ds(pl.multiple_of(jnp.bitwise_xor(near[0], k) * panel, panel), panel)
        out[...] = held[place, :] * (WIDE if k else 1.0)
        if k == 0:
            weights[...] = coef[place, :]


def base_ratio(genes, columns, moments, parts, far, near, n_far, n_near, design):
    here, width = columns.shape
    size = (genes.shape[0] - DPAD) // n_far
    outs = (result((size // n_near, width), jnp.float32),) * 2
    outs += (result((8, width), jnp.float32), result((size // n_near, LANES), jnp.float32))
    kernel = functools.partial(base_kernel, float(here), design, n_near)
    scratch = [
        pltpu.VMEM((LANES, width), jnp.float32),
        pltpu.VMEM((size, width), jnp.float32),
        pltpu.VMEM((LANES, size), jnp.float32),
        pltpu.VMEM((size, LANES), jnp.float32),
    ]
    arrays = [genes, columns, *moments, *parts]
    return call(kernel, "base_ratio", outs, [far, near], arrays, scratch)


def permute_xor(value, axes, bits):
    size = lax.axis_size(axes)
    return lax.ppermute(value, axes, [(i, i ^ bits) for i in range(size)])


def on_device(images, genotypes, covariates, site_codes):
    subjects, maps, planes, plane = images.shape
    n_vox, n_far, n_near = (lax.axis_size(name) for name in ("vox", "far", "near"))
    vox, far, near = (lax.axis_index(name) for name in ("vox", "far", "near"))
    snps = genotypes.shape[1]
    design = SITES + covariates.shape[1]
    per_vox = planes // n_vox
    count = n_vox * n_near
    here = count * subjects

    def exchange(value):
        value = lax.all_to_all(value, ("vox", "near"), 0, 0, tiled=True)
        return value.reshape(here, value.shape[2])

    tall = tall_design(genotypes, covariates, site_codes)
    other = n_near
    offsets = [o for o in range(count) if not o & other]
    blocks = [tall] + [permute_xor(tall, ("vox", "near"), o) for o in offsets[1:]]
    (smoothed,) = smooth(images, n_vox, n_near, 1)
    smoothed, *blocks = lax.optimization_barrier((smoothed, *blocks))
    columns = exchange(smoothed)
    blocks = jnp.stack(blocks)
    others = permute_xor(blocks, ("vox", "near"), other)
    order = offsets + [o | other for o in offsets]
    slots = tuple(order.index(o) for o in range(count))
    genes, moment = moments(blocks, others, slots, (vox * n_near + near)[None])
    pair_coef = pair_fit(moment, snps, design)
    moment_parts = [moment] + [permute_xor(moment, "far", j) for j in range(1, n_far)]
    columns, pair_coef, moment_parts = lax.optimization_barrier(
        (columns, pair_coef, moment_parts)
    )
    stats = column_sums(genes, columns)
    stat_parts = [stats] + [permute_xor(stats, "far", j) for j in range(1, n_far)]

    size = snps // n_far
    panel = size // n_near
    freedom = float(here * n_far - design - 1)
    line = ("far", "near")
    where = [far[None], near[None], n_far, n_near]
    sent = list(far_products(genes, columns, pair_coef, stats, *where))
    sent[0] = sent[0].astype(jnp.float16)
    sent, stat_parts = lax.optimization_barrier((sent, stat_parts))
    sent = [piece.astype(jnp.float16) for piece in sent]
    pieces = {
        k: permute_xor(sent[k - n_near], line, k) for k in range(n_near, n_far * n_near)
    }
    home, away, factors, weights = base_ratio(
        genes, columns, moment_parts, stat_parts, *where, design
    )
    away = permute_xor(away.astype(jnp.float16), "near", 1)
    away = away.astype(jnp.float32) * (1.0 / WIDE)
    away_factors = permute_xor(factors, "near", 1)

    def t_of(ratio, factors, offset):
        for j in range(1, n_far):
            weight = weights[:, SCALE_LANE + 1 + j, None] * factors[None, j]
            ratio = ratio + pieces[j * n_near + offset].astype(jnp.float32) * weight
        return ratio * jnp.sqrt(freedom / (1.0 - ratio * ratio))

    shape = (panel, maps // n_near, per_vox, plane)
    home = t_of(home, factors, 0)
    away_factors, home = lax.optimization_barrier((away_factors, home))
    home = home.reshape(shape)
    away = t_of(away, away_factors, 1).reshape(shape)
    both = [jnp.concatenate(pair, axis=1) for pair in ([home, away], [away, home])]
    return jnp.where(near == 0, *both)


def solution(mesh):
    sizes = dict(mesh.shape)
    devices = mesh.devices.reshape(sizes["group"], sizes["vox"], sizes["snp"] // 2, 2)
    split = Mesh(devices, ("group", "vox", "far", "near"))
    owner = ("group", "vox", "far", "near")
    placed = (P(owner, None, None, None), P(owner, None), P(owner, None), P(owner))
    return jax.shard_map(
        on_device,
        mesh=split,
        in_specs=placed,
        out_specs=P(("group", "far", "near"), None, "vox", None),
        check_vma=False,
    )
```

```python
import functools

import jax
import jax.numpy as jnp
import ml_dtypes
import numpy as np
from jax import lax
from jax.experimental import pallas as pl
from jax.experimental.pallas import tpu as pltpu
from jax.sharding import Mesh
from jax.sharding import PartitionSpec as P

SY = 16
SZ = 16
SITES = 4
REACH = 2
DPAD = 24
LANES = 128
SUBJ_TILE = 16
HIGHEST = lax.Precision.HIGHEST
VMEM_MOST = 56 * 2**20
VMEM_BASE = 12 * 2**20
SQUARE_ROW = 20
WIDE = 2.0**8
FINE = 2.0**11
SCALE_LANE = DPAD
STRIDE = 32


def kernel_table(length):
    position = np.arange(length)
    offset = (position[:, None] - position[None, :]).astype(np.float32)
    weights = np.where(np.abs(offset) <= REACH, np.exp(-offset * offset / np.float32(2.0)), np.float32(0.0))
    total = sum(np.exp(-(k * k) / 2.0) for k in range(-REACH, REACH + 1))
    return (weights / np.float32(total)).astype(np.float32)


def plane_kernel(plane):
    row, depth = kernel_table(SY), kernel_table(SZ)
    table = row[:, None, :, None] * depth[None, :, None, :]
    return table.reshape(plane, plane).astype(ml_dtypes.bfloat16)


def row_order(maps, planes):
    rows = SUBJ_TILE * maps * planes
    source = np.arange(rows).reshape(SUBJ_TILE, maps * planes).T.reshape(-1)
    return np.eye(rows, dtype=np.float32)[source].astype(ml_dtypes.bfloat16)


def tree_sum(terms):
    while len(terms) > 1:
        terms = [terms[i] + terms[i + 1] for i in range(0, len(terms), 2)]
    return terms[0]


RESIDENT = 3 * 2**20
IN_VMEM = pl.BlockSpec(memory_space=pltpu.VMEM)
IN_SMEM = pl.BlockSpec(memory_space=pltpu.SMEM)


def params(extra=0):
    return pltpu.CompilerParams(vmem_limit_bytes=min(VMEM_MOST, VMEM_BASE + extra))


def size_of(value):
    return int(np.prod(value.shape)) * jnp.dtype(value.dtype).itemsize


def small(shape, dtype):
    return int(np.prod(shape)) * jnp.dtype(dtype).itemsize <= RESIDENT


def keep(value):
    if small(value.shape, value.dtype):
        return pltpu.with_memory_space_constraint(value, pltpu.VMEM)
    return value


def result(shape, dtype):
    if small(shape, dtype):
        return pltpu.VMEM(shape, dtype)
    return jax.ShapeDtypeStruct(shape, dtype)


def call(kernel, name, outs, scalars, arrays, scratch=(), moved=0):
    many = isinstance(outs, tuple)
    sizes = [size_of(value) for value in (*arrays, *(outs if many else (outs,)))]
    extra = 3 * sum(size for size in sizes if size > RESIDENT)
    return pl.pallas_call(
        kernel,
        out_shape=outs,
        in_specs=[IN_SMEM] * len(scalars) + [IN_VMEM] * len(arrays),
        out_specs=(IN_VMEM,) * len(outs) if many else IN_VMEM,
        scratch_shapes=list(scratch),
        compiler_params=params(extra),
        name=name,
    )(*scalars, *arrays[:moved], *[keep(value) for value in arrays[moved:]])


def tall_kernel(genotypes, codes, covariates, out, rows):
    snps = genotypes.shape[1]
    out[:snps, :] = jnp.transpose(genotypes[...])
    count = covariates.shape[0]
    site = lax.broadcasted_iota(jnp.int32, (SITES, codes.shape[1]), 0)
    rows[...] = jnp.zeros(rows.shape, jnp.float32)
    rows[:SITES, :] = (site == codes[...]).astype(jnp.float32)
    rows[SITES : SITES + count, :] = covariates[...].astype(jnp.float32)
    out[snps:, :] = rows[...].astype(jnp.bfloat16)


def tall_design(genotypes, covariates, site_codes):
    subjects, snps = genotypes.shape
    return pl.pallas_call(
        tall_kernel,
        out_shape=result((snps + DPAD, subjects), jnp.bfloat16),
        in_specs=[IN_VMEM] * 3,
        out_specs=IN_VMEM,
        scratch_shapes=[pltpu.VMEM((DPAD, subjects), jnp.float32)],
        compiler_params=params(VMEM_MOST),
        name="tall_design",
    )(genotypes, site_codes[None, :], covariates.T)


def smooth_kernel(group, planes, per_vox, parts, width, images, order, table, *outs):
    plane = table.shape[0]
    size = width // len(outs)
    groups = images.shape[1] // (group * planes)
    near = kernel_table(2 * REACH + 1)[REACH]
    for tile in range(images.shape[0] // SUBJ_TILE):
        here = pl.ds(tile * SUBJ_TILE, SUBJ_TILE)
        for part in range(groups):
            rows = images[here, part * group * planes : (part + 1) * group * planes, :]
            rows = rows.reshape(SUBJ_TILE * group * planes, plane)
            rows = jnp.dot(order[...], rows, preferred_element_type=jnp.float32)
            inplane = jnp.dot(
                rows.astype(jnp.bfloat16), table[...], preferred_element_type=jnp.float32
            )
            for m in range(group):
                slabs = [
                    inplane[(m * planes + x) * SUBJ_TILE : (m * planes + x + 1) * SUBJ_TILE]
                    for x in range(planes)
                ]
                for x in range(planes):
                    total = slabs[x] * float(near[REACH])
                    for lag in range(1, REACH + 1):
                        sides = [slabs[k] for k in (x - lag, x + lag) if 0 <= k < planes]
                        if sides:
                            total = total + functools.reduce(jnp.add, sides) * float(
                                near[REACH + lag]
                            )
                    column = ((part * group + m) * per_vox + x % per_vox) * plane
                    target = (x // per_vox) * parts + column // width
                    chunk, first = column % width // size, column % size
                    out = outs[chunk]
                    out[target, here, first : first + plane] = total.astype(jnp.bfloat16)


def smooth(images, n_vox, parts, chunks):
    subjects, maps, planes, plane = images.shape
    per_vox = planes // n_vox
    width = maps * per_vox * plane // parts
    size = width // chunks
    assert size % plane == 0
    group = max(1, min(maps, 256 // (SUBJ_TILE * planes)))
    step = min(subjects, 64)
    order = jnp.asarray(row_order(group, planes))
    table = jnp.asarray(plane_kernel(plane))
    return pl.pallas_call(
        functools.partial(smooth_kernel, group, planes, per_vox, parts, width),
        out_shape=[jax.ShapeDtypeStruct((n_vox * parts, subjects, size), jnp.bfloat16)] * chunks,
        grid=(subjects // step,),
        in_specs=[
            pl.BlockSpec((step, maps * planes, plane), lambda i: (i, 0, 0)),
            pl.BlockSpec(order.shape, lambda i: (0, 0)),
            pl.BlockSpec(table.shape, lambda i: (0, 0)),
        ],
        out_specs=[pl.BlockSpec((n_vox * parts, step, size), lambda i: (0, i, 0))] * chunks,
        compiler_params=params(VMEM_MOST),
        name="smooth",
    )(images.reshape(subjects, maps * planes, plane), order, table)


def moments_kernel(snps, slots, me, blocks, others, joined, out):
    rows = []
    half = len(slots) // 2
    for source in range(len(slots)):
        offset = jnp.bitwise_xor(me[0], source)
        index = 0
        for place, slot in enumerate(slots):
            index = index + jnp.where(offset == place, slot, 0)
        place = lax.rem(index, half)
        rows.append(jnp.where(index < half, blocks[place], others[place]))
    rows = jnp.concatenate(rows, axis=1)
    joined[...] = rows
    across = (((1,), (1,)), ((), ()))
    out[...] = jnp.zeros(out.shape, jnp.float32)
    out[:DPAD, : snps + DPAD] = lax.dot_general(
        rows[snps:], rows, across, preferred_element_type=jnp.float32
    )
    wide = rows[:snps].astype(jnp.float32)
    wide = wide * wide
    high = wide.astype(jnp.bfloat16)
    low = (wide - high.astype(jnp.float32)).astype(jnp.bfloat16)
    ones = jnp.ones((8, rows.shape[1]), jnp.bfloat16)
    squares = lax.dot_general(ones, high, across, preferred_element_type=jnp.float32)
    squares = squares + lax.dot_general(ones, low, across, preferred_element_type=jnp.float32)
    out[DPAD:, :snps] = squares


def moments(blocks, others, slots, me):
    count, rows, subjects = blocks.shape
    snps = rows - DPAD
    spread = -(-rows // LANES) * LANES
    outs = (
        result((rows, 2 * count * subjects), blocks.dtype),
        pltpu.HBM((DPAD + 8, spread), jnp.float32),
    )
    kernel = functools.partial(moments_kernel, snps, slots)
    return call(kernel, "moments", outs, [me], [blocks, others], (), 2)


def eliminate(total, snps, design, guard):
    lane = lax.broadcasted_iota(jnp.int32, (DPAD, LANES), 1)
    row = lax.broadcasted_iota(jnp.int32, (DPAD, LANES), 0)
    shift = 32
    gram = total[:DPAD, snps : snps + LANES]
    work = jnp.where((row >= design) & (lane == row), 1.0, gram)
    work = jnp.where(lane == row + shift, 1.0, work)
    for k in range(design):
        pivot = work[k : k + 1, k : k + 1]
        line = work[k : k + 1, :] / pivot
        if guard:
            line = jnp.where(pivot > gram[k : k + 1, k : k + 1] * 2.0**-14, line, 0.0)
        work = jnp.where(row == k, line, work - work[:, k : k + 1] * line)
    solved = pltpu.roll(work, LANES - shift, 1)
    return jnp.where((lane < design) & (row < design), solved, 0.0)


def gene_fit(total, snps, design, guard):
    solved = eliminate(total, snps, design, guard)
    cross_gene = total[:DPAD, :snps]
    fitted = jnp.dot(
        solved[:, :DPAD], cross_gene, precision=HIGHEST, preferred_element_type=jnp.float32
    )
    square = total[DPAD : DPAD + 1, :snps]
    rss = square - jnp.sum(cross_gene * fitted, axis=0, keepdims=True)
    if guard:
        rss = jnp.maximum(rss, square * 2.0**-10) + 1e-30
    return solved, fitted, lax.rsqrt(rss)


def pair_kernel(snps, design, moment, coef, lines):
    _, fitted, scale = gene_fit(moment[...], snps, design, True)
    lines[...] = jnp.zeros(lines.shape, jnp.float32)
    lines[:DPAD, :] = fitted * scale
    lines[SCALE_LANE : SCALE_LANE + 1, :] = scale
    coef[...] = jnp.transpose(lines[...])


def pair_fit(moment, snps, design):
    kernel = functools.partial(pair_kernel, snps, design)
    scratch = [pltpu.VMEM((LANES, snps), jnp.float32)]
    return call(kernel, "pair_fit", result((snps, LANES), jnp.float32), [], [moment], scratch, 1)


def cohort_lines(moments, snps, design, lines):
    solved, fitted, scale = gene_fit(tree_sum(moments), snps, design, False)
    lines[...] = jnp.zeros(lines.shape, jnp.float32)
    lines[:DPAD, :] = fitted * -scale
    lines[SCALE_LANE : SCALE_LANE + 1, :] = scale
    for j in range(1, len(moments)):
        _, fit, own_scale = gene_fit(moments[j], snps, design, True)
        lane = SCALE_LANE + 1 + j
        lines[lane : lane + 1, :] = scale / own_scale
        lines[j * STRIDE : j * STRIDE + DPAD, :] = fit * scale
    return solved


def column_norm(sums, here):
    square = sums[SQUARE_ROW : SQUARE_ROW + 1, :]
    mean = jnp.sum(sums[:SITES, :], axis=0, keepdims=True) * (1.0 / here)
    spread = jnp.maximum(square - mean * mean * here, square * 2.0**-10)
    return jnp.sqrt(spread + 1e-30)


def sums_kernel(genes, columns, out):
    values = columns[...]
    wide = values.astype(jnp.float32)
    design = genes[genes.shape[0] - DPAD :, :]
    sums = jnp.dot(design, values, preferred_element_type=jnp.float32)
    square = jnp.sum(wide * wide, axis=0, keepdims=True)
    row = lax.broadcasted_iota(jnp.int32, sums.shape, 0)
    out[...] = jnp.where(row == SQUARE_ROW, square, sums)


def column_sums(genes, columns):
    outs = result((DPAD, columns.shape[1]), jnp.float32)
    return call(sums_kernel, "column_sums", outs, [], [genes, columns])


def far_kernel(here, count, far, near, genes, columns, coef, stats, *refs):
    outs, held = list(refs[:-1]), refs[-1]
    size = held.shape[0]
    panel = outs[0].shape[0]
    cross_image = stats[...]
    over = 1.0 / column_norm(cross_image, here)
    for j in range(1, count):
        block = pl.multiple_of(jnp.bitwise_xor(far[0], j) * size, size)
        held[...] = jnp.dot(
            genes[pl.ds(block, size), :], columns[...], preferred_element_type=jnp.float32
        )
        for k in range(size // panel):
            place = pl.multiple_of(jnp.bitwise_xor(near[0], k) * panel, panel)
            line = coef[pl.ds(block + place, panel), :]
            fit = jnp.dot(
                line[:, :DPAD], cross_image, precision=HIGHEST, preferred_element_type=jnp.float32
            )
            scale = line[:, SCALE_LANE : SCALE_LANE + 1]
            outs.pop(0)[...] = (scale * held[pl.ds(place, panel), :] - fit) * over


def far_products(genes, columns, coef, stats, far, near, n_far, n_near):
    here, width = columns.shape
    size = (genes.shape[0] - DPAD) // n_far
    outs = (result((size // n_near, width), jnp.float32),) * ((n_far - 1) * n_near)
    kernel = functools.partial(far_kernel, float(here), n_far)
    scratch = [pltpu.VMEM((size, width), jnp.float32)]
    return call(kernel, "far_products", outs, [far, near], [genes, columns, coef, stats], scratch)


def base_kernel(here, design, count, far, near, genes, columns, *refs):
    parts, (home, away, factors, weights, stack, held, lines, coef) = refs[:-8], refs[-8:]
    n_far = len(parts) // 2
    size = held.shape[0]
    snps = size * n_far
    block = pl.ds(pl.multiple_of(far[0] * size, size), size)
    moments = [
        jnp.concatenate([part[:, block], part[:, snps : snps + LANES]], axis=1)
        for part in parts[:n_far]
    ]
    inverse = cohort_lines(moments, size, design, lines)
    coef[...] = jnp.transpose(lines[...])
    stats = [part[...] for part in parts[n_far:]]
    row = lax.broadcasted_iota(jnp.int32, stats[0].shape, 0)
    total = tree_sum(stats)
    known = row < SQUARE_ROW
    cross_image = jnp.where(known, total, 0.0)
    solved = jnp.dot(
        inverse[:, :DPAD], cross_image, precision=HIGHEST, preferred_element_type=jnp.float32
    )
    rss = total[SQUARE_ROW : SQUARE_ROW + 1, :] - jnp.sum(
        cross_image * solved, axis=0, keepdims=True
    )
    scale = lax.rsqrt(rss)
    stack[...] = jnp.zeros(stack.shape, jnp.float32)
    stack[:DPAD, :] = cross_image
    factors[...] = jnp.zeros(factors.shape, jnp.float32)
    for j in range(1, len(stats)):
        factors[j : j + 1, :] = column_norm(stats[j], here) * scale
        stack[j * STRIDE : j * STRIDE + DPAD, :] = jnp.where(known, stats[j], 0.0)
    line = coef[...]
    sums = jnp.dot(genes[block, :], columns[...], preferred_element_type=jnp.float32)
    terms = jnp.dot(line, stack[...], precision=HIGHEST, preferred_element_type=jnp.float32)
    held[...] = (line[:, SCALE_LANE : SCALE_LANE + 1] * sums + terms) * scale
    panel = size // count
    for k, out in enumerate((home, away)):
        place = pl.ds(pl.multiple_of(jnp.bitwise_xor(near[0], k) * panel, panel), panel)
        out[...] = held[place, :] * (WIDE if k else 1.0)
        if k == 0:
            weights[...] = coef[place, :]


def base_ratio(genes, columns, moments, parts, far, near, n_far, n_near, design):
    here, width = columns.shape
    size = (genes.shape[0] - DPAD) // n_far
    outs = (result((size // n_near, width), jnp.float32),) * 2
    outs += (result((8, width), jnp.float32), result((size // n_near, LANES), jnp.float32))
    kernel = functools.partial(base_kernel, float(here), design, n_near)
    scratch = [
        pltpu.VMEM((LANES, width), jnp.float32),
        pltpu.VMEM((size, width), jnp.float32),
        pltpu.VMEM((LANES, size), jnp.float32),
        pltpu.VMEM((size, LANES), jnp.float32),
    ]
    arrays = [genes, columns, *moments, *parts]
    return call(kernel, "base_ratio", outs, [far, near], arrays, scratch)


def permute_xor(value, axes, bits):
    size = lax.axis_size(axes)
    return lax.ppermute(value, axes, [(i, i ^ bits) for i in range(size)])


def on_device(images, genotypes, covariates, site_codes):
    subjects, maps, planes, plane = images.shape
    n_vox, n_far, n_near = (lax.axis_size(name) for name in ("vox", "far", "near"))
    vox, far, near = (lax.axis_index(name) for name in ("vox", "far", "near"))
    snps = genotypes.shape[1]
    design = SITES + covariates.shape[1]
    per_vox = planes // n_vox
    count = n_vox * n_near
    here = count * subjects

    def exchange(value):
        value = lax.all_to_all(value, ("vox", "near"), 0, 0, tiled=True)
        return value.reshape(here, value.shape[2])

    tall = tall_design(genotypes, covariates, site_codes)
    other = n_near
    offsets = [o for o in range(count) if not o & other]
    blocks = [tall] + [permute_xor(tall, ("vox", "near"), o) for o in offsets[1:]]
    (smoothed,) = smooth(images, n_vox, n_near, 1)
    smoothed, *blocks = lax.optimization_barrier((smoothed, *blocks))
    columns = exchange(smoothed)
    blocks = jnp.stack(blocks)
    others = permute_xor(blocks, ("vox", "near"), other)
    order = offsets + [o | other for o in offsets]
    slots = tuple(order.index(o) for o in range(count))
    genes, moment = moments(blocks, others, slots, (vox * n_near + near)[None])
    pair_coef = pair_fit(moment, snps, design)
    moment_parts = [moment] + [permute_xor(moment, "far", j) for j in range(1, n_far)]
    columns, pair_coef, moment_parts = lax.optimization_barrier(
        (columns, pair_coef, moment_parts)
    )
    stats = column_sums(genes, columns)
    stat_parts = [stats] + [permute_xor(stats, "far", j) for j in range(1, n_far)]

    size = snps // n_far
    panel = size // n_near
    freedom = float(here * n_far - design - 1)
    line = ("far", "near")
    where = [far[None], near[None], n_far, n_near]
    sent = list(far_products(genes, columns, pair_coef, stats, *where))
    sent[0] = sent[0].astype(jnp.float16)
    sent, stat_parts = lax.optimization_barrier((sent, stat_parts))
    sent = [piece.astype(jnp.float16) for piece in sent]
    pieces = {
        k: permute_xor(sent[k - n_near], line, k) for k in range(n_near, n_far * n_near)
    }
    home, away, factors, weights = base_ratio(
        genes, columns, moment_parts, stat_parts, *where, design
    )
    coarse = lax.reduce_precision(factors, 5, 10)
    fine = (factors - coarse) * FINE
    away = jnp.concatenate([away, coarse, fine], axis=0).astype(jnp.float16)
    away = permute_xor(away, "near", 1).astype(jnp.float32)
    away_factors = away[panel : panel + 8] + away[panel + 8 :] * (1.0 / FINE)
    away = away[:panel] * (1.0 / WIDE)

    def t_of(ratio, factors, offset):
        for j in range(1, n_far):
            weight = weights[:, SCALE_LANE + 1 + j, None] * factors[None, j]
            ratio = ratio + pieces[j * n_near + offset].astype(jnp.float32) * weight
        return ratio * jnp.sqrt(freedom / (1.0 - ratio * ratio))

    home = t_of(home, factors, 0)
    away_factors, home = lax.optimization_barrier((away_factors, home))
    away = t_of(away, away_factors, 1)
    both = jnp.where(near == 0, jnp.stack([home, away], 1), jnp.stack([away, home], 1))
    return both.reshape(panel, maps, per_vox, plane)


def solution(mesh):
    sizes = dict(mesh.shape)
    devices = mesh.devices.reshape(sizes["group"], sizes["vox"], sizes["snp"] // 2, 2)
    split = Mesh(devices, ("group", "vox", "far", "near"))
    owner = ("group", "vox", "far", "near")
    placed = (P(owner, None, None, None), P(owner, None), P(owner, None), P(owner))
    return jax.shard_map(
        on_device,
        mesh=split,
        in_specs=placed,
        out_specs=P(("group", "far", "near"), None, "vox", None),
        check_vma=False,
    )
```

```python
import functools

import jax
import jax.numpy as jnp
import ml_dtypes
import numpy as np
from jax import lax
from jax.experimental import pallas as pl
from jax.experimental.pallas import tpu as pltpu
from jax.sharding import Mesh
from jax.sharding import PartitionSpec as P

SY = 16
SZ = 16
SITES = 4
REACH = 2
DPAD = 24
LANES = 128
SUBJ_TILE = 16
HIGHEST = lax.Precision.HIGHEST
VMEM_MOST = 56 * 2**20
VMEM_BASE = 12 * 2**20
SQUARE_ROW = 20
WIDE = 2.0**8
FINE = 2.0**11
SCALE_LANE = DPAD
STRIDE = 32


def kernel_table(length):
    position = np.arange(length)
    offset = (position[:, None] - position[None, :]).astype(np.float32)
    weights = np.where(np.abs(offset) <= REACH, np.exp(-offset * offset / np.float32(2.0)), np.float32(0.0))
    total = sum(np.exp(-(k * k) / 2.0) for k in range(-REACH, REACH + 1))
    return (weights / np.float32(total)).astype(np.float32)


def plane_kernel(plane):
    row, depth = kernel_table(SY), kernel_table(SZ)
    table = row[:, None, :, None] * depth[None, :, None, :]
    return table.reshape(plane, plane).astype(ml_dtypes.bfloat16)


def row_order(maps, planes):
    rows = SUBJ_TILE * maps * planes
    source = np.arange(rows).reshape(SUBJ_TILE, maps * planes).T.reshape(-1)
    return np.eye(rows, dtype=np.float32)[source].astype(ml_dtypes.bfloat16)


def tree_sum(terms):
    while len(terms) > 1:
        terms = [terms[i] + terms[i + 1] for i in range(0, len(terms), 2)]
    return terms[0]


RESIDENT = 3 * 2**20
IN_VMEM = pl.BlockSpec(memory_space=pltpu.VMEM)
IN_SMEM = pl.BlockSpec(memory_space=pltpu.SMEM)


def params(extra=0):
    return pltpu.CompilerParams(vmem_limit_bytes=min(VMEM_MOST, VMEM_BASE + extra))


def size_of(value):
    return int(np.prod(value.shape)) * jnp.dtype(value.dtype).itemsize


def small(shape, dtype):
    return int(np.prod(shape)) * jnp.dtype(dtype).itemsize <= RESIDENT


def keep(value):
    if small(value.shape, value.dtype):
        return pltpu.with_memory_space_constraint(value, pltpu.VMEM)
    return value


def result(shape, dtype):
    if small(shape, dtype):
        return pltpu.VMEM(shape, dtype)
    return jax.ShapeDtypeStruct(shape, dtype)


def call(kernel, name, outs, scalars, arrays, scratch=(), moved=0):
    many = isinstance(outs, tuple)
    sizes = [size_of(value) for value in (*arrays, *(outs if many else (outs,)))]
    extra = 3 * sum(size for size in sizes if size > RESIDENT)
    return pl.pallas_call(
        kernel,
        out_shape=outs,
        in_specs=[IN_SMEM] * len(scalars) + [IN_VMEM] * len(arrays),
        out_specs=(IN_VMEM,) * len(outs) if many else IN_VMEM,
        scratch_shapes=list(scratch),
        compiler_params=params(extra),
        name=name,
    )(*scalars, *arrays[:moved], *[keep(value) for value in arrays[moved:]])


def tall_kernel(genotypes, codes, covariates, out, rows):
    snps = genotypes.shape[1]
    out[:snps, :] = jnp.transpose(genotypes[...])
    count = covariates.shape[0]
    site = lax.broadcasted_iota(jnp.int32, (SITES, codes.shape[1]), 0)
    rows[...] = jnp.zeros(rows.shape, jnp.float32)
    rows[:SITES, :] = (site == codes[...]).astype(jnp.float32)
    rows[SITES : SITES + count, :] = covariates[...].astype(jnp.float32)
    out[snps:, :] = rows[...].astype(jnp.bfloat16)


def tall_design(genotypes, covariates, site_codes):
    subjects, snps = genotypes.shape
    return pl.pallas_call(
        tall_kernel,
        out_shape=result((snps + DPAD, subjects), jnp.bfloat16),
        in_specs=[IN_VMEM] * 3,
        out_specs=IN_VMEM,
        scratch_shapes=[pltpu.VMEM((DPAD, subjects), jnp.float32)],
        compiler_params=params(VMEM_MOST),
        name="tall_design",
    )(genotypes, site_codes[None, :], covariates.T)


def smooth_kernel(group, planes, per_vox, parts, width, images, order, table, *outs):
    plane = table.shape[0]
    size = width // len(outs)
    groups = images.shape[1] // (group * planes)
    near = kernel_table(2 * REACH + 1)[REACH]
    for tile in range(images.shape[0] // SUBJ_TILE):
        here = pl.ds(tile * SUBJ_TILE, SUBJ_TILE)
        for part in range(groups):
            rows = images[here, part * group * planes : (part + 1) * group * planes, :]
            rows = rows.reshape(SUBJ_TILE * group * planes, plane)
            rows = jnp.dot(order[...], rows, preferred_element_type=jnp.float32)
            inplane = jnp.dot(
                rows.astype(jnp.bfloat16), table[...], preferred_element_type=jnp.float32
            )
            for m in range(group):
                slabs = [
                    inplane[(m * planes + x) * SUBJ_TILE : (m * planes + x + 1) * SUBJ_TILE]
                    for x in range(planes)
                ]
                for x in range(planes):
                    total = slabs[x] * float(near[REACH])
                    for lag in range(1, REACH + 1):
                        sides = [slabs[k] for k in (x - lag, x + lag) if 0 <= k < planes]
                        if sides:
                            total = total + functools.reduce(jnp.add, sides) * float(
                                near[REACH + lag]
                            )
                    column = ((part * group + m) * per_vox + x % per_vox) * plane
                    target = (x // per_vox) * parts + column // width
                    chunk, first = column % width // size, column % size
                    out = outs[chunk]
                    out[target, here, first : first + plane] = total.astype(jnp.bfloat16)


def smooth(images, n_vox, parts, chunks):
    subjects, maps, planes, plane = images.shape
    per_vox = planes // n_vox
    width = maps * per_vox * plane // parts
    size = width // chunks
    assert size % plane == 0
    group = max(1, min(maps, 256 // (SUBJ_TILE * planes)))
    step = min(subjects, 64)
    order = jnp.asarray(row_order(group, planes))
    table = jnp.asarray(plane_kernel(plane))
    return pl.pallas_call(
        functools.partial(smooth_kernel, group, planes, per_vox, parts, width),
        out_shape=[jax.ShapeDtypeStruct((n_vox * parts, subjects, size), jnp.bfloat16)] * chunks,
        grid=(subjects // step,),
        in_specs=[
            pl.BlockSpec((step, maps * planes, plane), lambda i: (i, 0, 0)),
            pl.BlockSpec(order.shape, lambda i: (0, 0)),
            pl.BlockSpec(table.shape, lambda i: (0, 0)),
        ],
        out_specs=[pl.BlockSpec((n_vox * parts, step, size), lambda i: (0, i, 0))] * chunks,
        compiler_params=params(VMEM_MOST),
        name="smooth",
    )(images.reshape(subjects, maps * planes, plane), order, table)


def moments_kernel(snps, slots, me, blocks, others, joined, out):
    rows = []
    half = len(slots) // 2
    for source in range(len(slots)):
        offset = jnp.bitwise_xor(me[0], source)
        index = 0
        for place, slot in enumerate(slots):
            index = index + jnp.where(offset == place, slot, 0)
        place = lax.rem(index, half)
        rows.append(jnp.where(index < half, blocks[place], others[place]))
    rows = jnp.concatenate(rows, axis=1)
    joined[...] = rows
    across = (((1,), (1,)), ((), ()))
    out[...] = jnp.zeros(out.shape, jnp.float32)
    out[:DPAD, : snps + DPAD] = lax.dot_general(
        rows[snps:], rows, across, preferred_element_type=jnp.float32
    )
    wide = rows[:snps].astype(jnp.float32)
    wide = wide * wide
    high = wide.astype(jnp.bfloat16)
    low = (wide - high.astype(jnp.float32)).astype(jnp.bfloat16)
    ones = jnp.ones((8, rows.shape[1]), jnp.bfloat16)
    squares = lax.dot_general(ones, high, across, preferred_element_type=jnp.float32)
    squares = squares + lax.dot_general(ones, low, across, preferred_element_type=jnp.float32)
    out[DPAD:, :snps] = squares


def moments(blocks, others, slots, me):
    count, rows, subjects = blocks.shape
    snps = rows - DPAD
    spread = -(-rows // LANES) * LANES
    outs = (
        result((rows, 2 * count * subjects), blocks.dtype),
        pltpu.HBM((DPAD + 8, spread), jnp.float32),
    )
    kernel = functools.partial(moments_kernel, snps, slots)
    return call(kernel, "moments", outs, [me], [blocks, others], (), 2)


def eliminate(total, snps, design, guard):
    lane = lax.broadcasted_iota(jnp.int32, (DPAD, LANES), 1)
    row = lax.broadcasted_iota(jnp.int32, (DPAD, LANES), 0)
    shift = 32
    gram = total[:DPAD, snps : snps + LANES]
    work = jnp.where((row >= design) & (lane == row), 1.0, gram)
    work = jnp.where(lane == row + shift, 1.0, work)
    for k in range(design):
        pivot = work[k : k + 1, k : k + 1]
        line = work[k : k + 1, :] / pivot
        if guard:
            line = jnp.where(pivot > gram[k : k + 1, k : k + 1] * 2.0**-14, line, 0.0)
        work = jnp.where(row == k, line, work - work[:, k : k + 1] * line)
    solved = pltpu.roll(work, LANES - shift, 1)
    return jnp.where((lane < design) & (row < design), solved, 0.0)


def gene_fit(total, snps, design, guard):
    solved = eliminate(total, snps, design, guard)
    cross_gene = total[:DPAD, :snps]
    fitted = jnp.dot(
        solved[:, :DPAD], cross_gene, precision=HIGHEST, preferred_element_type=jnp.float32
    )
    square = total[DPAD : DPAD + 1, :snps]
    rss = square - jnp.sum(cross_gene * fitted, axis=0, keepdims=True)
    if guard:
        rss = jnp.maximum(rss, square * 2.0**-10) + 1e-30
    return solved, fitted, lax.rsqrt(rss)


def pair_kernel(snps, design, moment, coef, lines):
    _, fitted, scale = gene_fit(moment[...], snps, design, True)
    lines[...] = jnp.zeros(lines.shape, jnp.float32)
    lines[:DPAD, :] = fitted * scale
    lines[SCALE_LANE : SCALE_LANE + 1, :] = scale
    coef[...] = jnp.transpose(lines[...])


def pair_fit(moment, snps, design):
    kernel = functools.partial(pair_kernel, snps, design)
    scratch = [pltpu.VMEM((LANES, snps), jnp.float32)]
    return call(kernel, "pair_fit", result((snps, LANES), jnp.float32), [], [moment], scratch, 1)


def cohort_lines(moments, snps, design, lines):
    solved, fitted, scale = gene_fit(tree_sum(moments), snps, design, False)
    lines[...] = jnp.zeros(lines.shape, jnp.float32)
    lines[:DPAD, :] = fitted * -scale
    lines[SCALE_LANE : SCALE_LANE + 1, :] = scale
    for j in range(1, len(moments)):
        _, fit, own_scale = gene_fit(moments[j], snps, design, True)
        lane = SCALE_LANE + 1 + j
        lines[lane : lane + 1, :] = scale / own_scale
        lines[j * STRIDE : j * STRIDE + DPAD, :] = fit * scale
    return solved


def column_norm(sums, here):
    square = sums[SQUARE_ROW : SQUARE_ROW + 1, :]
    mean = jnp.sum(sums[:SITES, :], axis=0, keepdims=True) * (1.0 / here)
    spread = jnp.maximum(square - mean * mean * here, square * 2.0**-10)
    return jnp.sqrt(spread + 1e-30)


def sums_kernel(genes, columns, out):
    values = columns[...]
    wide = values.astype(jnp.float32)
    design = genes[genes.shape[0] - DPAD :, :]
    sums = jnp.dot(design, values, preferred_element_type=jnp.float32)
    square = jnp.sum(wide * wide, axis=0, keepdims=True)
    row = lax.broadcasted_iota(jnp.int32, sums.shape, 0)
    out[...] = jnp.where(row == SQUARE_ROW, square, sums)


def column_sums(genes, columns):
    outs = result((DPAD, columns.shape[1]), jnp.float32)
    return call(sums_kernel, "column_sums", outs, [], [genes, columns])


def far_kernel(here, count, far, near, genes, columns, coef, stats, *refs):
    outs, held = list(refs[:-1]), refs[-1]
    size = held.shape[0]
    panel = outs[0].shape[0]
    cross_image = stats[...]
    over = 1.0 / column_norm(cross_image, here)
    for j in range(1, count):
        block = pl.multiple_of(jnp.bitwise_xor(far[0], j) * size, size)
        held[...] = jnp.dot(
            genes[pl.ds(block, size), :], columns[...], preferred_element_type=jnp.float32
        )
        for k in range(size // panel):
            place = pl.multiple_of(jnp.bitwise_xor(near[0], k) * panel, panel)
            line = coef[pl.ds(block + place, panel), :]
            fit = jnp.dot(
                line[:, :DPAD], cross_image, precision=HIGHEST, preferred_element_type=jnp.float32
            )
            scale = line[:, SCALE_LANE : SCALE_LANE + 1]
            outs.pop(0)[...] = (scale * held[pl.ds(place, panel), :] - fit) * over


def far_products(genes, columns, coef, stats, far, near, n_far, n_near):
    here, width = columns.shape
    size = (genes.shape[0] - DPAD) // n_far
    outs = (result((size // n_near, width), jnp.float32),) * ((n_far - 1) * n_near)
    kernel = functools.partial(far_kernel, float(here), n_far)
    scratch = [pltpu.VMEM((size, width), jnp.float32)]
    return call(kernel, "far_products", outs, [far, near], [genes, columns, coef, stats], scratch)


def base_kernel(here, design, count, far, near, genes, columns, *refs):
    parts, (home, away, factors, weights, stack, held, lines, coef) = refs[:-8], refs[-8:]
    n_far = len(parts) // 2
    size = held.shape[0]
    snps = size * n_far
    block = pl.ds(pl.multiple_of(far[0] * size, size), size)
    moments = [
        jnp.concatenate([part[:, block], part[:, snps : snps + LANES]], axis=1)
        for part in parts[:n_far]
    ]
    inverse = cohort_lines(moments, size, design, lines)
    coef[...] = jnp.transpose(lines[...])
    stats = [part[...] for part in parts[n_far:]]
    row = lax.broadcasted_iota(jnp.int32, stats[0].shape, 0)
    total = tree_sum(stats)
    known = row < SQUARE_ROW
    cross_image = jnp.where(known, total, 0.0)
    solved = jnp.dot(
        inverse[:, :DPAD], cross_image, precision=HIGHEST, preferred_element_type=jnp.float32
    )
    rss = total[SQUARE_ROW : SQUARE_ROW + 1, :] - jnp.sum(
        cross_image * solved, axis=0, keepdims=True
    )
    scale = lax.rsqrt(rss)
    stack[...] = jnp.zeros(stack.shape, jnp.float32)
    stack[:DPAD, :] = cross_image
    factors[...] = jnp.zeros(factors.shape, jnp.float32)
    for j in range(1, len(stats)):
        factors[j : j + 1, :] = column_norm(stats[j], here) * scale
        stack[j * STRIDE : j * STRIDE + DPAD, :] = jnp.where(known, stats[j], 0.0)
    line = coef[...]
    sums = jnp.dot(genes[block, :], columns[...], preferred_element_type=jnp.float32)
    terms = jnp.dot(line, stack[...], precision=HIGHEST, preferred_element_type=jnp.float32)
    held[...] = (line[:, SCALE_LANE : SCALE_LANE + 1] * sums + terms) * scale
    panel = size // count
    for k, out in enumerate((home, away)):
        place = pl.ds(pl.multiple_of(jnp.bitwise_xor(near[0], k) * panel, panel), panel)
        out[...] = held[place, :] * (WIDE if k else 1.0)
        if k == 0:
            weights[...] = coef[place, :]


def base_ratio(genes, columns, moments, parts, far, near, n_far, n_near, design):
    here, width = columns.shape
    size = (genes.shape[0] - DPAD) // n_far
    outs = (result((size // n_near, width), jnp.float32),) * 2
    outs += (result((8, width), jnp.float32), result((size // n_near, LANES), jnp.float32))
    kernel = functools.partial(base_kernel, float(here), design, n_near)
    scratch = [
        pltpu.VMEM((LANES, width), jnp.float32),
        pltpu.VMEM((size, width), jnp.float32),
        pltpu.VMEM((LANES, size), jnp.float32),
        pltpu.VMEM((size, LANES), jnp.float32),
    ]
    arrays = [genes, columns, *moments, *parts]
    return call(kernel, "base_ratio", outs, [far, near], arrays, scratch)


def permute_xor(value, axes, bits):
    size = lax.axis_size(axes)
    return lax.ppermute(value, axes, [(i, i ^ bits) for i in range(size)])


def on_device(images, genotypes, covariates, site_codes):
    subjects, maps, planes, plane = images.shape
    n_vox, n_far, n_near = (lax.axis_size(name) for name in ("vox", "far", "near"))
    vox, far, near = (lax.axis_index(name) for name in ("vox", "far", "near"))
    snps = genotypes.shape[1]
    design = SITES + covariates.shape[1]
    per_vox = planes // n_vox
    count = n_vox * n_near
    here = count * subjects

    def exchange(value):
        value = lax.all_to_all(value, ("vox", "near"), 0, 0, tiled=True)
        return value.reshape(here, value.shape[2])

    tall = tall_design(genotypes, covariates, site_codes)
    other = n_near
    offsets = [o for o in range(count) if not o & other]
    blocks = [tall] + [permute_xor(tall, ("vox", "near"), o) for o in offsets[1:]]
    (smoothed,) = smooth(images, n_vox, n_near, 1)
    smoothed, *blocks = lax.optimization_barrier((smoothed, *blocks))
    columns = exchange(smoothed)
    blocks = jnp.stack(blocks)
    others = permute_xor(blocks, ("vox", "near"), other)
    order = offsets + [o | other for o in offsets]
    slots = tuple(order.index(o) for o in range(count))
    genes, moment = moments(blocks, others, slots, (vox * n_near + near)[None])
    pair_coef = pair_fit(moment, snps, design)
    moment_parts = [moment] + [permute_xor(moment, "far", j) for j in range(1, n_far)]
    columns, pair_coef, moment_parts = lax.optimization_barrier(
        (columns, pair_coef, moment_parts)
    )
    stats = column_sums(genes, columns)
    stat_parts = [stats] + [permute_xor(stats, "far", j) for j in range(1, n_far)]

    size = snps // n_far
    panel = size // n_near
    freedom = float(here * n_far - design - 1)
    line = ("far", "near")
    where = [far[None], near[None], n_far, n_near]
    sent = list(far_products(genes, columns, pair_coef, stats, *where))
    sent[0] = sent[0].astype(jnp.float16)
    sent, stat_parts = lax.optimization_barrier((sent, stat_parts))
    sent = [piece.astype(jnp.float16) for piece in sent]
    pieces = {
        k: permute_xor(sent[k - n_near], line, k) for k in range(n_near, n_far * n_near)
    }
    home, away, factors, weights = base_ratio(
        genes, columns, moment_parts, stat_parts, *where, design
    )
    coarse = lax.reduce_precision(factors, 5, 10)
    fine = (factors - coarse) * FINE
    away = jnp.concatenate([away, coarse, fine], axis=0).astype(jnp.float16)
    away = permute_xor(away, "near", 1)
    away_factors = away[panel : panel + 8].astype(jnp.float32)
    away_factors = away_factors + away[panel + 8 :].astype(jnp.float32) * (1.0 / FINE)
    away = away[:panel].astype(jnp.float32) * (1.0 / WIDE)

    def t_of(ratio, factors, offset):
        for j in range(1, n_far):
            weight = weights[:, SCALE_LANE + 1 + j, None] * factors[None, j]
            ratio = ratio + pieces[j * n_near + offset].astype(jnp.float32) * weight
        return ratio * jnp.sqrt(freedom / (1.0 - ratio * ratio))

    home = t_of(home, factors, 0)
    away_factors, home = lax.optimization_barrier((away_factors, home))
    away = t_of(away, away_factors, 1)
    both = jnp.where(near == 0, jnp.stack([home, away], 1), jnp.stack([away, home], 1))
    return both.reshape(panel, maps, per_vox, plane)


def solution(mesh):
    sizes = dict(mesh.shape)
    devices = mesh.devices.reshape(sizes["group"], sizes["vox"], sizes["snp"] // 2, 2)
    split = Mesh(devices, ("group", "vox", "far", "near"))
    owner = ("group", "vox", "far", "near")
    placed = (P(owner, None, None, None), P(owner, None), P(owner, None), P(owner))
    return jax.shard_map(
        on_device,
        mesh=split,
        in_specs=placed,
        out_specs=P(("group", "far", "near"), None, "vox", None),
        check_vma=False,
    )
```
